512 devices in a mesh: pairs: 16 (over z), hours: 32 (over x, y, core).
Axes of the slice: x: 4, y: 4, z: 16, core: 2. Of those that a mesh axis runs over, the one named last changes fastest.
Arguments:
- spectra: bfloat16 [128, 64, 8, 2, 1024], P('pairs', 'hours'), may hold values from -6 to 6
- masks: int32 [128, 64, 8], P('pairs', 'hours'), may hold values 0 or 1
- pair_rows: int32 [192, 2], P('pairs'), may hold values from 0 to 127, as said below
- start_basis: float32 [4, 2048], replicated, may hold values from -6 to 6
Outputs:
- window_stacks: float32 [192, 64, 2048], P('pairs', 'hours')
- stack: float32 [192, 2048], P('pairs', 'hours')
- basis: float32 [192, 4, 2048], P('pairs', None, 'hours')
The draws below stay inside these ranges and needn't reach their ends.
Inputs may be any that keep to these rules, and one draw needn't show every extreme that they name: pair_rows[p, 0] is a station of group p // 12, the group being stations 8 * i to 8 * i + 7 for group i; pair_rows[p, 1] is another station of that group or a station of the group just before or just after it, counted around all groups; each block of 12 rows has pairs with all three of these groups, and its pairs reach exactly 4 distinct stations of the group just before and exactly 4 of the group just after.
All inputs are finite; a program needn't handle non-finite values. No bound on the sum of `masks` on one device may be relied on, other than what follows from the above.
Results may differ from the reference program's by a relative error of at most 0.0064.
Values may be sent and summed in bfloat16 or wider, within the bound.
A program may use at most 64 MiB of HBM per device.

```python
import math
import jax
import jax.numpy as jnp
from jax import lax

STA_DEV = 8
PAIR_DEV = 12
SEG = 8
FREQ = 1024
LAGS = 2048
BAND = 64
RANK = 4
TURNS = 2
STATIONS = 128
PAIRS = 192
WINDOWS = 64


def draw_pair_rows(key, part):
    groups = STATIONS // STA_DEV
    near = STA_DEV // 2
    row = jnp.arange(PAIRS, dtype=jnp.int32)
    block = row // PAIR_DEV
    within = row % PAIR_DEV
    keys = jax.random.split(key, 7)
    role_perm = jax.vmap(lambda k: jax.random.permutation(k, PAIR_DEV))(jax.random.split(keys[0], groups)).astype(jnp.int32)
    left_perm = jax.vmap(lambda k: jax.random.permutation(k, STA_DEV))(jax.random.split(keys[1], groups)).astype(jnp.int32)
    right_perm = jax.vmap(lambda k: jax.random.permutation(k, STA_DEV))(jax.random.split(keys[2], groups)).astype(jnp.int32)
    role = role_perm[block, within]
    first_local = jax.random.randint(keys[3], (PAIRS,), 0, STA_DEV, dtype=jnp.int32)
    drawn = jax.random.randint(keys[4], (PAIRS,), -1, 2, dtype=jnp.int32)
    pick = jax.random.randint(keys[5], (PAIRS,), 0, near, dtype=jnp.int32)
    stride = jax.random.randint(keys[6], (PAIRS,), 1, STA_DEV, dtype=jnp.int32)
    offset = jnp.where(role < near, -1, jnp.where(role < 2 * near, 1, jnp.where(role == 2 * near, 0, drawn)))
    slot = jnp.where(role < near, role, jnp.where(role < 2 * near, role - near, pick))
    slot = jnp.clip(slot, 0, near - 1)
    neighbour_local = jnp.where(offset < 0, left_perm[block, slot], right_perm[block, slot])
    second_local = jnp.where(offset == 0, jnp.mod(first_local + stride, STA_DEV), neighbour_local)
    second_group = jnp.mod(block + offset, groups)
    first = block * STA_DEV + first_local
    second = second_group * STA_DEV + second_local
    return jnp.stack([first, second], 1).astype(jnp.int32)


def touch_ends(array, rng, low, largest):
    dims = array.shape
    spot = [jax.random.randint(jax.random.fold_in(rng, axis), (), 0, dims[axis]) for axis in range(len(dims))]
    array = array.at[tuple(spot)].set(low)
    longest = dims.index(max(dims))
    spot[longest] = (spot[longest] + 1) % dims[longest]
    return array.at[tuple(spot)].set(largest)


def steps_of(own_key, extent, shards, low, top_value):
    gain, own = 1.0, jax.random.fold_in(own_key, 6)
    for position, shards_of in shards:
        steps = jnp.exp(jax.random.uniform(jax.random.fold_in(own, position), (shards_of,), jnp.float32, low / len(shards), top_value / len(shards)))
        gain = gain * jnp.repeat(steps, extent[position] // shards_of).reshape([-1 if axis == position else 1 for axis in range(len(extent))])
    return gain


def normal_values(own_key, dims, deviation, most, pieces=(), held_as=jnp.bfloat16):
    values = deviation * jax.random.normal(own_key, dims, jnp.float32)
    if pieces:
        values = values * steps_of(own_key, dims, pieces, -0.22, 0.18)
    return jnp.clip(values, -most, most).astype(held_as)


def setup_inputs(seed: int = 0) -> dict:
    splits = jax.random.split(jax.random.key(seed), 5)
    return {
        "spectra": normal_values(splits[0], (STATIONS, WINDOWS, SEG, 2, FREQ), 1.0, 6.0, ((0, 16), (1, 32))),
        "masks": touch_ends((jax.random.randint(splits[1], (STATIONS, WINDOWS, SEG), 0, 8) < 7).astype(jnp.int32), jax.random.fold_in(splits[1], 1), 0, 1),
        "pair_rows": draw_pair_rows(jax.random.fold_in(splits[4], 71), 0),
        "start_basis": normal_values(splits[3], (RANK, LAGS), 1.0, 6.0, (), jnp.float32),
    }


HIGH = lax.Precision.HIGHEST

def whiten(spectra, masks):
    values = spectra.astype(jnp.float32)
    shape = values.shape
    banded = values.reshape(shape[:-1] + (shape[-1] // BAND, BAND))
    power = lax.optimization_barrier(jnp.mean(banded * banded, axis=(3, 5), keepdims=True))
    scaled = banded * lax.rsqrt(power + 1e-06) * masks.astype(jnp.float32)[:, :, :, None, None, None]
    return scaled.reshape(shape).astype(jnp.bfloat16)

def kernel_table(freq, lags):
    nfft = 2 * lags
    bins = jnp.arange(1, freq + 1, dtype=jnp.int32)[:, None]
    shifts = jnp.arange(lags, dtype=jnp.int32)[None, :] - lags // 2
    phase = jnp.mod(bins * shifts, nfft).astype(jnp.float32) * (2.0 * math.pi / nfft)
    scale = freq ** (-0.5)
    return jnp.concatenate([jnp.cos(phase) * scale, -jnp.sin(phase) * scale], 0).astype(jnp.bfloat16)

def cross_spectra(first, second):
    a_re = first[..., 0, :].astype(jnp.float32)
    a_im = first[..., 1, :].astype(jnp.float32)
    b_re = second[..., 0, :].astype(jnp.float32)
    b_im = second[..., 1, :].astype(jnp.float32)
    real_part = a_re * b_re + a_im * b_im
    imag_part = a_im * b_re - a_re * b_im
    return jnp.concatenate([real_part, imag_part], -1).astype(jnp.bfloat16)

def from_gram(vectors, gram):
    rank = vectors.shape[-2]
    lower = [[None] * rank for index in range(rank)]
    for row in range(rank):
        for col in range(row + 1):
            total = gram[..., row, col]
            for inner in range(col):
                total = total - lower[row][inner] * lower[col][inner]
            if row == col:
                lower[row][row] = jnp.sqrt(total)
            else:
                lower[row][col] = total / lower[col][col]
    result = []
    for row in range(rank):
        current = vectors[..., row, :]
        for inner in range(row):
            current = current - lower[row][inner][..., None] * result[inner]
        result.append(current / lower[row][row][..., None])
    return jnp.stack(result, -2)

def orthonormal(vectors):
    gram = jnp.einsum('...il,...jl->...ij', vectors, vectors, precision=HIGH)
    return from_gram(vectors, gram)

def power_step(basis, corr):
    proj = jnp.einsum('wrl,wgl->wrg', basis, corr, precision=HIGH)
    back = jnp.einsum('wrg,wgl->wrl', proj, corr, precision=HIGH)
    return back + float(LAGS) * basis

def reference(spectra, masks, pair_rows, start_basis):
    whitened = whiten(spectra, masks)
    table = kernel_table(FREQ, LAGS).astype(jnp.float32)

    def per_pair(rows):
        first = whitened[rows[0]]
        second = whitened[rows[1]]
        cross = cross_spectra(first, second).astype(jnp.float32)
        corr = jnp.dot(cross.reshape(WINDOWS * SEG, 2 * FREQ), table, precision=HIGH)
        corr = corr.reshape(WINDOWS, SEG, LAGS)
        basis_now = jnp.broadcast_to(start_basis, (WINDOWS, RANK, LAGS)).astype(jnp.float32)
        for turn in range(TURNS):
            basis_now = orthonormal(power_step(basis_now, corr))
        final_terms = power_step(basis_now, corr)
        summed = lax.optimization_barrier(jnp.sum(corr, axis=1))
        coef = jnp.einsum('wl,wrl->wr', summed, basis_now, precision=HIGH)
        windows = jnp.einsum('wr,wrl->wl', coef, basis_now, precision=HIGH) / math.sqrt(SEG)
        merged = lax.optimization_barrier(jnp.sum(final_terms, axis=0))
        stack = lax.optimization_barrier(jnp.sum(windows, axis=0)) / math.sqrt(WINDOWS)
        basis = math.sqrt(LAGS) * orthonormal(merged)
        return (windows, stack, basis)
    window_stacks, stack, basis = lax.map(per_pair, pair_rows)
    return (window_stacks, stack, basis)
```

```python
import functools
import math

import jax
import jax.numpy as jnp
import numpy as np
from jax import lax
from jax.experimental import pallas as pl
from jax.experimental.pallas import tpu as pltpu
from jax.sharding import PartitionSpec as P

BAND = 64
TURNS = 2
RANK = 4
MESH = pl.DeviceIdType.MESH
F32 = jnp.float32
BF16 = jnp.bfloat16


def half_table(freq, half):
    nfft = 4 * half
    bins = np.arange(1, freq + 1, dtype=np.int64)[:, None]
    shifts = np.arange(half, dtype=np.int64)[None, :]
    phase = np.mod(bins * shifts, nfft).astype(np.float64) * (2.0 * math.pi / nfft)
    scale = freq ** (-0.5)
    table = np.concatenate([np.cos(phase) * scale, -np.sin(phase) * scale], 0)
    return table.astype(np.float32).astype(jnp.bfloat16)


def whiten(spectra, masks):
    values = spectra.astype(F32)
    shape = values.shape
    banded = values.reshape(shape[:-1] + (shape[-1] // BAND, BAND))
    power = jnp.mean(banded * banded, axis=(3, 5), keepdims=True)
    scaled = banded * lax.rsqrt(power + 1e-06) * masks.astype(F32)[:, :, :, None, None, None]
    return scaled.reshape(shape).astype(BF16)


def nt(a, b):
    return lax.dot_general(a, b, (((1,), (1,)), ((), ())), preferred_element_type=F32)


def split(x):
    hi = x.astype(BF16)
    return hi, (x - hi.astype(F32)).astype(BF16)


def cholesky(gram):
    lower = [[None] * RANK for _ in range(RANK)]
    for row in range(RANK):
        for col in range(row + 1):
            total = gram[row][col]
            for inner in range(col):
                total = total - lower[row][inner] * lower[col][inner]
            lower[row][col] = jnp.sqrt(total) if row == col else total / lower[col][col]
    return lower


def solve(lower, vectors):
    result = []
    for row in range(RANK):
        current = vectors[row]
        for inner in range(row):
            current = current - lower[row][inner] * result[inner]
        result.append(current / lower[row][row])
    return result


def fold8(x, batch_of_lane, batch):
    kept = jnp.where(batch_of_lane == batch, x, 0.0)
    total = kept[:, :128] + kept[:, 128:]
    for shift in (64, 32, 16, 8):
        total = total + pltpu.roll(total, shift, 1)
    return total


def correlate_kernel(
    stations, segments, windows, pairs, freq, half,
    rows_ref, wh_ref, table_ref, start_ref,
    ws_ref, part_ref,
    near, cross, table, vhi, vlo, square, wide, coef,
    send_sem, recv_sem, own_sem,
):
    me, ring = lax.axis_index("pairs"), lax.axis_size("pairs")
    after, before = lax.rem(me + 1, ring), lax.rem(me + ring - 1, ring)
    block = windows * segments
    count = pairs * block
    batches = pairs * windows
    lags = 2 * half
    slots = coef.shape[0] // 2 - batches // 2
    own = pltpu.make_async_copy(wh_ref, near.at[pl.ds(stations, stations)], own_sem.at[0])
    fill = pltpu.make_async_copy(table_ref, table, own_sem.at[1])
    own.start()
    fill.start()

    barrier = pltpu.get_barrier_semaphore()
    for other in (before, after):
        pl.semaphore_signal(barrier, inc=1, device_id={"pairs": other}, device_id_type=MESH)
    pl.semaphore_wait(barrier, 2)
    sends = []
    for index, (other, slot) in enumerate(((after, 0), (before, 2 * stations))):
        copy = pltpu.make_async_remote_copy(
            src_ref=wh_ref,
            dst_ref=near.at[pl.ds(slot, stations)],
            send_sem=send_sem.at[index],
            recv_sem=recv_sem.at[index],
            device_id={"pairs": other},
            device_id_type=MESH,
        )
        copy.start()
        sends.append(copy)

    coef[...] = jnp.zeros_like(coef)
    extra = vhi.shape[1] - count
    for h in range(2):
        rows = jnp.concatenate(
            [start_ref[:, h * half : (h + 1) * half], jnp.zeros((extra - RANK, half), F32)], 0
        )
        hi, lo = split(rows)
        vhi[h, count:, :] = hi
        vlo[h, count:, :] = lo
    own.wait()
    for copy in sends:
        copy.wait()

    turn = lax.rem(lax.broadcasted_iota(jnp.int32, (1, freq), 1), 4)
    swap = lax.rem(turn, 2) == 0
    sign_re = jnp.where((turn == 0) | (turn == 3), 1.0, -1.0)
    sign_im = jnp.where(turn >= 2, 1.0, -1.0)

    def pair_body(p, carry):
        first, second = rows_ref[p, 0], rows_ref[p, 1]
        relative = lax.rem(lax.div(second, stations) - me + 1 + ring, ring)
        at_a = stations + lax.rem(first, stations)
        relative = jnp.minimum(relative, 2)
        at_b = relative * stations + lax.rem(second, stations)
        a = near[at_a].astype(F32)
        b = near[at_b].astype(F32)
        re = a[0] * b[0] + a[1] * b[1]
        im = a[1] * b[0] - a[0] * b[1]
        low, high = pl.ds(pl.multiple_of(p * block, block), block), pl.ds(
            pl.multiple_of(count + p * block, block), block
        )
        cross[high, :freq] = re.astype(BF16)
        cross[high, freq:] = im.astype(BF16)
        cross[low, :freq] = (jnp.where(swap, im, re) * sign_re).astype(BF16)
        cross[low, freq:] = (jnp.where(swap, re, im) * sign_im).astype(BF16)
        return carry

    lax.fori_loop(0, pairs, pair_body, 0)
    fill.wait()
    tile = 256

    def lag_body(n, carry):
        columns = pl.ds(pl.multiple_of(n * tile, tile), tile)
        y = jnp.dot(cross[...], table[:, columns], preferred_element_type=F32)
        hi, lo = split(y)
        vhi[0, :count, columns] = hi[:count]
        vhi[1, :count, columns] = hi[count:]
        vlo[0, :count, columns] = lo[:count]
        vlo[1, :count, columns] = lo[count:]
        return carry

    lax.fori_loop(0, half // tile, lag_body, 0)

    gram = None
    for h in range(2):
        hi, lo = vhi[h], vlo[h]
        term = nt(hi, hi) + nt(lo, hi) + nt(hi, lo)
        gram = term if gram is None else gram + term
    lane = lax.broadcasted_iota(jnp.int32, (1, 128), 1)
    group = lax.div(lax.broadcasted_iota(jnp.int32, (1, 256), 1), 8)
    row_batch = lax.div(lax.broadcasted_iota(jnp.int32, (count, 1), 0), 8)
    batch = lax.broadcasted_iota(jnp.int32, (batches, 1), 0)
    mixed = lane >= segments
    near_lanes = lane < segments
    both = lane < segments + RANK
    shift = (128 - (count - 128) + segments) % 128

    def twelve(folded, tail):
        moved = pltpu.roll(tail, shift, 1)
        return jnp.where(near_lanes, folded, jnp.where(both, moved, 0.0))

    square[...] = twelve(fold8(gram[:count], group, row_batch), gram[:count, 128:])
    rows12 = [square[pl.ds(g, batches, stride=segments), :] for g in range(segments)]
    for r in range(RANK):
        line = jnp.broadcast_to(gram[count + r : count + r + 1], (batches, 256))
        rows12.append(twelve(fold8(line, group, batch), line[:, 128:]))

    def product(vectors):
        out = []
        for vector in vectors:
            total = vector[:, 0:1] * rows12[0]
            for j in range(1, segments + RANK):
                total = total + vector[:, j : j + 1] * rows12[j]
            out.append(total)
        return out

    weight = float(lags)
    held = [jnp.where(lane == segments + r, 1.0, 0.0) for r in range(RANK)]
    seen = [rows12[segments + r] for r in range(RANK)]
    for _ in range(TURNS):
        stepped = [weight * held[r] + jnp.where(near_lanes, seen[r], 0.0) for r in range(RANK)]
        image = product(stepped)
        small = [
            [jnp.sum(image[i] * stepped[j], axis=1, keepdims=True) for j in range(i + 1)]
            for i in range(RANK)
        ]
        lower = cholesky(small)
        held = solve(lower, stepped)
        seen = solve(lower, image)
    onto = [jnp.where(near_lanes, seen[r], 0.0) for r in range(RANK)]
    final = [weight * held[r] + onto[r] for r in range(RANK)]
    window = None
    for r in range(RANK):
        term = jnp.sum(onto[r], axis=1, keepdims=True) * held[r]
        window = term if window is None else window + term
    window = window * (1.0 / math.sqrt(segments))

    def spread(x):
        tail = pltpu.roll(jnp.where(mixed, x, 0.0), 128 - shift, 1)
        base = jnp.where(near_lanes, x, 0.0)
        for step in (8, 16, 32, 64):
            base = base + pltpu.roll(base, step, 1)
        left = jnp.where(group[:, :128] == batch, base, 0.0)
        right = jnp.where(group[:, 128:] == batch, base, 0.0) + tail
        return jnp.concatenate([left, right], 1)

    shown = spread(window)
    coef[:batches] = shown
    hours = lax.axis_size("hours")
    units = [spread(x) for x in final] + [shown * (1.0 / math.sqrt(windows * hours))]
    each = pairs // 2
    for r, unit in enumerate(units):
        for side in range(2):
            wide[side] = unit[:, side * 128 : (side + 1) * 128]
            total = wide.at[side][pl.ds(0, pairs, stride=windows), :]
            for w in range(1, windows):
                total = total + wide.at[side][pl.ds(w, pairs, stride=windows), :]
            for c in range(2):
                start = batches + c * slots + r * each
                columns = slice(side * 128, (side + 1) * 128)
                coef[start : start + each, columns] = total[c * each : (c + 1) * each]

    chi, clo = split(coef[...])
    for h in range(2):
        for n in range(half // 512):
            a, b = vhi[h, :, n * 512 : (n + 1) * 512], vlo[h, :, n * 512 : (n + 1) * 512]
            out = (
                jnp.dot(chi, a, preferred_element_type=F32)
                + jnp.dot(clo, a, preferred_element_type=F32)
                + jnp.dot(chi, b, preferred_element_type=F32)
            )
            columns = slice(h * half + n * 512, h * half + (n + 1) * 512)
            ws_ref[:, columns] = out[:batches]
            for c in range(2):
                part_ref[c, :, columns] = out[batches + c * slots : batches + (c + 1) * slots]


def merge_kernel(
    each, lags, part_ref, out_ref, sib, outgoing, incoming, total, grams, fin, theirs,
    sib_send, sib_recv, out_send, in_recv, gram_send, gram_recv, fin_send, fin_recv,
):
    hour = lax.axis_index("hours")
    chips = lax.axis_size("hours") // 2
    core, chip = lax.rem(hour, 2), lax.div(hour, 2)
    twin = hour + 1 - 2 * core
    width = lags // chips

    barrier = pltpu.get_barrier_semaphore()
    pl.semaphore_signal(barrier, inc=1, device_id={"hours": twin}, device_id_type=MESH)

    def target(d):
        return 2 * lax.rem(chip + d, chips) + core

    def greet(d, carry):
        pl.semaphore_signal(barrier, inc=1, device_id={"hours": target(d)}, device_id_type=MESH)
        return carry

    lax.fori_loop(1, chips, greet, 0)
    pl.semaphore_wait(barrier, chips)

    swap = pltpu.make_async_remote_copy(
        src_ref=part_ref.at[1 - core], dst_ref=sib, send_sem=sib_send, recv_sem=sib_recv,
        device_id={"hours": twin}, device_id_type=MESH,
    )
    swap.start()
    swap.wait()
    for q in range(chips):
        columns = slice(q * width, (q + 1) * width)
        outgoing[q] = part_ref[core, :, columns] + sib[:, columns]
    incoming[chip] = outgoing[chip]

    def sending(d):
        goal = lax.rem(chip + d, chips)
        return pltpu.make_async_remote_copy(
            src_ref=outgoing.at[goal], dst_ref=incoming.at[chip],
            send_sem=out_send.at[d - 1], recv_sem=in_recv.at[d - 1],
            device_id={"hours": 2 * goal + core}, device_id_type=MESH,
        )

    def start_send(d, carry):
        sending(d).start()
        return carry

    def wait_send(d, carry):
        sending(d).wait()
        return carry

    lax.fori_loop(1, chips, start_send, 0)
    lax.fori_loop(1, chips, wait_send, 0)
    merged = incoming[0]
    for q in range(1, chips):
        merged = merged + incoming[q]
    total[...] = merged
    vectors = [total[r * each : (r + 1) * each] for r in range(RANK)]
    lane = lax.broadcasted_iota(jnp.int32, (1, 128), 1)
    tile = jnp.zeros((each, 128), F32)
    order = [(i, j) for i in range(RANK) for j in range(i + 1)]
    for index, (i, j) in enumerate(order):
        value = jnp.sum(vectors[i] * vectors[j], axis=1, keepdims=True)
        tile = tile + jnp.where(lane == index, value, 0.0)
    grams[chip, :each] = tile

    def telling(d):
        goal = lax.rem(chip + d, chips)
        return pltpu.make_async_remote_copy(
            src_ref=grams.at[chip], dst_ref=grams.at[chip],
            send_sem=gram_send.at[d - 1], recv_sem=gram_recv.at[d - 1],
            device_id={"hours": 2 * goal + core}, device_id_type=MESH,
        )

    def start_tell(d, carry):
        telling(d).start()
        return carry

    def wait_tell(d, carry):
        telling(d).wait()
        return carry

    lax.fori_loop(1, chips, start_tell, 0)
    lax.fori_loop(1, chips, wait_tell, 0)
    summed = grams[0, :each]
    for q in range(1, chips):
        summed = summed + grams[q, :each]
    small = [[None] * RANK for _ in range(RANK)]
    for index, (i, j) in enumerate(order):
        small[i][j] = summed[:, index : index + 1]
    result = solve(cholesky(small), vectors)
    for r in range(RANK):
        fin[r * each : (r + 1) * each] = result[r] * math.sqrt(lags)
    fin[RANK * each :] = total[RANK * each :]

    last = pltpu.make_async_remote_copy(
        src_ref=fin, dst_ref=theirs, send_sem=fin_send, recv_sem=fin_recv,
        device_id={"hours": twin}, device_id_type=MESH,
    )
    last.start()
    own_half = width // 2

    def mine(x):
        return jnp.where(core == 0, x[:, :own_half], x[:, own_half:])

    out_ref[core] = mine(fin[...])
    last.wait()
    out_ref[1 - core] = mine(theirs[...])


def on_device(table, spectra, masks, pair_rows, start_basis):
    stations, windows, segments, _, freq = spectra.shape
    lags = start_basis.shape[1]
    half = lags // 2
    pairs = pair_rows.shape[0]
    block = windows * segments
    count = pairs * block
    batches = pairs * windows
    each = pairs // 2
    slots = 32
    chips = lax.axis_size("hours") // 2
    width = lags // chips
    whitened = whiten(spectra, masks).transpose(0, 3, 1, 2, 4).reshape(stations, 2, block, freq)
    vmem = pl.BlockSpec(memory_space=pltpu.VMEM)
    hbm = pl.BlockSpec(memory_space=pl.ANY)
    windows_out, part = pl.pallas_call(
        functools.partial(correlate_kernel, stations, segments, windows, pairs, freq, half),
        out_shape=(
            jax.ShapeDtypeStruct((batches, lags), F32),
            jax.ShapeDtypeStruct((2, slots, lags), F32),
        ),
        in_specs=[pl.BlockSpec(memory_space=pltpu.SMEM), hbm, hbm, vmem],
        out_specs=(vmem, vmem),
        scratch_shapes=[
            pltpu.VMEM((3 * stations, 2, block, freq), BF16),
            pltpu.VMEM((2 * count, 2 * freq), BF16),
            pltpu.VMEM((2 * freq, half), BF16),
            pltpu.VMEM((2, 256, half), BF16),
            pltpu.VMEM((2, 256, half), BF16),
            pltpu.VMEM((count, 128), F32),
            pltpu.VMEM((2, batches, 128), F32),
            pltpu.VMEM((batches + 2 * slots, 256), F32),
            pltpu.SemaphoreType.DMA((2,)),
            pltpu.SemaphoreType.DMA((2,)),
            pltpu.SemaphoreType.DMA((2,)),
        ],
        compiler_params=pltpu.CompilerParams(
            collective_id=0, has_side_effects=True, vmem_limit_bytes=40 << 20
        ),
        name="correlate",
    )(pair_rows, whitened, table, start_basis)
    merged = pl.pallas_call(
        functools.partial(merge_kernel, each, lags),
        out_shape=jax.ShapeDtypeStruct((2, slots, width // 2), F32),
        in_specs=[vmem],
        out_specs=vmem,
        scratch_shapes=[
            pltpu.VMEM((slots, lags), F32),
            pltpu.VMEM((chips, slots, width), F32),
            pltpu.VMEM((chips, slots, width), F32),
            pltpu.VMEM((slots, width), F32),
            pltpu.VMEM((chips, 8, 128), F32),
            pltpu.VMEM((slots, width), F32),
            pltpu.VMEM((slots, width), F32),
            pltpu.SemaphoreType.DMA,
            pltpu.SemaphoreType.DMA,
            pltpu.SemaphoreType.DMA((chips - 1,)),
            pltpu.SemaphoreType.DMA((chips - 1,)),
            pltpu.SemaphoreType.DMA((chips - 1,)),
            pltpu.SemaphoreType.DMA((chips - 1,)),
            pltpu.SemaphoreType.DMA,
            pltpu.SemaphoreType.DMA,
        ],
        compiler_params=pltpu.CompilerParams(
            collective_id=1, has_side_effects=True, vmem_limit_bytes=16 << 20
        ),
        name="merge",
    )(part)
    window_stacks = windows_out.reshape(pairs, windows, lags)
    basis = merged[:, : RANK * each].reshape(2, RANK, each, width // 2)
    basis = basis.transpose(0, 2, 1, 3).reshape(pairs, RANK, width // 2)
    stack = merged[:, RANK * each : (RANK + 1) * each].reshape(pairs, width // 2)
    return (window_stacks, stack, basis)


def solution(mesh):
    in_specs = (
        P("pairs", "hours", None, None, None),
        P("pairs", "hours", None),
        P("pairs", None),
        P(),
    )
    out_specs = (P("pairs", "hours", None), P("pairs", "hours"), P("pairs", None, "hours"))

    def whole(spectra, masks, pair_rows, start_basis):
        table = jnp.asarray(half_table(spectra.shape[4], start_basis.shape[1] // 2))
        return jax.shard_map(
            on_device, mesh=mesh, in_specs=(P(), *in_specs), out_specs=out_specs, check_vma=False
        )(table, spectra, masks, pair_rows, start_basis)

    return whole
```

```python
import functools
import math

import jax
import jax.numpy as jnp
import numpy as np
from jax import lax
from jax.experimental import pallas as pl
from jax.experimental.pallas import tpu as pltpu
from jax.sharding import PartitionSpec as P

BAND = 64
TURNS = 2
RANK = 4
MESH = pl.DeviceIdType.MESH
F32 = jnp.float32
BF16 = jnp.bfloat16


def full_table(freq, lags):
    bins = np.arange(1, freq + 1, dtype=np.int64)[:, None]
    shifts = np.arange(lags, dtype=np.int64)[None, :] - lags // 2
    phase = np.mod(bins * shifts, 2 * lags).astype(np.float64) * (math.pi / lags)
    scale = freq ** (-0.5)
    table = np.concatenate([np.cos(phase) * scale, -np.sin(phase) * scale], 0)
    return table.astype(np.float32).astype(jnp.bfloat16)


def whiten(spectra, masks):
    values = spectra.astype(F32)
    shape = values.shape
    banded = values.reshape(shape[:-1] + (shape[-1] // BAND, BAND))
    power = jnp.mean(banded * banded, axis=(3, 5), keepdims=True)
    scaled = banded * lax.rsqrt(power + 1e-06) * masks.astype(F32)[:, :, :, None, None, None]
    return scaled.reshape(shape).astype(BF16)


def nt(a, b):
    return lax.dot_general(a, b, (((1,), (1,)), ((), ())), preferred_element_type=F32)


def split(x):
    hi = x.astype(BF16)
    return hi, (x - hi.astype(F32)).astype(BF16)


def cholesky(gram):
    lower = [[None] * RANK for _ in range(RANK)]
    for row in range(RANK):
        for col in range(row + 1):
            total = gram[row][col]
            for inner in range(col):
                total = total - lower[row][inner] * lower[col][inner]
            lower[row][col] = jnp.sqrt(total) if row == col else total / lower[col][col]
    return lower


def solve(lower, vectors):
    result = []
    for row in range(RANK):
        current = vectors[row]
        for inner in range(row):
            current = current - lower[row][inner] * result[inner]
        result.append(current / lower[row][row])
    return result


def fold8(x, batch_of_lane, batch):
    kept = jnp.where(batch_of_lane == batch, x, 0.0)
    total = kept[:, :128] + kept[:, 128:]
    for shift in (64, 32, 16, 8):
        total = total + pltpu.roll(total, shift, 1)
    return total


def torus_offsets(chips):
    side = math.isqrt(chips)
    side = side if side * side == chips else 1
    other = chips // side
    offsets = [(dx, dy) for dx in range(other) for dy in range(side) if dx or dy]
    return side, other, sorted(
        offsets, key=lambda o: -(min(o[0], other - o[0]) + min(o[1], side - o[1]))
    )


def station_kernel(
    stations, segments, windows, pairs, freq, half,
    rows_ref, wh_ref, table_ref, start_ref,
    ws_ref, out_ref,
    near, cross, table, vhi, vlo, square, wide, coef,
    part, sib, keep, outgoing, incoming, summed_rows, grams, fin, theirs,
    send_sem, recv_sem, own_sem, out_send, in_recv, gram_send, gram_recv,
):
    me, ring = lax.axis_index("pairs"), lax.axis_size("pairs")
    after, before = lax.rem(me + 1, ring), lax.rem(me + ring - 1, ring)
    block = windows * segments
    count = pairs * block
    batches = pairs * windows
    lags = 2 * half
    slots = coef.shape[0] // 2 - batches // 2
    own = pltpu.make_async_copy(wh_ref, near.at[pl.ds(stations, stations)], own_sem.at[0])
    fill = pltpu.make_async_copy(table_ref, table, own_sem.at[1])
    own.start()
    fill.start()

    hour = lax.axis_index("hours")
    chips = lax.axis_size("hours") // 2
    core, chip = lax.rem(hour, 2), lax.div(hour, 2)
    twin = {"hours": hour + 1 - 2 * core}
    side, other_side, offsets = torus_offsets(chips)
    goals = [
        side * lax.rem(lax.div(chip, side) + dx, other_side) + lax.rem(lax.rem(chip, side) + dy, side)
        for dx, dy in offsets
    ]
    barrier = pltpu.get_barrier_semaphore()
    partners = [{"pairs": before}, {"pairs": after}, twin]
    partners += [{"hours": 2 * goal + core} for goal in goals]
    for other in partners:
        pl.semaphore_signal(barrier, inc=1, device_id=other, device_id_type=MESH)
    pl.semaphore_wait(barrier, len(partners))
    sends = []
    for index, (other, slot) in enumerate(((after, 0), (before, 2 * stations))):
        copy = pltpu.make_async_remote_copy(
            src_ref=wh_ref,
            dst_ref=near.at[pl.ds(slot, stations)],
            send_sem=send_sem.at[index],
            recv_sem=recv_sem.at[index],
            device_id={"pairs": other},
            device_id_type=MESH,
        )
        copy.start()
        sends.append(copy)

    coef[...] = jnp.zeros_like(coef)
    extra = vhi.shape[1] - count
    for h in range(2):
        rows = jnp.concatenate(
            [start_ref[:, h * half : (h + 1) * half], jnp.zeros((extra - RANK, half), F32)], 0
        )
        hi, lo = split(rows)
        vhi[h, count:, :] = hi
        vlo[h, count:, :] = lo
    own.wait()
    for copy in sends:
        copy.wait()

    def pair_body(p, carry):
        first, second = rows_ref[p, 0], rows_ref[p, 1]
        relative = lax.rem(lax.div(second, stations) - me + 1 + ring, ring)
        at_a = stations + lax.rem(first, stations)
        relative = jnp.minimum(relative, 2)
        at_b = relative * stations + lax.rem(second, stations)
        a = near[at_a].astype(F32)
        b = near[at_b].astype(F32)
        re = a[0] * b[0] + a[1] * b[1]
        im = a[1] * b[0] - a[0] * b[1]
        rows = pl.ds(pl.multiple_of(p * block, block), block)
        cross[rows, :freq] = re.astype(BF16)
        cross[rows, freq:] = im.astype(BF16)
        return carry

    lax.fori_loop(0, pairs, pair_body, 0, unroll=2)
    fill.wait()
    tile = 256

    for h in range(2):

        def lag_body(n, carry, h=h):
            columns = pl.ds(pl.multiple_of(n * tile, tile), tile)
            source = pl.ds(pl.multiple_of(h * half + n * tile, tile), tile)
            y = jnp.dot(cross[...], table[:, source], preferred_element_type=F32)
            hi, lo = split(y)
            vhi[h, :count, columns] = hi
            vlo[h, :count, columns] = lo
            return carry

        lax.fori_loop(0, half // tile, lag_body, 0)

    gram = None
    for h in range(2):
        hi, lo = vhi[h], vlo[h]
        term = nt(hi, hi) + nt(lo, hi) + nt(hi, lo)
        gram = term if gram is None else gram + term
    lane = lax.broadcasted_iota(jnp.int32, (1, 128), 1)
    group = lax.div(lax.broadcasted_iota(jnp.int32, (1, 256), 1), 8)
    row_batch = lax.div(lax.broadcasted_iota(jnp.int32, (count, 1), 0), 8)
    batch = lax.broadcasted_iota(jnp.int32, (batches, 1), 0)
    mixed = lane >= segments
    near_lanes = lane < segments
    both = lane < segments + RANK
    shift = (128 - (count - 128) + segments) % 128

    def twelve(folded, tail):
        moved = pltpu.roll(tail, shift, 1)
        return jnp.where(near_lanes, folded, jnp.where(both, moved, 0.0))

    square[...] = twelve(fold8(gram[:count], group, row_batch), gram[:count, 128:])
    rows12 = [square[pl.ds(g, batches, stride=segments), :] for g in range(segments)]
    for r in range(RANK):
        line = jnp.broadcast_to(gram[count + r : count + r + 1], (batches, 256))
        rows12.append(twelve(fold8(line, group, batch), line[:, 128:]))

    def product(vectors):
        out = []
        for vector in vectors:
            total = vector[:, 0:1] * rows12[0]
            for j in range(1, segments + RANK):
                total = total + vector[:, j : j + 1] * rows12[j]
            out.append(total)
        return out

    weight = float(lags)
    held = [jnp.where(lane == segments + r, 1.0, 0.0) for r in range(RANK)]
    seen = [rows12[segments + r] for r in range(RANK)]
    for _ in range(TURNS):
        stepped = [weight * held[r] + jnp.where(near_lanes, seen[r], 0.0) for r in range(RANK)]
        image = product(stepped)
        small = [
            [jnp.sum(image[i] * stepped[j], axis=1, keepdims=True) for j in range(i + 1)]
            for i in range(RANK)
        ]
        lower = cholesky(small)
        held = solve(lower, stepped)
        seen = solve(lower, image)
    onto = [jnp.where(near_lanes, seen[r], 0.0) for r in range(RANK)]
    final = [weight * held[r] + onto[r] for r in range(RANK)]
    window = None
    for r in range(RANK):
        term = jnp.sum(onto[r], axis=1, keepdims=True) * held[r]
        window = term if window is None else window + term
    window = window * (1.0 / math.sqrt(segments))

    def spread(x):
        tail = pltpu.roll(jnp.where(mixed, x, 0.0), 128 - shift, 1)
        base = jnp.where(near_lanes, x, 0.0)
        for step in (8, 16, 32, 64):
            base = base + pltpu.roll(base, step, 1)
        left = jnp.where(group[:, :128] == batch, base, 0.0)
        right = jnp.where(group[:, 128:] == batch, base, 0.0) + tail
        return jnp.concatenate([left, right], 1)

    shown = spread(window)
    coef[:batches] = shown
    hours = lax.axis_size("hours")
    units = [spread(x) for x in final] + [shown * (1.0 / math.sqrt(windows * hours))]
    each = pairs // 2
    for r, unit in enumerate(units):
        for side in range(2):
            wide[side] = unit[:, side * 128 : (side + 1) * 128]
            total = wide.at[side][pl.ds(0, pairs, stride=windows), :]
            for w in range(1, windows):
                total = total + wide.at[side][pl.ds(w, pairs, stride=windows), :]
            for c in range(2):
                start = batches + c * slots + r * each
                columns = slice(side * 128, (side + 1) * 128)
                coef[start : start + each, columns] = total[c * each : (c + 1) * each]

    chi, clo = split(coef[...])
    for h in range(2):
        for n in range(half // 512):
            a, b = vhi[h, :, n * 512 : (n + 1) * 512], vlo[h, :, n * 512 : (n + 1) * 512]
            out = (
                jnp.dot(chi, a, preferred_element_type=F32)
                + jnp.dot(clo, a, preferred_element_type=F32)
                + jnp.dot(chi, b, preferred_element_type=F32)
            )
            columns = slice(h * half + n * 512, h * half + (n + 1) * 512)
            ws_ref[:, columns] = out[:batches]
            for c in range(2):
                part[c, :, columns] = out[batches + c * slots : batches + (c + 1) * slots]


    width = lags // chips
    swap = pltpu.make_async_remote_copy(
        src_ref=part.at[1 - core], dst_ref=sib, send_sem=send_sem.at[2], recv_sem=recv_sem.at[2],
        device_id=twin, device_id_type=MESH,
    )
    swap.start()
    swap.wait()
    for q in range(chips):
        columns = slice(q * width, (q + 1) * width)
        keep[q] = part[core, :, columns] + sib[:, columns]
        outgoing[q] = keep[q].astype(BF16)
    sends = []
    for index, goal in enumerate(goals):
        copy = pltpu.make_async_remote_copy(
            src_ref=outgoing.at[goal], dst_ref=incoming.at[index],
            send_sem=out_send.at[index], recv_sem=in_recv.at[index],
            device_id={"hours": 2 * goal + core}, device_id_type=MESH,
        )
        copy.start()
        sends.append(copy)
    merged = keep[chip]
    for copy in reversed(sends):
        copy.wait()
    for index in range(chips - 1):
        merged = merged + incoming[index].astype(F32)
    summed_rows[...] = merged
    vectors = [summed_rows[r * each : (r + 1) * each] for r in range(RANK)]
    lane = lax.broadcasted_iota(jnp.int32, (1, 128), 1)
    tile = jnp.zeros((each, 128), F32)
    order = [(i, j) for i in range(RANK) for j in range(i + 1)]
    for index, (i, j) in enumerate(order):
        value = jnp.sum(vectors[i] * vectors[j], axis=1, keepdims=True)
        tile = tile + jnp.where(lane == index, value, 0.0)
    grams[chips - 1, :each] = tile

    sends = []
    for index, goal in enumerate(goals):
        copy = pltpu.make_async_remote_copy(
            src_ref=grams.at[chips - 1], dst_ref=grams.at[index],
            send_sem=gram_send.at[index], recv_sem=gram_recv.at[index],
            device_id={"hours": 2 * goal + core}, device_id_type=MESH,
        )
        copy.start()
        sends.append(copy)
    for copy in reversed(sends):
        copy.wait()
    summed = grams[0, :each]
    for q in range(1, chips):
        summed = summed + grams[q, :each]
    small = [[None] * RANK for _ in range(RANK)]
    for index, (i, j) in enumerate(order):
        small[i][j] = summed[:, index : index + 1]
    result = solve(cholesky(small), vectors)
    for r in range(RANK):
        fin[r * each : (r + 1) * each] = result[r] * math.sqrt(lags)
    fin[RANK * each :] = summed_rows[RANK * each :]

    last = pltpu.make_async_remote_copy(
        src_ref=fin, dst_ref=theirs, send_sem=send_sem.at[3], recv_sem=recv_sem.at[3],
        device_id=twin, device_id_type=MESH,
    )
    last.start()
    own_half = width // 2

    def mine(x):
        return jnp.where(core == 0, x[:, :own_half], x[:, own_half:])

    out_ref[core] = mine(fin[...])
    last.wait()
    out_ref[1 - core] = mine(theirs[...])


def on_device(table, spectra, masks, pair_rows, start_basis):
    stations, windows, segments, _, freq = spectra.shape
    lags = start_basis.shape[1]
    half = lags // 2
    pairs = pair_rows.shape[0]
    block = windows * segments
    count = pairs * block
    batches = pairs * windows
    each = pairs // 2
    slots = 32
    chips = lax.axis_size("hours") // 2
    width = lags // chips
    whitened = whiten(spectra, masks).transpose(0, 3, 1, 2, 4).reshape(stations, 2, block, freq)
    vmem = pl.BlockSpec(memory_space=pltpu.VMEM)
    windows_out, merged = pl.pallas_call(
        functools.partial(station_kernel, stations, segments, windows, pairs, freq, half),
        out_shape=(
            jax.ShapeDtypeStruct((batches, lags), F32),
            jax.ShapeDtypeStruct((2, slots, width // 2), F32),
        ),
        in_specs=[
            pl.BlockSpec(memory_space=pltpu.SMEM),
            pl.BlockSpec(memory_space=pl.ANY),
            pl.BlockSpec(memory_space=pltpu.HBM),
            vmem,
        ],
        out_specs=(vmem, vmem),
        scratch_shapes=[
            pltpu.VMEM((3 * stations, 2, block, freq), BF16),
            pltpu.VMEM((count, 2 * freq), BF16),
            pltpu.VMEM((2 * freq, lags), BF16),
            pltpu.VMEM((2, 256, half), BF16),
            pltpu.VMEM((2, 256, half), BF16),
            pltpu.VMEM((count, 128), F32),
            pltpu.VMEM((2, batches, 128), F32),
            pltpu.VMEM((batches + 2 * slots, 256), F32),
            pltpu.VMEM((2, slots, lags), F32),
            pltpu.VMEM((slots, lags), F32),
            pltpu.VMEM((chips, slots, width), F32),
            pltpu.VMEM((chips, slots, width), BF16),
            pltpu.VMEM((chips - 1, slots, width), BF16),
            pltpu.VMEM((slots, width), F32),
            pltpu.VMEM((chips, 8, 128), F32),
            pltpu.VMEM((slots, width), F32),
            pltpu.VMEM((slots, width), F32),
            pltpu.SemaphoreType.DMA((4,)),
            pltpu.SemaphoreType.DMA((4,)),
            pltpu.SemaphoreType.DMA((2,)),
            pltpu.SemaphoreType.DMA((chips - 1,)),
            pltpu.SemaphoreType.DMA((chips - 1,)),
            pltpu.SemaphoreType.DMA((chips - 1,)),
            pltpu.SemaphoreType.DMA((chips - 1,)),
        ],
        compiler_params=pltpu.CompilerParams(
            collective_id=0, has_side_effects=True, vmem_limit_bytes=48 << 20
        ),
        name="station_pairs",
    )(pair_rows, whitened, table, start_basis)
    window_stacks = windows_out.reshape(pairs, windows, lags)
    basis = merged[:, : RANK * each].reshape(2, RANK, each, width // 2)
    basis = basis.transpose(0, 2, 1, 3).reshape(pairs, RANK, width // 2)
    stack = merged[:, RANK * each : (RANK + 1) * each].reshape(pairs, width // 2)
    return (window_stacks, stack, basis)


def solution(mesh):
    in_specs = (
        P("pairs", "hours", None, None, None),
        P("pairs", "hours", None),
        P("pairs", None),
        P(),
    )
    out_specs = (P("pairs", "hours", None), P("pairs", "hours"), P("pairs", None, "hours"))

    def whole(spectra, masks, pair_rows, start_basis):
        table = jnp.asarray(full_table(spectra.shape[4], start_basis.shape[1]))
        return jax.shard_map(
            on_device, mesh=mesh, in_specs=(P(), *in_specs), out_specs=out_specs, check_vma=False
        )(table, spectra, masks, pair_rows, start_basis)

    return whole
```

```python
import functools
import math

import jax
import jax.numpy as jnp
import numpy as np
from jax import lax
from jax.experimental import pallas as pl
from jax.experimental.pallas import tpu as pltpu
from jax.sharding import PartitionSpec as P

BAND = 64
TURNS = 2
RANK = 4
MESH = pl.DeviceIdType.MESH
F32 = jnp.float32
BF16 = jnp.bfloat16


def full_table(freq, lags):
    bins = np.arange(1, freq + 1, dtype=np.int64)[:, None]
    shifts = np.arange(lags, dtype=np.int64)[None, :] - lags // 2
    phase = np.mod(bins * shifts, 2 * lags).astype(np.float64) * (math.pi / lags)
    scale = freq ** (-0.5)
    table = np.concatenate([np.cos(phase) * scale, -np.sin(phase) * scale], 0)
    return table.astype(np.float32).astype(jnp.bfloat16)


def whiten(x, mask, ones):
    rows, freq = x.shape[1:]
    square = x[0] * x[0] + x[1] * x[1]
    tiles = freq // 128
    stacked = jnp.concatenate([square[:, t * 128 : (t + 1) * 128] for t in range(tiles)], 0)
    hi, lo = split(stacked)
    power = jnp.dot(hi, ones, preferred_element_type=F32) + jnp.dot(
        lo, ones, preferred_element_type=F32
    )
    scale = lax.rsqrt(power * (0.5 / BAND) + 1e-06)
    scale = jnp.concatenate([scale[t * rows : (t + 1) * rows] for t in range(tiles)], 1) * mask
    return (x[0] * scale).astype(BF16), (x[1] * scale).astype(BF16)


def nt(a, b):
    return lax.dot_general(a, b, (((1,), (1,)), ((), ())), preferred_element_type=F32)


def split(x):
    hi = x.astype(BF16)
    return hi, (x - hi.astype(F32)).astype(BF16)


def cholesky(gram):
    lower = [[None] * RANK for _ in range(RANK)]
    for row in range(RANK):
        for col in range(row + 1):
            total = gram[row][col]
            for inner in range(col):
                total = total - lower[row][inner] * lower[col][inner]
            lower[row][col] = jnp.sqrt(total) if row == col else total / lower[col][col]
    return lower


def solve(lower, vectors):
    result = []
    for row in range(RANK):
        current = vectors[row]
        for inner in range(row):
            current = current - lower[row][inner] * result[inner]
        result.append(current / lower[row][row])
    return result


def fold8(x, batch_of_lane, batch):
    kept = jnp.where(batch_of_lane == batch, x, 0.0)
    total = kept[:, :128] + kept[:, 128:]
    for shift in (64, 32, 16, 8):
        total = total + pltpu.roll(total, shift, 1)
    return total


def torus_offsets(chips):
    side = math.isqrt(chips)
    side = side if side * side == chips else 1
    other = chips // side
    offsets = [(dx, dy) for dx in range(other) for dy in range(side) if dx or dy]
    return side, other, sorted(
        offsets, key=lambda o: -(min(o[0], other - o[0]) + min(o[1], side - o[1]))
    )


def station_kernel(
    stations, segments, windows, pairs, freq, half,
    rows_ref, masks_ref, raw_ref, table_ref, start_ref,
    ws_ref, out_ref,
    raw, mine, packed, wants, asked, near, cross, table, vhi, vlo, square, wide, coef,
    part, sib, keep, outgoing, incoming, summed_rows, grams, fin, theirs,
    list_send, list_recv, halo_send, halo_recv, send_sem, recv_sem, own_sem, out_send, in_recv, gram_send, gram_recv,
):
    me, ring = lax.axis_index("pairs"), lax.axis_size("pairs")
    after, before = lax.rem(me + 1, ring), lax.rem(me + ring - 1, ring)
    block = windows * segments
    count = pairs * block
    batches = pairs * windows
    lags = 2 * half
    slots = coef.shape[0] // 2 - batches // 2
    some = stations // 2
    own = pltpu.make_async_copy(raw_ref, raw, own_sem.at[0])
    fill = pltpu.make_async_copy(table_ref, table, own_sem.at[1])
    own.start()
    fill.start()

    hour = lax.axis_index("hours")
    chips = lax.axis_size("hours") // 2
    core, chip = lax.rem(hour, 2), lax.div(hour, 2)
    twin = {"hours": hour + 1 - 2 * core}
    side, other_side, offsets = torus_offsets(chips)
    goals = [
        side * lax.rem(lax.div(chip, side) + dx, other_side) + lax.rem(lax.rem(chip, side) + dy, side)
        for dx, dy in offsets
    ]
    barrier = pltpu.get_barrier_semaphore()
    partners = [{"pairs": before}, {"pairs": after}, twin]
    partners += [{"hours": 2 * goal + core} for goal in goals]
    for other in partners:
        pl.semaphore_signal(barrier, inc=1, device_id=other, device_id_type=MESH)

    keys = []
    for p in range(pairs):
        second = rows_ref[p, 1]
        relative = lax.rem(lax.div(second, stations) - me + 1 + ring, ring)
        keys.append(relative * stations + lax.rem(second, stations))
    place = []
    for side in range(2):
        taken, slots_of = 0, []
        picks = [0] * some
        for j in range(stations):
            found = keys[0] == 2 * side * stations + j
            for key in keys[1:]:
                found = found | (key == 2 * side * stations + j)
            used = found.astype(jnp.int32)
            slots_of.append(taken)
            for t in range(some):
                picks[t] = picks[t] + jnp.where(found & (taken == t), j, 0)
            taken = taken + used
        place.append(slots_of)
        for t in range(some):
            wants[side, t] = picks[t]
    pl.semaphore_wait(barrier, len(partners))
    asks = []
    for side, other in ((0, before), (1, after)):
        copy = pltpu.make_async_remote_copy(
            src_ref=wants.at[side], dst_ref=asked.at[1 - side],
            send_sem=list_send.at[side], recv_sem=list_recv.at[1 - side],
            device_id={"pairs": other}, device_id_type=MESH,
        )
        copy.start()
        asks.append(copy)

    own.wait()
    ones = jnp.where(
        lax.div(lax.broadcasted_iota(jnp.int32, (128, 128), 0), BAND)
        == lax.div(lax.broadcasted_iota(jnp.int32, (128, 128), 1), BAND),
        1.0, 0.0,
    ).astype(BF16)
    diagonal = lax.rem(
        lax.broadcasted_iota(jnp.int32, (block, segments), 0), segments
    ) == lax.broadcasted_iota(jnp.int32, (block, segments), 1)

    def station_body(s, carry):
        flags = masks_ref[s].astype(F32)
        lines = jnp.concatenate(
            [jnp.broadcast_to(flags[w : w + 1], (segments, segments)) for w in range(windows)], 0
        )
        mask = jnp.sum(jnp.where(diagonal, lines, 0.0), axis=1, keepdims=True)
        x = jnp.swapaxes(raw[s].astype(F32), 0, 1)
        re, im = whiten(x, mask, ones)
        mine[s, 0], mine[s, 1] = re, im
        near[some + s, 0], near[some + s, 1] = re, im
        return carry

    lax.fori_loop(0, stations, station_body, 0, unroll=2)
    sends = []
    for side, other in ((1, after), (0, before)):
        asks[1 - side].wait_recv()
        slot = 0 if side == 1 else some + stations
        for t in range(some):
            packed[side, t] = mine[jnp.clip(asked[side, t], 0, stations - 1)]
            copy = pltpu.make_async_remote_copy(
                src_ref=packed.at[side, t], dst_ref=near.at[slot + t],
                send_sem=halo_send.at[side, t], recv_sem=halo_recv.at[side, t],
                device_id={"pairs": other}, device_id_type=MESH,
            )
            copy.start()
            sends.append(copy)
    for copy in asks:
        copy.wait_send()

    coef[...] = jnp.zeros_like(coef)
    extra = vhi.shape[1] - count
    for h in range(2):
        rows = jnp.concatenate(
            [start_ref[:, h * half : (h + 1) * half], jnp.zeros((extra - RANK, half), F32)], 0
        )
        hi, lo = split(rows)
        vhi[h, count:, :] = hi
        vlo[h, count:, :] = lo
    for copy in sends:
        copy.wait()

    def pair_body(p, carry):
        first, second = rows_ref[p, 0], rows_ref[p, 1]
        relative = lax.rem(lax.div(second, stations) - me + 1 + ring, ring)
        local = lax.rem(second, stations)
        low, high = place[0][0], some + stations + place[1][0]
        for j in range(1, stations):
            low = jnp.where(local == j, place[0][j], low)
            high = jnp.where(local == j, some + stations + place[1][j], high)
        at_a = some + lax.rem(first, stations)
        at_b = jnp.where(relative == 0, low, jnp.where(relative == 1, some + local, high))
        at_b = jnp.clip(at_b, 0, 2 * stations - 1)
        a = near[at_a].astype(F32)
        b = near[at_b].astype(F32)
        re = a[0] * b[0] + a[1] * b[1]
        im = a[1] * b[0] - a[0] * b[1]
        rows = pl.ds(pl.multiple_of(p * block, block), block)
        cross[rows, :freq] = re.astype(BF16)
        cross[rows, freq:] = im.astype(BF16)
        return carry

    lax.fori_loop(0, pairs, pair_body, 0, unroll=2)
    fill.wait()
    tile = 256

    for h in range(2):

        def lag_body(n, carry, h=h):
            columns = pl.ds(pl.multiple_of(n * tile, tile), tile)
            source = pl.ds(pl.multiple_of(h * half + n * tile, tile), tile)
            y = jnp.dot(cross[...], table[:, source], preferred_element_type=F32)
            hi, lo = split(y)
            vhi[h, :count, columns] = hi
            vlo[h, :count, columns] = lo
            return carry

        lax.fori_loop(0, half // tile, lag_body, 0)

    gram = None
    for h in range(2):
        hi, lo = vhi[h], vlo[h]
        term = nt(hi, hi) + nt(lo, hi) + nt(hi, lo)
        gram = term if gram is None else gram + term
    lane = lax.broadcasted_iota(jnp.int32, (1, 128), 1)
    group = lax.div(lax.broadcasted_iota(jnp.int32, (1, 256), 1), 8)
    row_batch = lax.div(lax.broadcasted_iota(jnp.int32, (count, 1), 0), 8)
    batch = lax.broadcasted_iota(jnp.int32, (batches, 1), 0)
    mixed = lane >= segments
    near_lanes = lane < segments
    both = lane < segments + RANK
    shift = (128 - (count - 128) + segments) % 128

    def twelve(folded, tail):
        moved = pltpu.roll(tail, shift, 1)
        return jnp.where(near_lanes, folded, jnp.where(both, moved, 0.0))

    square[...] = twelve(fold8(gram[:count], group, row_batch), gram[:count, 128:])
    rows12 = [square[pl.ds(g, batches, stride=segments), :] for g in range(segments)]
    for r in range(RANK):
        line = jnp.broadcast_to(gram[count + r : count + r + 1], (batches, 256))
        rows12.append(twelve(fold8(line, group, batch), line[:, 128:]))

    def product(vectors):
        out = []
        for vector in vectors:
            total = vector[:, 0:1] * rows12[0]
            for j in range(1, segments + RANK):
                total = total + vector[:, j : j + 1] * rows12[j]
            out.append(total)
        return out

    weight = float(lags)
    held = [jnp.where(lane == segments + r, 1.0, 0.0) for r in range(RANK)]
    seen = [rows12[segments + r] for r in range(RANK)]
    for _ in range(TURNS):
        stepped = [weight * held[r] + jnp.where(near_lanes, seen[r], 0.0) for r in range(RANK)]
        image = product(stepped)
        small = [
            [jnp.sum(image[i] * stepped[j], axis=1, keepdims=True) for j in range(i + 1)]
            for i in range(RANK)
        ]
        lower = cholesky(small)
        held = solve(lower, stepped)
        seen = solve(lower, image)
    onto = [jnp.where(near_lanes, seen[r], 0.0) for r in range(RANK)]
    final = [weight * held[r] + onto[r] for r in range(RANK)]
    window = None
    for r in range(RANK):
        term = jnp.sum(onto[r], axis=1, keepdims=True) * held[r]
        window = term if window is None else window + term
    window = window * (1.0 / math.sqrt(segments))

    def spread(x):
        tail = pltpu.roll(jnp.where(mixed, x, 0.0), 128 - shift, 1)
        base = jnp.where(near_lanes, x, 0.0)
        for step in (8, 16, 32, 64):
            base = base + pltpu.roll(base, step, 1)
        left = jnp.where(group[:, :128] == batch, base, 0.0)
        right = jnp.where(group[:, 128:] == batch, base, 0.0) + tail
        return jnp.concatenate([left, right], 1)

    shown = spread(window)
    coef[:batches] = shown
    hours = lax.axis_size("hours")
    units = [spread(x) for x in final] + [shown * (1.0 / math.sqrt(windows * hours))]
    each = pairs // 2
    for r, unit in enumerate(units):
        for side in range(2):
            wide[side] = unit[:, side * 128 : (side + 1) * 128]
            total = wide.at[side][pl.ds(0, pairs, stride=windows), :]
            for w in range(1, windows):
                total = total + wide.at[side][pl.ds(w, pairs, stride=windows), :]
            for c in range(2):
                start = batches + c * slots + r * each
                columns = slice(side * 128, (side + 1) * 128)
                coef[start : start + each, columns] = total[c * each : (c + 1) * each]

    chi, clo = split(coef[...])
    for h in range(2):
        for n in range(half // 512):
            a, b = vhi[h, :, n * 512 : (n + 1) * 512], vlo[h, :, n * 512 : (n + 1) * 512]
            out = (
                jnp.dot(chi, a, preferred_element_type=F32)
                + jnp.dot(clo, a, preferred_element_type=F32)
                + jnp.dot(chi, b, preferred_element_type=F32)
            )
            columns = slice(h * half + n * 512, h * half + (n + 1) * 512)
            ws_ref[:, columns] = out[:batches]
            for c in range(2):
                part[c, :, columns] = out[batches + c * slots : batches + (c + 1) * slots]


    width = lags // chips
    swap = pltpu.make_async_remote_copy(
        src_ref=part.at[1 - core], dst_ref=sib, send_sem=send_sem.at[2], recv_sem=recv_sem.at[2],
        device_id=twin, device_id_type=MESH,
    )
    swap.start()
    swap.wait()
    for q in range(chips):
        columns = slice(q * width, (q + 1) * width)
        keep[q] = part[core, :, columns] + sib[:, columns]
        outgoing[q] = keep[q].astype(BF16)
    sends = []
    for index, goal in enumerate(goals):
        copy = pltpu.make_async_remote_copy(
            src_ref=outgoing.at[goal], dst_ref=incoming.at[index],
            send_sem=out_send.at[index], recv_sem=in_recv.at[index],
            device_id={"hours": 2 * goal + core}, device_id_type=MESH,
        )
        copy.start()
        sends.append(copy)
    merged = keep[chip]
    for copy in reversed(sends):
        copy.wait()
    for index in range(chips - 1):
        merged = merged + incoming[index].astype(F32)
    summed_rows[...] = merged
    vectors = [summed_rows[r * each : (r + 1) * each] for r in range(RANK)]
    lane = lax.broadcasted_iota(jnp.int32, (1, 128), 1)
    tile = jnp.zeros((each, 128), F32)
    order = [(i, j) for i in range(RANK) for j in range(i + 1)]
    for index, (i, j) in enumerate(order):
        value = jnp.sum(vectors[i] * vectors[j], axis=1, keepdims=True)
        tile = tile + jnp.where(lane == index, value, 0.0)
    grams[chips - 1, :each] = tile

    sends = []
    for index, goal in enumerate(goals):
        copy = pltpu.make_async_remote_copy(
            src_ref=grams.at[chips - 1], dst_ref=grams.at[index],
            send_sem=gram_send.at[index], recv_sem=gram_recv.at[index],
            device_id={"hours": 2 * goal + core}, device_id_type=MESH,
        )
        copy.start()
        sends.append(copy)
    for copy in reversed(sends):
        copy.wait()
    summed = grams[0, :each]
    for q in range(1, chips):
        summed = summed + grams[q, :each]
    small = [[None] * RANK for _ in range(RANK)]
    for index, (i, j) in enumerate(order):
        small[i][j] = summed[:, index : index + 1]
    result = solve(cholesky(small), vectors)
    for r in range(RANK):
        fin[r * each : (r + 1) * each] = result[r] * math.sqrt(lags)
    fin[RANK * each :] = summed_rows[RANK * each :]

    last = pltpu.make_async_remote_copy(
        src_ref=fin, dst_ref=theirs, send_sem=send_sem.at[3], recv_sem=recv_sem.at[3],
        device_id=twin, device_id_type=MESH,
    )
    last.start()
    own_half = width // 2

    def halved(x):
        return jnp.where(core == 0, x[:, :own_half], x[:, own_half:])

    out_ref[core] = halved(fin[...])
    last.wait()
    out_ref[1 - core] = halved(theirs[...])


def on_device(table, spectra, masks, pair_rows, start_basis):
    stations, windows, segments, _, freq = spectra.shape
    lags = start_basis.shape[1]
    half = lags // 2
    pairs = pair_rows.shape[0]
    block = windows * segments
    count = pairs * block
    batches = pairs * windows
    each = pairs // 2
    slots = 32
    chips = lax.axis_size("hours") // 2
    width = lags // chips
    raw = spectra.reshape(stations, block, 2, freq)
    vmem = pl.BlockSpec(memory_space=pltpu.VMEM)
    windows_out, merged = pl.pallas_call(
        functools.partial(station_kernel, stations, segments, windows, pairs, freq, half),
        out_shape=(
            jax.ShapeDtypeStruct((batches, lags), F32),
            jax.ShapeDtypeStruct((2, slots, width // 2), F32),
        ),
        in_specs=[
            pl.BlockSpec(memory_space=pltpu.SMEM),
            vmem,
            pl.BlockSpec(memory_space=pltpu.HBM),
            pl.BlockSpec(memory_space=pltpu.HBM),
            vmem,
        ],
        out_specs=(vmem, vmem),
        scratch_shapes=[
            pltpu.VMEM((stations, block, 2, freq), BF16),
            pltpu.VMEM((stations, 2, block, freq), BF16),
            pltpu.VMEM((2, stations // 2, 2, block, freq), BF16),
            pltpu.SMEM((2, stations // 2), jnp.int32),
            pltpu.SMEM((2, stations // 2), jnp.int32),
            pltpu.VMEM((2 * stations, 2, block, freq), BF16),
            pltpu.VMEM((count, 2 * freq), BF16),
            pltpu.VMEM((2 * freq, lags), BF16),
            pltpu.VMEM((2, 256, half), BF16),
            pltpu.VMEM((2, 256, half), BF16),
            pltpu.VMEM((count, 128), F32),
            pltpu.VMEM((2, batches, 128), F32),
            pltpu.VMEM((batches + 2 * slots, 256), F32),
            pltpu.VMEM((2, slots, lags), F32),
            pltpu.VMEM((slots, lags), F32),
            pltpu.VMEM((chips, slots, width), F32),
            pltpu.VMEM((chips, slots, width), BF16),
            pltpu.VMEM((chips - 1, slots, width), BF16),
            pltpu.VMEM((slots, width), F32),
            pltpu.VMEM((chips, 8, 128), F32),
            pltpu.VMEM((slots, width), F32),
            pltpu.VMEM((slots, width), F32),
            pltpu.SemaphoreType.DMA((2,)),
            pltpu.SemaphoreType.DMA((2,)),
            pltpu.SemaphoreType.DMA((2, stations // 2)),
            pltpu.SemaphoreType.DMA((2, stations // 2)),
            pltpu.SemaphoreType.DMA((4,)),
            pltpu.SemaphoreType.DMA((4,)),
            pltpu.SemaphoreType.DMA((2,)),
            pltpu.SemaphoreType.DMA((chips - 1,)),
            pltpu.SemaphoreType.DMA((chips - 1,)),
            pltpu.SemaphoreType.DMA((chips - 1,)),
            pltpu.SemaphoreType.DMA((chips - 1,)),
        ],
        compiler_params=pltpu.CompilerParams(
            collective_id=0, has_side_effects=True, vmem_limit_bytes=48 << 20
        ),
        name="station_pairs",
    )(pair_rows, masks, raw, table, start_basis)
    window_stacks = windows_out.reshape(pairs, windows, lags)
    basis = merged[:, : RANK * each].reshape(2, RANK, each, width // 2)
    basis = basis.transpose(0, 2, 1, 3).reshape(pairs, RANK, width // 2)
    stack = merged[:, RANK * each : (RANK + 1) * each].reshape(pairs, width // 2)
    return (window_stacks, stack, basis)


def solution(mesh):
    in_specs = (
        P("pairs", "hours", None, None, None),
        P("pairs", "hours", None),
        P("pairs", None),
        P(),
    )
    out_specs = (P("pairs", "hours", None), P("pairs", "hours"), P("pairs", None, "hours"))

    def whole(spectra, masks, pair_rows, start_basis):
        table = jnp.asarray(full_table(spectra.shape[4], start_basis.shape[1]))
        return jax.shard_map(
            on_device, mesh=mesh, in_specs=(P(), *in_specs), out_specs=out_specs, check_vma=False
        )(table, spectra, masks, pair_rows, start_basis)

    return whole
```

```python
import functools
import math

import jax
import jax.numpy as jnp
import numpy as np
from jax import lax
from jax.experimental import pallas as pl
from jax.experimental.pallas import tpu as pltpu
from jax.sharding import PartitionSpec as P

BAND = 64
TURNS = 2
RANK = 4
MESH = pl.DeviceIdType.MESH
F32 = jnp.float32
BF16 = jnp.bfloat16


def full_table(freq, lags):
    bins = np.arange(1, freq + 1, dtype=np.int64)[:, None]
    shifts = np.arange(lags, dtype=np.int64)[None, :] - lags // 2
    phase = np.mod(bins * shifts, 2 * lags).astype(np.float64) * (math.pi / lags)
    scale = freq ** (-0.5)
    table = np.concatenate([np.cos(phase) * scale, -np.sin(phase) * scale], 0)
    return table.astype(np.float32).astype(jnp.bfloat16)


def whiten(x, mask, ones):
    rows, freq = x.shape[1:]
    square = x[0] * x[0] + x[1] * x[1]
    tiles = freq // 128
    stacked = jnp.concatenate([square[:, t * 128 : (t + 1) * 128] for t in range(tiles)], 0)
    hi, lo = split(stacked)
    power = jnp.dot(hi, ones, preferred_element_type=F32) + jnp.dot(
        lo, ones, preferred_element_type=F32
    )
    scale = lax.rsqrt(power * (0.5 / BAND) + 1e-06)
    scale = jnp.concatenate([scale[t * rows : (t + 1) * rows] for t in range(tiles)], 1) * mask
    return (x[0] * scale).astype(BF16), (x[1] * scale).astype(BF16)


def nt(a, b):
    return lax.dot_general(a, b, (((1,), (1,)), ((), ())), preferred_element_type=F32)


def split(x):
    hi = x.astype(BF16)
    return hi, (x - hi.astype(F32)).astype(BF16)


def cholesky(gram):
    lower = [[None] * RANK for _ in range(RANK)]
    for row in range(RANK):
        for col in range(row + 1):
            total = gram[row][col]
            for inner in range(col):
                total = total - lower[row][inner] * lower[col][inner]
            lower[row][col] = jnp.sqrt(total) if row == col else total / lower[col][col]
    return lower


def solve(lower, vectors):
    result = []
    for row in range(RANK):
        current = vectors[row]
        for inner in range(row):
            current = current - lower[row][inner] * result[inner]
        result.append(current / lower[row][row])
    return result


def fold8(x, batch_of_lane, batch):
    kept = jnp.where(batch_of_lane == batch, x, 0.0)
    total = kept[:, :128] + kept[:, 128:]
    for shift in (64, 32, 16, 8):
        total = total + pltpu.roll(total, shift, 1)
    return total


def torus_offsets(chips):
    side = math.isqrt(chips)
    side = side if side * side == chips else 1
    other = chips // side
    offsets = [(dx, dy) for dx in range(other) for dy in range(side) if dx or dy]
    return side, other, sorted(
        offsets, key=lambda o: -(min(o[0], other - o[0]) + min(o[1], side - o[1]))
    )


def station_kernel(
    stations, segments, windows, pairs, freq, half,
    rows_hbm, masks_hbm, raw_ref, table_ref, start_hbm,
    ws_ref, out_ref,
    rows_ref, masks_ref, start_ref, raw, mine, packed, wants, asked, near, cross, table, vhi, vlo, square, wide, coef,
    part, sib, keep, outgoing, incoming, summed_rows, grams, fin, theirs,
    list_send, list_recv, halo_send, halo_recv, send_sem, recv_sem, own_sem, out_send, in_recv, gram_send, gram_recv,
):
    me, ring = lax.axis_index("pairs"), lax.axis_size("pairs")
    after, before = lax.rem(me + 1, ring), lax.rem(me + ring - 1, ring)
    block = windows * segments
    count = pairs * block
    batches = pairs * windows
    lags = 2 * half
    slots = coef.shape[0] // 2 - batches // 2
    some = stations // 2
    own = pltpu.make_async_copy(raw_ref, raw, own_sem.at[0])
    fill = pltpu.make_async_copy(table_ref, table, own_sem.at[1])
    gathers = [
        pltpu.make_async_copy(source, target, own_sem.at[2 + index])
        for index, (source, target) in enumerate(
            ((rows_hbm, rows_ref), (masks_hbm, masks_ref), (start_hbm, start_ref))
        )
    ]
    for copy in gathers:
        copy.start()
    own.start()
    fill.start()

    hour = lax.axis_index("hours")
    chips = lax.axis_size("hours") // 2
    core, chip = lax.rem(hour, 2), lax.div(hour, 2)
    twin = {"hours": hour + 1 - 2 * core}
    side, other_side, offsets = torus_offsets(chips)
    goals = [
        side * lax.rem(lax.div(chip, side) + dx, other_side) + lax.rem(lax.rem(chip, side) + dy, side)
        for dx, dy in offsets
    ]
    barrier = pltpu.get_barrier_semaphore()
    partners = [{"pairs": before}, {"pairs": after}, twin]
    partners += [{"hours": 2 * goal + core} for goal in goals]
    for other in partners:
        pl.semaphore_signal(barrier, inc=1, device_id=other, device_id_type=MESH)

    gathers[0].wait()
    keys = []
    for p in range(pairs):
        second = rows_ref[1, p]
        relative = lax.rem(lax.div(second, stations) - me + 1 + ring, ring)
        keys.append(relative * stations + lax.rem(second, stations))
    place = []
    for side in range(2):
        taken, slots_of = 0, []
        picks = [0] * some
        for j in range(stations):
            found = keys[0] == 2 * side * stations + j
            for key in keys[1:]:
                found = found | (key == 2 * side * stations + j)
            used = found.astype(jnp.int32)
            slots_of.append(taken)
            for t in range(some):
                picks[t] = picks[t] + jnp.where(found & (taken == t), j, 0)
            taken = taken + used
        place.append(slots_of)
        for t in range(some):
            wants[side, t] = picks[t]
    pl.semaphore_wait(barrier, len(partners))
    asks = []
    for side, other in ((0, before), (1, after)):
        copy = pltpu.make_async_remote_copy(
            src_ref=wants.at[side], dst_ref=asked.at[1 - side],
            send_sem=list_send.at[side], recv_sem=list_recv.at[1 - side],
            device_id={"pairs": other}, device_id_type=MESH,
        )
        copy.start()
        asks.append(copy)

    own.wait()
    for copy in gathers[1:]:
        copy.wait()
    ones = jnp.where(
        lax.div(lax.broadcasted_iota(jnp.int32, (128, 128), 0), BAND)
        == lax.div(lax.broadcasted_iota(jnp.int32, (128, 128), 1), BAND),
        1.0, 0.0,
    ).astype(BF16)
    diagonal = lax.rem(
        lax.broadcasted_iota(jnp.int32, (block, segments), 0), segments
    ) == lax.broadcasted_iota(jnp.int32, (block, segments), 1)

    def station_body(s, carry):
        flags = masks_ref[s].astype(F32)
        lines = jnp.concatenate(
            [jnp.broadcast_to(flags[w : w + 1], (segments, segments)) for w in range(windows)], 0
        )
        mask = jnp.sum(jnp.where(diagonal, lines, 0.0), axis=1, keepdims=True)
        x = jnp.swapaxes(raw[s].astype(F32), 0, 1)
        re, im = whiten(x, mask, ones)
        mine[s, 0], mine[s, 1] = re, im
        near[some + s, 0], near[some + s, 1] = re, im
        return carry

    lax.fori_loop(0, stations, station_body, 0, unroll=2)
    sends = []
    for side, other in ((1, after), (0, before)):
        asks[1 - side].wait_recv()
        slot = 0 if side == 1 else some + stations
        for t in range(some):
            packed[side, t] = mine[jnp.clip(asked[side, t], 0, stations - 1)]
            copy = pltpu.make_async_remote_copy(
                src_ref=packed.at[side, t], dst_ref=near.at[slot + t],
                send_sem=halo_send.at[side, t], recv_sem=halo_recv.at[side, t],
                device_id={"pairs": other}, device_id_type=MESH,
            )
            copy.start()
            sends.append(copy)
    for copy in asks:
        copy.wait_send()

    coef[...] = jnp.zeros_like(coef)
    extra = vhi.shape[1] - count
    for h in range(2):
        rows = jnp.concatenate(
            [start_ref[:, h * half : (h + 1) * half], jnp.zeros((extra - RANK, half), F32)], 0
        )
        hi, lo = split(rows)
        vhi[h, count:, :] = hi
        vlo[h, count:, :] = lo
    for copy in sends:
        copy.wait()

    def pair_body(p, carry):
        first, second = rows_ref[0, p], rows_ref[1, p]
        relative = lax.rem(lax.div(second, stations) - me + 1 + ring, ring)
        local = lax.rem(second, stations)
        low, high = place[0][0], some + stations + place[1][0]
        for j in range(1, stations):
            low = jnp.where(local == j, place[0][j], low)
            high = jnp.where(local == j, some + stations + place[1][j], high)
        at_a = some + lax.rem(first, stations)
        at_b = jnp.where(relative == 0, low, jnp.where(relative == 1, some + local, high))
        at_b = jnp.clip(at_b, 0, 2 * stations - 1)
        a = near[at_a].astype(F32)
        b = near[at_b].astype(F32)
        re = a[0] * b[0] + a[1] * b[1]
        im = a[1] * b[0] - a[0] * b[1]
        rows = pl.ds(pl.multiple_of(p * block, block), block)
        cross[rows, :freq] = re.astype(BF16)
        cross[rows, freq:] = im.astype(BF16)
        return carry

    lax.fori_loop(0, pairs, pair_body, 0, unroll=2)
    fill.wait()
    tile = 256

    for h in range(2):

        def lag_body(n, carry, h=h):
            columns = pl.ds(pl.multiple_of(n * tile, tile), tile)
            source = pl.ds(pl.multiple_of(h * half + n * tile, tile), tile)
            y = jnp.dot(cross[...], table[:, source], preferred_element_type=F32)
            hi, lo = split(y)
            vhi[h, :count, columns] = hi
            vlo[h, :count, columns] = lo
            return carry

        lax.fori_loop(0, half // tile, lag_body, 0)

    gram = None
    for h in range(2):
        hi, lo = vhi[h], vlo[h]
        term = nt(hi, hi) + nt(lo, hi) + nt(hi, lo)
        gram = term if gram is None else gram + term
    lane = lax.broadcasted_iota(jnp.int32, (1, 128), 1)
    group = lax.div(lax.broadcasted_iota(jnp.int32, (1, 256), 1), 8)
    row_batch = lax.div(lax.broadcasted_iota(jnp.int32, (count, 1), 0), 8)
    batch = lax.broadcasted_iota(jnp.int32, (batches, 1), 0)
    mixed = lane >= segments
    near_lanes = lane < segments
    both = lane < segments + RANK
    shift = (128 - (count - 128) + segments) % 128

    def twelve(folded, tail):
        moved = pltpu.roll(tail, shift, 1)
        return jnp.where(near_lanes, folded, jnp.where(both, moved, 0.0))

    square[...] = twelve(fold8(gram[:count], group, row_batch), gram[:count, 128:])
    rows12 = [square[pl.ds(g, batches, stride=segments), :] for g in range(segments)]
    for r in range(RANK):
        line = jnp.broadcast_to(gram[count + r : count + r + 1], (batches, 256))
        rows12.append(twelve(fold8(line, group, batch), line[:, 128:]))

    def product(vectors):
        out = []
        for vector in vectors:
            total = vector[:, 0:1] * rows12[0]
            for j in range(1, segments + RANK):
                total = total + vector[:, j : j + 1] * rows12[j]
            out.append(total)
        return out

    weight = float(lags)
    held = [jnp.where(lane == segments + r, 1.0, 0.0) for r in range(RANK)]
    seen = [rows12[segments + r] for r in range(RANK)]
    for _ in range(TURNS):
        stepped = [weight * held[r] + jnp.where(near_lanes, seen[r], 0.0) for r in range(RANK)]
        image = product(stepped)
        small = [
            [jnp.sum(image[i] * stepped[j], axis=1, keepdims=True) for j in range(i + 1)]
            for i in range(RANK)
        ]
        lower = cholesky(small)
        held = solve(lower, stepped)
        seen = solve(lower, image)
    onto = [jnp.where(near_lanes, seen[r], 0.0) for r in range(RANK)]
    final = [weight * held[r] + onto[r] for r in range(RANK)]
    window = None
    for r in range(RANK):
        term = jnp.sum(onto[r], axis=1, keepdims=True) * held[r]
        window = term if window is None else window + term
    window = window * (1.0 / math.sqrt(segments))

    def spread(x):
        tail = pltpu.roll(jnp.where(mixed, x, 0.0), 128 - shift, 1)
        base = jnp.where(near_lanes, x, 0.0)
        for step in (8, 16, 32, 64):
            base = base + pltpu.roll(base, step, 1)
        left = jnp.where(group[:, :128] == batch, base, 0.0)
        right = jnp.where(group[:, 128:] == batch, base, 0.0) + tail
        return jnp.concatenate([left, right], 1)

    shown = spread(window)
    coef[:batches] = shown
    hours = lax.axis_size("hours")
    units = [spread(x) for x in final] + [shown * (1.0 / math.sqrt(windows * hours))]
    each = pairs // 2
    for r, unit in enumerate(units):
        for side in range(2):
            wide[side] = unit[:, side * 128 : (side + 1) * 128]
            total = wide.at[side][pl.ds(0, pairs, stride=windows), :]
            for w in range(1, windows):
                total = total + wide.at[side][pl.ds(w, pairs, stride=windows), :]
            for c in range(2):
                start = batches + c * slots + r * each
                columns = slice(side * 128, (side + 1) * 128)
                coef[start : start + each, columns] = total[c * each : (c + 1) * each]

    chi, clo = split(coef[...])
    for h in range(2):
        for n in range(half // 512):
            a, b = vhi[h, :, n * 512 : (n + 1) * 512], vlo[h, :, n * 512 : (n + 1) * 512]
            out = (
                jnp.dot(chi, a, preferred_element_type=F32)
                + jnp.dot(clo, a, preferred_element_type=F32)
                + jnp.dot(chi, b, preferred_element_type=F32)
            )
            columns = slice(h * half + n * 512, h * half + (n + 1) * 512)
            ws_ref[:, columns] = out[:batches]
            for c in range(2):
                part[c, :, columns] = out[batches + c * slots : batches + (c + 1) * slots]


    width = lags // chips
    swap = pltpu.make_async_remote_copy(
        src_ref=part.at[1 - core], dst_ref=sib, send_sem=send_sem.at[2], recv_sem=recv_sem.at[2],
        device_id=twin, device_id_type=MESH,
    )
    swap.start()
    swap.wait()
    for q in range(chips):
        columns = slice(q * width, (q + 1) * width)
        keep[q] = part[core, :, columns] + sib[:, columns]
        outgoing[q] = keep[q].astype(BF16)
    sends = []
    for index, goal in enumerate(goals):
        copy = pltpu.make_async_remote_copy(
            src_ref=outgoing.at[goal], dst_ref=incoming.at[index],
            send_sem=out_send.at[index], recv_sem=in_recv.at[index],
            device_id={"hours": 2 * goal + core}, device_id_type=MESH,
        )
        copy.start()
        sends.append(copy)
    merged = keep[chip]
    for copy in reversed(sends):
        copy.wait()
    for index in range(chips - 1):
        merged = merged + incoming[index].astype(F32)
    summed_rows[...] = merged
    vectors = [summed_rows[r * each : (r + 1) * each] for r in range(RANK)]
    lane = lax.broadcasted_iota(jnp.int32, (1, 128), 1)
    tile = jnp.zeros((each, 128), F32)
    order = [(i, j) for i in range(RANK) for j in range(i + 1)]
    for index, (i, j) in enumerate(order):
        value = jnp.sum(vectors[i] * vectors[j], axis=1, keepdims=True)
        tile = tile + jnp.where(lane == index, value, 0.0)
    grams[chips - 1, :each] = tile

    sends = []
    for index, goal in enumerate(goals):
        copy = pltpu.make_async_remote_copy(
            src_ref=grams.at[chips - 1], dst_ref=grams.at[index],
            send_sem=gram_send.at[index], recv_sem=gram_recv.at[index],
            device_id={"hours": 2 * goal + core}, device_id_type=MESH,
        )
        copy.start()
        sends.append(copy)
    for copy in reversed(sends):
        copy.wait()
    summed = grams[0, :each]
    for q in range(1, chips):
        summed = summed + grams[q, :each]
    small = [[None] * RANK for _ in range(RANK)]
    for index, (i, j) in enumerate(order):
        small[i][j] = summed[:, index : index + 1]
    result = solve(cholesky(small), vectors)
    for r in range(RANK):
        fin[r * each : (r + 1) * each] = result[r] * math.sqrt(lags)
    fin[RANK * each :] = summed_rows[RANK * each :]

    last = pltpu.make_async_remote_copy(
        src_ref=fin, dst_ref=theirs, send_sem=send_sem.at[3], recv_sem=recv_sem.at[3],
        device_id=twin, device_id_type=MESH,
    )
    last.start()
    own_half = width // 2

    def halved(x):
        return jnp.where(core == 0, x[:, :own_half], x[:, own_half:])

    out_ref[core] = halved(fin[...])
    last.wait()
    out_ref[1 - core] = halved(theirs[...])


def finish_kernel(pairs, windows, windows_ref, merged_ref, ws_ref, stack_ref, basis_ref):
    each = pairs // 2
    for p in range(pairs):
        ws_ref[p] = windows_ref[windows * p : windows * (p + 1)]
    rows = merged_ref[...]
    stack_ref[...] = jnp.concatenate(
        [rows[c, RANK * each : (RANK + 1) * each] for c in range(2)], 0
    )
    for p in range(pairs):
        c, q = divmod(p, each)
        for r in range(RANK):
            basis_ref[p, r : r + 1] = rows[c, r * each + q : r * each + q + 1]


def on_device(table, spectra, masks, pair_rows, start_basis):
    stations, windows, segments, _, freq = spectra.shape
    lags = start_basis.shape[1]
    half = lags // 2
    pairs = pair_rows.shape[0]
    block = windows * segments
    count = pairs * block
    batches = pairs * windows
    each = pairs // 2
    slots = 32
    chips = lax.axis_size("hours") // 2
    width = lags // chips
    raw = spectra.reshape(stations, block, 2, freq)
    vmem = pl.BlockSpec(memory_space=pltpu.VMEM)
    windows_out, merged = pl.pallas_call(
        functools.partial(station_kernel, stations, segments, windows, pairs, freq, half),
        out_shape=(
            pltpu.VMEM((batches, lags), F32),
            pltpu.VMEM((2, slots, width // 2), F32),
        ),
        in_specs=[
            pl.BlockSpec(memory_space=pltpu.HBM),
        ]
        * 5,
        out_specs=(vmem, vmem),
        scratch_shapes=[
            pltpu.SMEM((2, pairs), jnp.int32),
            pltpu.VMEM((stations, windows, segments), jnp.int32),
            pltpu.VMEM((RANK, lags), F32),
            pltpu.VMEM((stations, block, 2, freq), BF16),
            pltpu.VMEM((stations, 2, block, freq), BF16),
            pltpu.VMEM((2, stations // 2, 2, block, freq), BF16),
            pltpu.SMEM((2, stations // 2), jnp.int32),
            pltpu.SMEM((2, stations // 2), jnp.int32),
            pltpu.VMEM((2 * stations, 2, block, freq), BF16),
            pltpu.VMEM((count, 2 * freq), BF16),
            pltpu.VMEM((2 * freq, lags), BF16),
            pltpu.VMEM((2, 256, half), BF16),
            pltpu.VMEM((2, 256, half), BF16),
            pltpu.VMEM((count, 128), F32),
            pltpu.VMEM((2, batches, 128), F32),
            pltpu.VMEM((batches + 2 * slots, 256), F32),
            pltpu.VMEM((2, slots, lags), F32),
            pltpu.VMEM((slots, lags), F32),
            pltpu.VMEM((chips, slots, width), F32),
            pltpu.VMEM((chips, slots, width), BF16),
            pltpu.VMEM((chips - 1, slots, width), BF16),
            pltpu.VMEM((slots, width), F32),
            pltpu.VMEM((chips, 8, 128), F32),
            pltpu.VMEM((slots, width), F32),
            pltpu.VMEM((slots, width), F32),
            pltpu.SemaphoreType.DMA((2,)),
            pltpu.SemaphoreType.DMA((2,)),
            pltpu.SemaphoreType.DMA((2, stations // 2)),
            pltpu.SemaphoreType.DMA((2, stations // 2)),
            pltpu.SemaphoreType.DMA((4,)),
            pltpu.SemaphoreType.DMA((4,)),
            pltpu.SemaphoreType.DMA((5,)),
            pltpu.SemaphoreType.DMA((chips - 1,)),
            pltpu.SemaphoreType.DMA((chips - 1,)),
            pltpu.SemaphoreType.DMA((chips - 1,)),
            pltpu.SemaphoreType.DMA((chips - 1,)),
        ],
        compiler_params=pltpu.CompilerParams(
            collective_id=0, has_side_effects=True, vmem_limit_bytes=60 << 20
        ),
        name="station_pairs",
    )(pair_rows.T, masks, raw, table, start_basis)
    return pl.pallas_call(
        functools.partial(finish_kernel, pairs, windows),
        out_shape=(
            jax.ShapeDtypeStruct((pairs, windows, lags), F32),
            jax.ShapeDtypeStruct((pairs, width // 2), F32),
            jax.ShapeDtypeStruct((pairs, RANK, width // 2), F32),
        ),
        in_specs=[vmem, vmem],
        out_specs=(vmem, vmem, vmem),
        compiler_params=pltpu.CompilerParams(vmem_limit_bytes=4 << 20),
        name="outputs",
    )(windows_out, merged)


def solution(mesh):
    in_specs = (
        P("pairs", "hours", None, None, None),
        P("pairs", "hours", None),
        P("pairs", None),
        P(),
    )
    out_specs = (P("pairs", "hours", None), P("pairs", "hours"), P("pairs", None, "hours"))

    def whole(spectra, masks, pair_rows, start_basis):
        table = jnp.asarray(full_table(spectra.shape[4], start_basis.shape[1]))
        return jax.shard_map(
            on_device, mesh=mesh, in_specs=(P(), *in_specs), out_specs=out_specs, check_vma=False
        )(table, spectra, masks, pair_rows, start_basis)

    return whole
```

```python
import functools
import math

import jax
import jax.numpy as jnp
import numpy as np
from jax import lax
from jax.experimental import pallas as pl
from jax.experimental.pallas import tpu as pltpu
from jax.sharding import PartitionSpec as P

BAND = 64
TURNS = 2
RANK = 4
MESH = pl.DeviceIdType.MESH
F32 = jnp.float32
BF16 = jnp.bfloat16


def half_table(freq, half):
    bins = np.arange(1, freq + 1, dtype=np.int64)[:, None]
    shifts = np.arange(half, dtype=np.int64)[None, :]
    phase = np.mod(bins * shifts, 4 * half).astype(np.float64) * (math.pi / (2 * half))
    scale = freq ** (-0.5)
    table = np.concatenate([np.cos(phase) * scale, -np.sin(phase) * scale], 0)
    return table.astype(np.float32).astype(jnp.bfloat16)


def whiten(x, mask, ones):
    rows, freq = x.shape[1:]
    square = x[0] * x[0] + x[1] * x[1]
    tiles = freq // 128
    stacked = jnp.concatenate([square[:, t * 128 : (t + 1) * 128] for t in range(tiles)], 0)
    hi, lo = split(stacked)
    power = jnp.dot(hi, ones, preferred_element_type=F32) + jnp.dot(
        lo, ones, preferred_element_type=F32
    )
    scale = lax.rsqrt(power * (0.5 / BAND) + 1e-06)
    scale = jnp.concatenate([scale[t * rows : (t + 1) * rows] for t in range(tiles)], 1) * mask
    return (x[0] * scale).astype(BF16), (x[1] * scale).astype(BF16)


def nt(a, b):
    return lax.dot_general(a, b, (((1,), (1,)), ((), ())), preferred_element_type=F32)


def split(x):
    hi = x.astype(BF16)
    return hi, (x - hi.astype(F32)).astype(BF16)


def cholesky(gram):
    lower = [[None] * RANK for _ in range(RANK)]
    for row in range(RANK):
        for col in range(row + 1):
            total = gram[row][col]
            for inner in range(col):
                total = total - lower[row][inner] * lower[col][inner]
            lower[row][col] = jnp.sqrt(total) if row == col else total / lower[col][col]
    return lower


def solve(lower, vectors):
    result = []
    for row in range(RANK):
        current = vectors[row]
        for inner in range(row):
            current = current - lower[row][inner] * result[inner]
        result.append(current / lower[row][row])
    return result


def fold8(x, batch_of_lane, batch):
    kept = jnp.where(batch_of_lane == batch, x, 0.0)
    total = kept[:, :128] + kept[:, 128:]
    for shift in (64, 32, 16, 8):
        total = total + pltpu.roll(total, shift, 1)
    return total


def torus_offsets(chips):
    side = math.isqrt(chips)
    side = side if side * side == chips else 1
    other = chips // side
    offsets = [(dx, dy) for dx in range(other) for dy in range(side) if dx or dy]
    return side, other, sorted(
        offsets, key=lambda o: -(min(o[0], other - o[0]) + min(o[1], side - o[1]))
    )


def station_kernel(
    stations, segments, windows, pairs, freq, half,
    rows_hbm, masks_hbm, raw_ref, table_ref, start_hbm,
    ws_ref, out_ref,
    rows_ref, masks_ref, start_ref, raw, mine, packed, wants, asked, places, near,
    cross, table, held_rows, square, wide, coef,
    part, sib, outgoing, incoming, summed_rows, grams, fin, theirs,
    list_send, list_recv, halo_send, halo_recv, send_sem, recv_sem, own_sem, fill_sem,
    out_send, in_recv, gram_send, gram_recv,
):
    me, ring = lax.axis_index("pairs"), lax.axis_size("pairs")
    after, before = lax.rem(me + 1, ring), lax.rem(me + ring - 1, ring)
    block = windows * segments
    count = pairs * block
    batches = pairs * windows
    lags = 2 * half
    slots = coef.shape[0] // 2 - batches // 2
    some = stations // 2
    own = pltpu.make_async_copy(raw_ref, raw, own_sem.at[0])
    cuts = 4
    band = 2 * freq // cuts
    fills = [
        pltpu.make_async_copy(
            table_ref.at[pl.ds(i * band, band)], table.at[pl.ds(i * band, band)], fill_sem.at[i]
        )
        for i in range(cuts)
    ]
    gathers = [
        pltpu.make_async_copy(source, target, own_sem.at[2 + index])
        for index, (source, target) in enumerate(
            ((rows_hbm, rows_ref), (masks_hbm, masks_ref), (start_hbm, start_ref))
        )
    ]
    for copy in gathers:
        copy.start()
    own.start()
    for copy in fills:
        copy.start()

    hour = lax.axis_index("hours")
    chips = lax.axis_size("hours") // 2
    core, chip = lax.rem(hour, 2), lax.div(hour, 2)
    twin = {"hours": hour + 1 - 2 * core}
    across, other_side, offsets = torus_offsets(chips)
    goals = [
        across * lax.rem(lax.div(chip, across) + dx, other_side)
        + lax.rem(lax.rem(chip, across) + dy, across)
        for dx, dy in offsets
    ]
    barrier = pltpu.get_barrier_semaphore()
    partners = [{"pairs": before}, {"pairs": after}, twin]
    partners += [{"hours": 2 * goal + core} for goal in goals]
    for other in partners:
        pl.semaphore_signal(barrier, inc=1, device_id=other, device_id_type=MESH)

    gathers[0].wait()
    keys = []
    for p in range(pairs):
        second = rows_ref[1, p]
        relative = lax.rem(lax.div(second, stations) - me + 1 + ring, ring)
        keys.append(relative * stations + lax.rem(second, stations))
    place = []
    for side in range(2):
        taken, slots_of = 0, []
        picks = [0] * some
        for j in range(stations):
            found = keys[0] == 2 * side * stations + j
            for key in keys[1:]:
                found = found | (key == 2 * side * stations + j)
            used = found.astype(jnp.int32)
            slots_of.append(taken)
            for t in range(some):
                picks[t] = picks[t] + jnp.where(found & (taken == t), j, 0)
            taken = taken + used
        place.append(slots_of)
        for t in range(some):
            wants[side, t] = picks[t]
    pl.semaphore_wait(barrier, len(partners))
    asks = []
    for side, other in ((0, before), (1, after)):
        copy = pltpu.make_async_remote_copy(
            src_ref=wants.at[side], dst_ref=asked.at[1 - side],
            send_sem=list_send.at[side], recv_sem=list_recv.at[1 - side],
            device_id={"pairs": other}, device_id_type=MESH,
        )
        copy.start()
        asks.append(copy)

    own.wait()
    for copy in gathers[1:]:
        copy.wait()
    ones = jnp.where(
        lax.div(lax.broadcasted_iota(jnp.int32, (128, 128), 0), BAND)
        == lax.div(lax.broadcasted_iota(jnp.int32, (128, 128), 1), BAND),
        1.0, 0.0,
    ).astype(BF16)
    diagonal = lax.rem(
        lax.broadcasted_iota(jnp.int32, (block, segments), 0), segments
    ) == lax.broadcasted_iota(jnp.int32, (block, segments), 1)

    def station_body(s, carry):
        flags = masks_ref[s].astype(F32)
        lines = jnp.concatenate(
            [jnp.broadcast_to(flags[w : w + 1], (segments, segments)) for w in range(windows)], 0
        )
        mask = jnp.sum(jnp.where(diagonal, lines, 0.0), axis=1, keepdims=True)
        x = jnp.swapaxes(raw[s].astype(F32), 0, 1)
        re, im = whiten(x, mask, ones)
        mine[s, 0], mine[s, 1] = re, im
        near[some + s, 0], near[some + s, 1] = re, im
        return carry

    lax.fori_loop(0, stations, station_body, 0, unroll=2)
    sends = []
    for side, other in ((1, after), (0, before)):
        asks[1 - side].wait_recv()
        slot = 0 if side == 1 else some + stations
        for t in range(some):
            packed[side, t] = mine[jnp.clip(asked[side, t], 0, stations - 1)]
            copy = pltpu.make_async_remote_copy(
                src_ref=packed.at[side, t], dst_ref=near.at[slot + t],
                send_sem=halo_send.at[side, t], recv_sem=halo_recv.at[side, t],
                device_id={"pairs": other}, device_id_type=MESH,
            )
            copy.start()
            sends.append(copy)
    for copy in asks:
        copy.wait_send()

    coef[...] = jnp.zeros_like(coef)
    extra = held_rows.shape[0] - count
    held_rows[count:, :] = jnp.concatenate(
        [start_ref[...], jnp.zeros((extra - RANK, lags), F32)], 0
    ).astype(BF16)
    for p in range(pairs):
        local = lax.rem(rows_ref[1, p], stations)
        relative = lax.div(keys[p], stations)
        low, high = place[0][0], some + stations + place[1][0]
        for j in range(1, stations):
            low = jnp.where(local == j, place[0][j], low)
            high = jnp.where(local == j, some + stations + place[1][j], high)
        at_b = jnp.where(relative == 0, low, jnp.where(relative == 1, some + local, high))
        places[0, p] = some + lax.rem(rows_ref[0, p], stations)
        places[1, p] = jnp.clip(at_b, 0, 2 * stations - 1)
    turn = lax.rem(lax.broadcasted_iota(jnp.int32, (block, freq), 1), 4)
    swap_lanes = lax.rem(turn, 2) == 0
    sign_re = jnp.where((turn == 0) | (turn == 3), 1.0, -1.0)[:1].astype(BF16)
    sign_im = jnp.where(turn >= 2, 1.0, -1.0)[:1].astype(BF16)
    for copy in sends:
        copy.wait()

    def pair_body(p, carry):
        a = near[places[0, p]].astype(F32)
        b = near[places[1, p]].astype(F32)
        re = a[0] * b[0] + a[1] * b[1]
        im = a[1] * b[0] - a[0] * b[1]
        re, im = re.astype(BF16), im.astype(BF16)
        low = pl.ds(pl.multiple_of(p * block, block), block)
        high = pl.ds(pl.multiple_of(count + p * block, block), block)
        cross[high, :freq] = re
        cross[high, freq:] = im
        cross[low, :freq] = jnp.where(swap_lanes, im, re) * sign_re
        cross[low, freq:] = jnp.where(swap_lanes, re, im) * sign_im
        return carry

    lax.fori_loop(0, pairs, pair_body, 0, unroll=3)
    for copy in fills:
        copy.wait()
    tile = 256

    def lag_body(n, carry):
        y = jnp.dot(
            cross[...],
            table[:, pl.ds(pl.multiple_of(n * tile, tile), tile)],
            preferred_element_type=F32,
        ).astype(BF16)
        held_rows[:count, pl.ds(pl.multiple_of(n * tile, tile), tile)] = y[:count]
        held_rows[:count, pl.ds(pl.multiple_of(half + n * tile, tile), tile)] = y[count:]
        return carry

    lax.fori_loop(0, half // tile, lag_body, 0)
    gram = nt(held_rows[...], held_rows[...])
    lane = lax.broadcasted_iota(jnp.int32, (1, 128), 1)
    group = lax.div(lax.broadcasted_iota(jnp.int32, (1, 256), 1), 8)
    row_batch = lax.div(lax.broadcasted_iota(jnp.int32, (count, 1), 0), 8)
    batch = lax.broadcasted_iota(jnp.int32, (batches, 1), 0)
    mixed = lane >= segments
    near_lanes = lane < segments
    both = lane < segments + RANK
    shift = (128 - (count - 128) + segments) % 128

    def twelve(folded, tail):
        moved = pltpu.roll(tail, shift, 1)
        return jnp.where(near_lanes, folded, jnp.where(both, moved, 0.0))

    square[...] = twelve(fold8(gram[:count], group, row_batch), gram[:count, 128:])
    rows12 = [square[pl.ds(g, batches, stride=segments), :] for g in range(segments)]
    for r in range(RANK):
        line = jnp.broadcast_to(gram[count + r : count + r + 1], (batches, 256))
        rows12.append(twelve(fold8(line, group, batch), line[:, 128:]))

    def product(vectors):
        out = []
        for vector in vectors:
            total = vector[:, 0:1] * rows12[0]
            for j in range(1, segments + RANK):
                total = total + vector[:, j : j + 1] * rows12[j]
            out.append(total)
        return out

    weight = float(lags)
    held = [jnp.where(lane == segments + r, 1.0, 0.0) for r in range(RANK)]
    seen = [rows12[segments + r] for r in range(RANK)]
    for _ in range(TURNS):
        stepped = [weight * held[r] + jnp.where(near_lanes, seen[r], 0.0) for r in range(RANK)]
        image = product(stepped)
        small = [
            [jnp.sum(image[i] * stepped[j], axis=1, keepdims=True) for j in range(i + 1)]
            for i in range(RANK)
        ]
        lower = cholesky(small)
        held = solve(lower, stepped)
        seen = solve(lower, image)
    onto = [jnp.where(near_lanes, seen[r], 0.0) for r in range(RANK)]
    final = [weight * held[r] + onto[r] for r in range(RANK)]
    window = None
    for r in range(RANK):
        term = jnp.sum(onto[r], axis=1, keepdims=True) * held[r]
        window = term if window is None else window + term
    window = window * (1.0 / math.sqrt(segments))

    def spread(x):
        tail = pltpu.roll(jnp.where(mixed, x, 0.0), 128 - shift, 1)
        base = jnp.where(near_lanes, x, 0.0)
        for step in (8, 16, 32, 64):
            base = base + pltpu.roll(base, step, 1)
        left = jnp.where(group[:, :128] == batch, base, 0.0)
        right = jnp.where(group[:, 128:] == batch, base, 0.0) + tail
        return jnp.concatenate([left, right], 1)

    shown = spread(window)
    coef[:batches] = shown
    hours = lax.axis_size("hours")
    units = [spread(x) for x in final] + [shown * (1.0 / math.sqrt(windows * hours))]
    each = pairs // 2
    for r, unit in enumerate(units):
        for side in range(2):
            wide[side] = unit[:, side * 128 : (side + 1) * 128]
            total = wide.at[side][pl.ds(0, pairs, stride=windows), :]
            for w in range(1, windows):
                total = total + wide.at[side][pl.ds(w, pairs, stride=windows), :]
            for c in range(2):
                start = batches + c * slots + r * each
                columns = slice(side * 128, (side + 1) * 128)
                coef[start : start + each, columns] = total[c * each : (c + 1) * each]

    coefs = jnp.concatenate(split(coef[...]), 0)
    size = coef.shape[0]
    width = lags // chips
    chunk = across * width
    row, column = lax.div(chip, across), lax.rem(chip, across)
    rows_order = sorted(range(other_side), key=lambda d: -min(d, other_side - d))
    columns_order = sorted(range(across), key=lambda d: -min(d, across - d))
    swaps, sends, merged = [], [], None

    def scatter(i):
        kept = None
        swaps[i].wait()
        for dy in columns_order:
            goal_column = lax.rem(column + dy, across)
            lanes = pl.ds(pl.multiple_of(goal_column * width, width), width)
            block_sum = part[i, core, :, lanes] + sib[i, :, lanes]
            if rows_order[i] == 0 and dy == 0:
                kept = block_sum
                continue
            index = len(sends)
            outgoing[index] = block_sum.astype(BF16)
            goal = across * lax.rem(row + rows_order[i], other_side) + goal_column
            copy = pltpu.make_async_remote_copy(
                src_ref=outgoing.at[index], dst_ref=incoming.at[index],
                send_sem=out_send.at[index], recv_sem=in_recv.at[index],
                device_id={"hours": 2 * goal + core}, device_id_type=MESH,
            )
            copy.start()
            sends.append(copy)
        return kept

    for i, dx in enumerate(rows_order):
        goal_row = lax.rem(row + dx, other_side)
        columns = pl.ds(pl.multiple_of(goal_row * chunk, chunk), chunk)
        out = jnp.dot(coefs, held_rows[:, columns], preferred_element_type=F32)
        out = out[:size] + out[size:]
        ws_ref[:, columns] = out[:batches]
        for c in range(2):
            part[i, c] = out[batches + c * slots : batches + (c + 1) * slots]
        copy = pltpu.make_async_remote_copy(
            src_ref=part.at[i, 1 - core], dst_ref=sib.at[i],
            send_sem=send_sem.at[i], recv_sem=recv_sem.at[i],
            device_id=twin, device_id_type=MESH,
        )
        copy.start()
        swaps.append(copy)
        if i > 0:
            scatter(i - 1)
    merged = scatter(other_side - 1)
    for copy in sends:
        copy.wait()
    for index in range(chips - 1):
        merged = merged + incoming[index].astype(F32)
    summed_rows[...] = merged
    vectors = [summed_rows[r * each : (r + 1) * each] for r in range(RANK)]
    lane = lax.broadcasted_iota(jnp.int32, (1, 128), 1)
    tile = jnp.zeros((each, 128), F32)
    order = [(i, j) for i in range(RANK) for j in range(i + 1)]
    for index, (i, j) in enumerate(order):
        value = jnp.sum(vectors[i] * vectors[j], axis=1, keepdims=True)
        tile = tile + jnp.where(lane == index, value, 0.0)
    grams[chips - 1, :each] = tile

    sends = []
    for index, goal in enumerate(goals):
        copy = pltpu.make_async_remote_copy(
            src_ref=grams.at[chips - 1], dst_ref=grams.at[index],
            send_sem=gram_send.at[index], recv_sem=gram_recv.at[index],
            device_id={"hours": 2 * goal + core}, device_id_type=MESH,
        )
        copy.start()
        sends.append(copy)
    for copy in reversed(sends):
        copy.wait()
    summed = grams[0, :each]
    for q in range(1, chips):
        summed = summed + grams[q, :each]
    small = [[None] * RANK for _ in range(RANK)]
    for index, (i, j) in enumerate(order):
        small[i][j] = summed[:, index : index + 1]
    result = solve(cholesky(small), vectors)
    for r in range(RANK):
        fin[r * each : (r + 1) * each] = result[r] * math.sqrt(lags)
    fin[RANK * each :] = summed_rows[RANK * each :]

    last = pltpu.make_async_remote_copy(
        src_ref=fin, dst_ref=theirs, send_sem=send_sem.at[other_side], recv_sem=recv_sem.at[other_side],
        device_id=twin, device_id_type=MESH,
    )
    last.start()
    own_half = width // 2

    def halved(x):
        return jnp.where(core == 0, x[:, :own_half], x[:, own_half:])

    out_ref[core] = halved(fin[...])
    last.wait()
    out_ref[1 - core] = halved(theirs[...])


def finish_kernel(pairs, windows, windows_ref, merged_ref, ws_ref, stack_ref, basis_ref):
    each = pairs // 2
    for p in range(pairs):
        ws_ref[p] = windows_ref[windows * p : windows * (p + 1)]
    rows = merged_ref[...]
    stack_ref[...] = jnp.concatenate(
        [rows[c, RANK * each : (RANK + 1) * each] for c in range(2)], 0
    )
    for p in range(pairs):
        c, q = divmod(p, each)
        for r in range(RANK):
            basis_ref[p, r : r + 1] = rows[c, r * each + q : r * each + q + 1]


def on_device(table, spectra, masks, pair_rows, start_basis):
    stations, windows, segments, _, freq = spectra.shape
    lags = start_basis.shape[1]
    half = lags // 2
    pairs = pair_rows.shape[0]
    block = windows * segments
    count = pairs * block
    batches = pairs * windows
    each = pairs // 2
    slots = 32
    chips = lax.axis_size("hours") // 2
    width = lags // chips
    rows_of_chips = torus_offsets(chips)[1]
    raw = spectra.reshape(stations, block, 2, freq)
    vmem = pl.BlockSpec(memory_space=pltpu.VMEM)
    windows_out, merged = pl.pallas_call(
        functools.partial(station_kernel, stations, segments, windows, pairs, freq, half),
        out_shape=(
            pltpu.VMEM((batches, lags), F32),
            pltpu.VMEM((2, slots, width // 2), F32),
        ),
        in_specs=[
            pl.BlockSpec(memory_space=pltpu.HBM),
        ]
        * 5,
        out_specs=(vmem, vmem),
        scratch_shapes=[
            pltpu.SMEM((2, pairs), jnp.int32),
            pltpu.VMEM((stations, windows, segments), jnp.int32),
            pltpu.VMEM((RANK, lags), F32),
            pltpu.VMEM((stations, block, 2, freq), BF16),
            pltpu.VMEM((stations, 2, block, freq), BF16),
            pltpu.VMEM((2, stations // 2, 2, block, freq), BF16),
            pltpu.SMEM((2, stations // 2), jnp.int32),
            pltpu.SMEM((2, stations // 2), jnp.int32),
            pltpu.SMEM((2, pairs), jnp.int32),
            pltpu.VMEM((2 * stations, 2, block, freq), BF16),
            pltpu.VMEM((2 * count, 2 * freq), BF16),
            pltpu.VMEM((2 * freq, half), BF16),
            pltpu.VMEM((256, lags), BF16),
            pltpu.VMEM((count, 128), F32),
            pltpu.VMEM((2, batches, 128), F32),
            pltpu.VMEM((batches + 2 * slots, 256), F32),
            pltpu.VMEM((rows_of_chips, 2, slots, lags // rows_of_chips), F32),
            pltpu.VMEM((rows_of_chips, slots, lags // rows_of_chips), F32),
            pltpu.VMEM((chips - 1, slots, width), BF16),
            pltpu.VMEM((chips - 1, slots, width), BF16),
            pltpu.VMEM((slots, width), F32),
            pltpu.VMEM((chips, 8, 128), F32),
            pltpu.VMEM((slots, width), F32),
            pltpu.VMEM((slots, width), F32),
            pltpu.SemaphoreType.DMA((2,)),
            pltpu.SemaphoreType.DMA((2,)),
            pltpu.SemaphoreType.DMA((2, stations // 2)),
            pltpu.SemaphoreType.DMA((2, stations // 2)),
            pltpu.SemaphoreType.DMA((rows_of_chips + 1,)),
            pltpu.SemaphoreType.DMA((rows_of_chips + 1,)),
            pltpu.SemaphoreType.DMA((5,)),
            pltpu.SemaphoreType.DMA((4,)),
            pltpu.SemaphoreType.DMA((chips - 1,)),
            pltpu.SemaphoreType.DMA((chips - 1,)),
            pltpu.SemaphoreType.DMA((chips - 1,)),
            pltpu.SemaphoreType.DMA((chips - 1,)),
        ],
        compiler_params=pltpu.CompilerParams(
            collective_id=0, has_side_effects=True, vmem_limit_bytes=60 << 20
        ),
        name="station_pairs",
    )(pair_rows.T, masks, raw, table, start_basis)
    return pl.pallas_call(
        functools.partial(finish_kernel, pairs, windows),
        out_shape=(
            jax.ShapeDtypeStruct((pairs, windows, lags), F32),
            jax.ShapeDtypeStruct((pairs, width // 2), F32),
            jax.ShapeDtypeStruct((pairs, RANK, width // 2), F32),
        ),
        in_specs=[vmem, vmem],
        out_specs=(vmem, vmem, vmem),
        compiler_params=pltpu.CompilerParams(vmem_limit_bytes=4 << 20),
        name="outputs",
    )(windows_out, merged)


def solution(mesh):
    in_specs = (
        P("pairs", "hours", None, None, None),
        P("pairs", "hours", None),
        P("pairs", None),
        P(),
    )
    out_specs = (P("pairs", "hours", None), P("pairs", "hours"), P("pairs", None, "hours"))

    def whole(spectra, masks, pair_rows, start_basis):
        table = jnp.asarray(half_table(spectra.shape[4], start_basis.shape[1] // 2))
        return jax.shard_map(
            on_device, mesh=mesh, in_specs=(P(), *in_specs), out_specs=out_specs, check_vma=False
        )(table, spectra, masks, pair_rows, start_basis)

    return whole
```

```python
import functools
import math

import jax
import jax.numpy as jnp
import numpy as np
from jax import lax
from jax.experimental import pallas as pl
from jax.experimental.pallas import tpu as pltpu
from jax.sharding import PartitionSpec as P

BAND = 64
TURNS = 2
RANK = 4
MESH = pl.DeviceIdType.MESH
F32 = jnp.float32
BF16 = jnp.bfloat16


def half_table(freq, half):
    bins = np.arange(1, freq + 1, dtype=np.int64)[:, None]
    shifts = np.arange(half, dtype=np.int64)[None, :]
    phase = np.mod(bins * shifts, 4 * half).astype(np.float64) * (math.pi / (2 * half))
    scale = freq ** (-0.5)
    table = np.concatenate([np.cos(phase) * scale, -np.sin(phase) * scale], 0)
    return table.astype(np.float32).astype(jnp.bfloat16)


def whiten(x, mask, ones):
    rows, freq = x.shape[1:]
    square = x[0] * x[0] + x[1] * x[1]
    tiles = freq // 128
    stacked = jnp.concatenate([square[:, t * 128 : (t + 1) * 128] for t in range(tiles)], 0)
    hi, lo = split(stacked)
    power = jnp.dot(hi, ones, preferred_element_type=F32) + jnp.dot(
        lo, ones, preferred_element_type=F32
    )
    scale = lax.rsqrt(power * (0.5 / BAND) + 1e-06)
    scale = jnp.concatenate([scale[t * rows : (t + 1) * rows] for t in range(tiles)], 1) * mask
    return (x[0] * scale).astype(BF16), (x[1] * scale).astype(BF16)


def nt(a, b):
    return lax.dot_general(a, b, (((1,), (1,)), ((), ())), preferred_element_type=F32)


def split(x):
    hi = x.astype(BF16)
    return hi, (x - hi.astype(F32)).astype(BF16)


def cholesky(gram):
    lower = [[None] * RANK for _ in range(RANK)]
    for row in range(RANK):
        for col in range(row + 1):
            total = gram[row][col]
            for inner in range(col):
                total = total - lower[row][inner] * lower[col][inner]
            lower[row][col] = jnp.sqrt(total) if row == col else total / lower[col][col]
    return lower


def solve(lower, vectors):
    result = []
    for row in range(RANK):
        current = vectors[row]
        for inner in range(row):
            current = current - lower[row][inner] * result[inner]
        result.append(current / lower[row][row])
    return result


def fold8(x, batch_of_lane, batch):
    kept = jnp.where(batch_of_lane == batch, x, 0.0)
    total = kept[:, :128] + kept[:, 128:]
    for shift in (64, 32, 16, 8):
        total = total + pltpu.roll(total, shift, 1)
    return total


def torus_offsets(chips):
    side = math.isqrt(chips)
    side = side if side * side == chips else 1
    other = chips // side
    offsets = [(dx, dy) for dx in range(other) for dy in range(side) if dx or dy]
    return side, other, sorted(
        offsets, key=lambda o: -(min(o[0], other - o[0]) + min(o[1], side - o[1]))
    )


def station_kernel(
    stations, segments, windows, pairs, freq, half,
    rows_hbm, masks_hbm, raw_ref, table_ref, start_hbm,
    ws_ref, out_ref,
    rows_ref, masks_ref, start_ref, raw, mine, packed, wants, asked, places, near,
    cross, table, held_rows, square, wide, coef,
    part, incoming, summed_rows, theirs, own_gram, grams,
    list_send, list_recv, halo_send, halo_recv, send_sem, recv_sem, own_sem, fill_sem,
    out_send, in_recv, gram_send, gram_recv,
):
    me, ring = lax.axis_index("pairs"), lax.axis_size("pairs")
    after, before = lax.rem(me + 1, ring), lax.rem(me + ring - 1, ring)
    block = windows * segments
    count = pairs * block
    batches = pairs * windows
    lags = 2 * half
    slots = coef.shape[0] // 2 - batches // 2
    some = stations // 2
    own = pltpu.make_async_copy(raw_ref, raw, own_sem.at[0])
    cuts = 4
    band = 2 * freq // cuts
    fills = [
        pltpu.make_async_copy(
            table_ref.at[pl.ds(i * band, band)], table.at[pl.ds(i * band, band)], fill_sem.at[i]
        )
        for i in range(cuts)
    ]
    gathers = [
        pltpu.make_async_copy(source, target, own_sem.at[2 + index])
        for index, (source, target) in enumerate(
            ((rows_hbm, rows_ref), (masks_hbm, masks_ref), (start_hbm, start_ref))
        )
    ]
    for copy in gathers:
        copy.start()
    own.start()
    for copy in fills:
        copy.start()

    hour = lax.axis_index("hours")
    chips = lax.axis_size("hours") // 2
    core, chip = lax.rem(hour, 2), lax.div(hour, 2)
    twin = {"hours": hour + 1 - 2 * core}
    across, other_side, offsets = torus_offsets(chips)
    row, column = lax.div(chip, across), lax.rem(chip, across)
    places_from = [(dx, dy, flip) for dx, dy in offsets + [(0, 0)] for flip in range(2)][:-2]
    places_from.append((0, 0, 1))

    def device(place):
        dx, dy, flip = place
        goal = across * lax.rem(row + dx, other_side) + lax.rem(column + dy, across)
        return {"hours": 2 * goal + (core if flip == 0 else 1 - core)}

    barrier = pltpu.get_barrier_semaphore()
    partners = [{"pairs": before}, {"pairs": after}]
    partners += [device(place) for place in places_from]
    for other in partners:
        pl.semaphore_signal(barrier, inc=1, device_id=other, device_id_type=MESH)

    gathers[0].wait()
    keys = []
    for p in range(pairs):
        second = rows_ref[1, p]
        relative = lax.rem(lax.div(second, stations) - me + 1 + ring, ring)
        keys.append(relative * stations + lax.rem(second, stations))
    place = []
    for side in range(2):
        taken, slots_of = 0, []
        picks = [0] * some
        for j in range(stations):
            found = keys[0] == 2 * side * stations + j
            for key in keys[1:]:
                found = found | (key == 2 * side * stations + j)
            used = found.astype(jnp.int32)
            slots_of.append(taken)
            for t in range(some):
                picks[t] = picks[t] + jnp.where(found & (taken == t), j, 0)
            taken = taken + used
        place.append(slots_of)
        for t in range(some):
            wants[side, t] = picks[t]
    pl.semaphore_wait(barrier, len(partners))
    asks = []
    for side, other in ((0, before), (1, after)):
        copy = pltpu.make_async_remote_copy(
            src_ref=wants.at[side], dst_ref=asked.at[1 - side],
            send_sem=list_send.at[side], recv_sem=list_recv.at[1 - side],
            device_id={"pairs": other}, device_id_type=MESH,
        )
        copy.start()
        asks.append(copy)

    own.wait()
    for copy in gathers[1:]:
        copy.wait()
    ones = jnp.where(
        lax.div(lax.broadcasted_iota(jnp.int32, (128, 128), 0), BAND)
        == lax.div(lax.broadcasted_iota(jnp.int32, (128, 128), 1), BAND),
        1.0, 0.0,
    ).astype(BF16)
    diagonal = lax.rem(
        lax.broadcasted_iota(jnp.int32, (block, segments), 0), segments
    ) == lax.broadcasted_iota(jnp.int32, (block, segments), 1)

    def station_body(s, carry):
        flags = masks_ref[s].astype(F32)
        lines = jnp.concatenate(
            [jnp.broadcast_to(flags[w : w + 1], (segments, segments)) for w in range(windows)], 0
        )
        mask = jnp.sum(jnp.where(diagonal, lines, 0.0), axis=1, keepdims=True)
        x = jnp.swapaxes(raw[s].astype(F32), 0, 1)
        re, im = whiten(x, mask, ones)
        mine[s, 0], mine[s, 1] = re, im
        near[some + s, 0], near[some + s, 1] = re, im
        return carry

    lax.fori_loop(0, stations, station_body, 0, unroll=2)
    sends = []
    for side, other in ((1, after), (0, before)):
        asks[1 - side].wait_recv()
        slot = 0 if side == 1 else some + stations
        for t in range(some):
            packed[side, t] = mine[jnp.clip(asked[side, t], 0, stations - 1)]
            copy = pltpu.make_async_remote_copy(
                src_ref=packed.at[side, t], dst_ref=near.at[slot + t],
                send_sem=halo_send.at[side, t], recv_sem=halo_recv.at[side, t],
                device_id={"pairs": other}, device_id_type=MESH,
            )
            copy.start()
            sends.append(copy)
    for copy in asks:
        copy.wait_send()

    coef[...] = jnp.zeros_like(coef)
    extra = held_rows.shape[0] - count
    held_rows[count:, :] = jnp.concatenate(
        [start_ref[...], jnp.zeros((extra - RANK, lags), F32)], 0
    ).astype(BF16)
    for p in range(pairs):
        local = lax.rem(rows_ref[1, p], stations)
        relative = lax.div(keys[p], stations)
        low, high = place[0][0], some + stations + place[1][0]
        for j in range(1, stations):
            low = jnp.where(local == j, place[0][j], low)
            high = jnp.where(local == j, some + stations + place[1][j], high)
        at_b = jnp.where(relative == 0, low, jnp.where(relative == 1, some + local, high))
        places[0, p] = some + lax.rem(rows_ref[0, p], stations)
        places[1, p] = jnp.clip(at_b, 0, 2 * stations - 1)
    turn = lax.rem(lax.broadcasted_iota(jnp.int32, (block, freq), 1), 4)
    swap_lanes = lax.rem(turn, 2) == 0
    sign_re = jnp.where((turn == 0) | (turn == 3), 1.0, -1.0)[:1].astype(BF16)
    sign_im = jnp.where(turn >= 2, 1.0, -1.0)[:1].astype(BF16)
    for copy in sends:
        copy.wait()

    def pair_body(p, carry):
        a = near[places[0, p]].astype(F32)
        b = near[places[1, p]].astype(F32)
        re = a[0] * b[0] + a[1] * b[1]
        im = a[1] * b[0] - a[0] * b[1]
        re, im = re.astype(BF16), im.astype(BF16)
        low = pl.ds(pl.multiple_of(p * block, block), block)
        high = pl.ds(pl.multiple_of(count + p * block, block), block)
        cross[high, :freq] = re
        cross[high, freq:] = im
        cross[low, :freq] = jnp.where(swap_lanes, im, re) * sign_re
        cross[low, freq:] = jnp.where(swap_lanes, re, im) * sign_im
        return carry

    lax.fori_loop(0, pairs, pair_body, 0, unroll=3)
    for copy in fills:
        copy.wait()
    tile = 256

    def lag_body(n, carry):
        y = jnp.dot(
            cross[...],
            table[:, pl.ds(pl.multiple_of(n * tile, tile), tile)],
            preferred_element_type=F32,
        ).astype(BF16)
        held_rows[:count, pl.ds(pl.multiple_of(n * tile, tile), tile)] = y[:count]
        held_rows[:count, pl.ds(pl.multiple_of(half + n * tile, tile), tile)] = y[count:]
        return carry

    lax.fori_loop(0, half // tile, lag_body, 0)
    gram = nt(held_rows[...], held_rows[...])
    lane = lax.broadcasted_iota(jnp.int32, (1, 128), 1)
    group = lax.div(lax.broadcasted_iota(jnp.int32, (1, 256), 1), 8)
    row_batch = lax.div(lax.broadcasted_iota(jnp.int32, (count, 1), 0), 8)
    batch = lax.broadcasted_iota(jnp.int32, (batches, 1), 0)
    mixed = lane >= segments
    near_lanes = lane < segments
    both = lane < segments + RANK
    shift = (128 - (count - 128) + segments) % 128

    def twelve(folded, tail):
        moved = pltpu.roll(tail, shift, 1)
        return jnp.where(near_lanes, folded, jnp.where(both, moved, 0.0))

    square[...] = twelve(fold8(gram[:count], group, row_batch), gram[:count, 128:])
    rows12 = [square[pl.ds(g, batches, stride=segments), :] for g in range(segments)]
    for r in range(RANK):
        line = jnp.broadcast_to(gram[count + r : count + r + 1], (batches, 256))
        rows12.append(twelve(fold8(line, group, batch), line[:, 128:]))

    def product(vectors):
        out = []
        for vector in vectors:
            total = vector[:, 0:1] * rows12[0]
            for j in range(1, segments + RANK):
                total = total + vector[:, j : j + 1] * rows12[j]
            out.append(total)
        return out

    weight = float(lags)
    held = [jnp.where(lane == segments + r, 1.0, 0.0) for r in range(RANK)]
    seen = [rows12[segments + r] for r in range(RANK)]
    for _ in range(TURNS):
        stepped = [weight * held[r] + jnp.where(near_lanes, seen[r], 0.0) for r in range(RANK)]
        image = product(stepped)
        small = [
            [jnp.sum(image[i] * stepped[j], axis=1, keepdims=True) for j in range(i + 1)]
            for i in range(RANK)
        ]
        lower = cholesky(small)
        held = solve(lower, stepped)
        seen = solve(lower, image)
    onto = [jnp.where(near_lanes, seen[r], 0.0) for r in range(RANK)]
    final = [weight * held[r] + onto[r] for r in range(RANK)]
    window = None
    for r in range(RANK):
        term = jnp.sum(onto[r], axis=1, keepdims=True) * held[r]
        window = term if window is None else window + term
    window = window * (1.0 / math.sqrt(segments))

    def spread(x):
        tail = pltpu.roll(jnp.where(mixed, x, 0.0), 128 - shift, 1)
        base = jnp.where(near_lanes, x, 0.0)
        for step in (8, 16, 32, 64):
            base = base + pltpu.roll(base, step, 1)
        left = jnp.where(group[:, :128] == batch, base, 0.0)
        right = jnp.where(group[:, 128:] == batch, base, 0.0) + tail
        return jnp.concatenate([left, right], 1)

    shown = spread(window)
    coef[:batches] = shown
    hours = lax.axis_size("hours")
    units = [spread(x) for x in final] + [shown * (1.0 / math.sqrt(windows * hours))]
    each = pairs // 2
    for r, unit in enumerate(units):
        for side in range(2):
            wide[side] = unit[:, side * 128 : (side + 1) * 128]
            total = wide.at[side][pl.ds(0, pairs, stride=windows), :]
            for w in range(1, windows):
                total = total + wide.at[side][pl.ds(w, pairs, stride=windows), :]
            for c in range(2):
                start = batches + c * slots + r * each
                columns = slice(side * 128, (side + 1) * 128)
                coef[start : start + each, columns] = total[c * each : (c + 1) * each]

    coefs = jnp.concatenate(split(coef[...]), 0)
    size = coef.shape[0]
    width = lags // chips
    chunk = across * width
    rows_order = sorted(range(other_side), key=lambda d: -min(d, other_side - d))
    columns_order = sorted(range(across), key=lambda d: -min(d, across - d))
    sends = []
    for i, dx in enumerate(rows_order):
        goal_row = lax.rem(row + dx, other_side)
        columns = pl.ds(pl.multiple_of(goal_row * chunk, chunk), chunk)
        out = jnp.dot(coefs, held_rows[:, columns], preferred_element_type=F32)
        out = out[:size] + out[size:]
        ws_ref[:, columns] = out[:batches]
        for c in range(2):
            block_rows = out[batches + c * slots : batches + (c + 1) * slots].astype(BF16)
            for y in range(across):
                part[i, c, y] = block_rows[:, y * width : (y + 1) * width]
        for dy in columns_order:
            for flip in range(2):
                if (dx, dy, flip) == (0, 0, 0):
                    continue
                index = places_from.index((dx, dy, flip))
                copy = pltpu.make_async_remote_copy(
                    src_ref=part.at[
                        i, core if flip == 0 else 1 - core, lax.rem(column + dy, across)
                    ],
                    dst_ref=incoming.at[index],
                    send_sem=out_send.at[index], recv_sem=in_recv.at[index],
                    device_id=device((dx, dy, flip)), device_id_type=MESH,
                )
                copy.start()
                sends.append((index, copy))
    merged = part[other_side - 1, core, column].astype(F32)
    for index, copy in sends:
        copy.wait()
        merged = merged + incoming[index].astype(F32)
    summed_rows[...] = merged

    swap = pltpu.make_async_remote_copy(
        src_ref=summed_rows, dst_ref=theirs, send_sem=send_sem.at[0], recv_sem=recv_sem.at[0],
        device_id=twin, device_id_type=MESH,
    )
    swap.start()
    vectors = [summed_rows[r * each : (r + 1) * each] for r in range(RANK)]
    order = [(i, j) for i in range(RANK) for j in range(i + 1)]
    line = lax.broadcasted_iota(jnp.int32, (each, 128), 1)
    pair_of = lax.broadcasted_iota(jnp.int32, (each, 128), 0)
    marks = [line == 8 * index + pair_of for index in range(len(order))]
    tile = jnp.zeros((each, 128), F32)
    for mark, (i, j) in zip(marks, order):
        tile = jnp.where(mark, jnp.sum(vectors[i] * vectors[j], axis=1, keepdims=True), tile)
    own_gram[...] = jnp.sum(tile, axis=0, keepdims=True)
    tells = []
    for index, place in enumerate(places_from):
        copy = pltpu.make_async_remote_copy(
            src_ref=own_gram, dst_ref=grams.at[index],
            send_sem=gram_send.at[index], recv_sem=gram_recv.at[index],
            device_id=device(place), device_id_type=MESH,
        )
        copy.start()
        tells.append(copy)
    swap.wait()
    for copy in reversed(tells):
        copy.wait()
    gram_sums = [own_gram[...], None]
    for index, (_, _, flip) in enumerate(places_from):
        value = grams[index]
        gram_sums[flip] = value if gram_sums[flip] is None else gram_sums[flip] + value
    own_half = width // 2

    def halved(x):
        return jnp.where(core == 0, x[:, :own_half], x[:, own_half:])

    for flip, source in enumerate((summed_rows, theirs)):
        target = core if flip == 0 else 1 - core
        small = [[None] * RANK for _ in range(RANK)]
        for mark, (i, j) in zip(marks, order):
            small[i][j] = jnp.sum(
                jnp.where(mark, gram_sums[flip], 0.0), axis=1, keepdims=True
            )
        pieces = [halved(source[r * each : (r + 1) * each]) for r in range(RANK)]
        for r, value in enumerate(solve(cholesky(small), pieces)):
            out_ref[target, r * each : (r + 1) * each] = value * math.sqrt(lags)
        out_ref[target, RANK * each :] = halved(source[RANK * each :])


def finish_kernel(pairs, windows, windows_ref, merged_ref, ws_ref, stack_ref, basis_ref):
    each = pairs // 2
    for p in range(pairs):
        ws_ref[p] = windows_ref[windows * p : windows * (p + 1)]
    rows = merged_ref[...]
    stack_ref[...] = jnp.concatenate(
        [rows[c, RANK * each : (RANK + 1) * each] for c in range(2)], 0
    )
    for p in range(pairs):
        c, q = divmod(p, each)
        for r in range(RANK):
            basis_ref[p, r : r + 1] = rows[c, r * each + q : r * each + q + 1]


def on_device(table, spectra, masks, pair_rows, start_basis):
    stations, windows, segments, _, freq = spectra.shape
    lags = start_basis.shape[1]
    half = lags // 2
    pairs = pair_rows.shape[0]
    block = windows * segments
    count = pairs * block
    batches = pairs * windows
    each = pairs // 2
    slots = 32
    chips = lax.axis_size("hours") // 2
    width = lags // chips
    rows_of_chips = torus_offsets(chips)[1]
    raw = spectra.reshape(stations, block, 2, freq)
    vmem = pl.BlockSpec(memory_space=pltpu.VMEM)
    windows_out, merged = pl.pallas_call(
        functools.partial(station_kernel, stations, segments, windows, pairs, freq, half),
        out_shape=(
            pltpu.VMEM((batches, lags), F32),
            pltpu.VMEM((2, slots, width // 2), F32),
        ),
        in_specs=[
            pl.BlockSpec(memory_space=pltpu.HBM),
        ]
        * 5,
        out_specs=(vmem, vmem),
        scratch_shapes=[
            pltpu.SMEM((2, pairs), jnp.int32),
            pltpu.VMEM((stations, windows, segments), jnp.int32),
            pltpu.VMEM((RANK, lags), F32),
            pltpu.VMEM((stations, block, 2, freq), BF16),
            pltpu.VMEM((stations, 2, block, freq), BF16),
            pltpu.VMEM((2, stations // 2, 2, block, freq), BF16),
            pltpu.SMEM((2, stations // 2), jnp.int32),
            pltpu.SMEM((2, stations // 2), jnp.int32),
            pltpu.SMEM((2, pairs), jnp.int32),
            pltpu.VMEM((2 * stations, 2, block, freq), BF16),
            pltpu.VMEM((2 * count, 2 * freq), BF16),
            pltpu.VMEM((2 * freq, half), BF16),
            pltpu.VMEM((256, lags), BF16),
            pltpu.VMEM((count, 128), F32),
            pltpu.VMEM((2, batches, 128), F32),
            pltpu.VMEM((batches + 2 * slots, 256), F32),
            pltpu.VMEM((rows_of_chips, 2, chips // rows_of_chips, slots, width), BF16),
            pltpu.VMEM((2 * chips - 1, slots, width), BF16),
            pltpu.VMEM((slots, width), F32),
            pltpu.VMEM((slots, width), F32),
            pltpu.VMEM((1, 128), F32),
            pltpu.VMEM((2 * chips - 1, 1, 128), F32),
            pltpu.SemaphoreType.DMA((2,)),
            pltpu.SemaphoreType.DMA((2,)),
            pltpu.SemaphoreType.DMA((2, stations // 2)),
            pltpu.SemaphoreType.DMA((2, stations // 2)),
            pltpu.SemaphoreType.DMA((1,)),
            pltpu.SemaphoreType.DMA((1,)),
            pltpu.SemaphoreType.DMA((5,)),
            pltpu.SemaphoreType.DMA((4,)),
            pltpu.SemaphoreType.DMA((2 * chips - 1,)),
            pltpu.SemaphoreType.DMA((2 * chips - 1,)),
            pltpu.SemaphoreType.DMA((2 * chips - 1,)),
            pltpu.SemaphoreType.DMA((2 * chips - 1,)),
        ],
        compiler_params=pltpu.CompilerParams(
            collective_id=0, has_side_effects=True, vmem_limit_bytes=60 << 20
        ),
        name="station_pairs",
    )(pair_rows.T, masks, raw, table, start_basis)
    return pl.pallas_call(
        functools.partial(finish_kernel, pairs, windows),
        out_shape=(
            jax.ShapeDtypeStruct((pairs, windows, lags), F32),
            jax.ShapeDtypeStruct((pairs, width // 2), F32),
            jax.ShapeDtypeStruct((pairs, RANK, width // 2), F32),
        ),
        in_specs=[vmem, vmem],
        out_specs=(vmem, vmem, vmem),
        compiler_params=pltpu.CompilerParams(vmem_limit_bytes=4 << 20),
        name="outputs",
    )(windows_out, merged)


def solution(mesh):
    in_specs = (
        P("pairs", "hours", None, None, None),
        P("pairs", "hours", None),
        P("pairs", None),
        P(),
    )
    out_specs = (P("pairs", "hours", None), P("pairs", "hours"), P("pairs", None, "hours"))

    def whole(spectra, masks, pair_rows, start_basis):
        table = jnp.asarray(half_table(spectra.shape[4], start_basis.shape[1] // 2))
        return jax.shard_map(
            on_device, mesh=mesh, in_specs=(P(), *in_specs), out_specs=out_specs, check_vma=False
        )(table, spectra, masks, pair_rows, start_basis)

    return whole
```

```python
import functools
import math

import jax
import jax.numpy as jnp
import numpy as np
from jax import lax
from jax.experimental import pallas as pl
from jax.experimental.pallas import tpu as pltpu
from jax.sharding import PartitionSpec as P

BAND = 64
TURNS = 2
RANK = 4
MESH = pl.DeviceIdType.MESH
F32 = jnp.float32
BF16 = jnp.bfloat16


def half_table(freq, half):
    bins = np.arange(1, freq + 1, dtype=np.int64)[:, None]
    shifts = np.arange(half, dtype=np.int64)[None, :]
    phase = np.mod(bins * shifts, 4 * half).astype(np.float64) * (math.pi / (2 * half))
    scale = freq ** (-0.5)
    table = np.concatenate([np.cos(phase) * scale, -np.sin(phase) * scale], 0)
    return table.astype(np.float32).astype(jnp.bfloat16)


def whiten(x, mask, ones):
    rows, freq = x.shape[1:]
    square = x[0] * x[0] + x[1] * x[1]
    tiles = freq // 128
    stacked = jnp.concatenate([square[:, t * 128 : (t + 1) * 128] for t in range(tiles)], 0)
    hi, lo = split(stacked)
    power = jnp.dot(hi, ones, preferred_element_type=F32) + jnp.dot(
        lo, ones, preferred_element_type=F32
    )
    scale = lax.rsqrt(power * (0.5 / BAND) + 1e-06)
    scale = jnp.concatenate([scale[t * rows : (t + 1) * rows] for t in range(tiles)], 1) * mask
    return (x[0] * scale).astype(BF16), (x[1] * scale).astype(BF16)


def nt(a, b):
    return lax.dot_general(a, b, (((1,), (1,)), ((), ())), preferred_element_type=F32)


def split(x):
    hi = x.astype(BF16)
    return hi, (x - hi.astype(F32)).astype(BF16)


def cholesky(gram):
    lower = [[None] * RANK for _ in range(RANK)]
    for row in range(RANK):
        for col in range(row + 1):
            total = gram[row][col]
            for inner in range(col):
                total = total - lower[row][inner] * lower[col][inner]
            lower[row][col] = 1.0 / jnp.sqrt(total) if row == col else total * lower[col][col]
    return lower


def solve(lower, vectors):
    result = []
    for row in range(RANK):
        current = vectors[row]
        for inner in range(row):
            current = current - lower[row][inner] * result[inner]
        result.append(current * lower[row][row])
    return result


def fold8(x, batch_of_lane, batch):
    kept = jnp.where(batch_of_lane == batch, x, 0.0)
    total = kept[:, :128] + kept[:, 128:]
    for shift in (64, 32, 16, 8):
        total = total + pltpu.roll(total, shift, 1)
    return total


def torus_offsets(chips):
    side = math.isqrt(chips)
    side = side if side * side == chips else 1
    other = chips // side
    offsets = [(dx, dy) for dx in range(other) for dy in range(side) if dx or dy]
    return side, other, sorted(
        offsets, key=lambda o: -(min(o[0], other - o[0]) + min(o[1], side - o[1]))
    )


def station_kernel(
    stations, segments, windows, pairs, freq, half,
    rows_hbm, masks_hbm, raw_ref, table_ref, start_hbm,
    ws_ref, out_ref,
    rows_ref, masks_ref, start_ref, raw, mine, packed, wants, asked, places, near,
    cross, table, held_rows, square, wide, coef,
    part, incoming, summed_rows, theirs, own_gram, grams,
    list_send, list_recv, halo_send, halo_recv, send_sem, recv_sem, own_sem, fill_sem,
    out_send, in_recv, gram_send, gram_recv,
):
    me, ring = lax.axis_index("pairs"), lax.axis_size("pairs")
    after, before = lax.rem(me + 1, ring), lax.rem(me + ring - 1, ring)
    block = windows * segments
    count = pairs * block
    batches = pairs * windows
    lags = 2 * half
    slots = coef.shape[0] // 2 - batches // 2
    some = stations // 2
    own = pltpu.make_async_copy(raw_ref, raw, own_sem.at[0])
    cuts = 4
    band = 2 * freq // cuts
    fills = [
        pltpu.make_async_copy(
            table_ref.at[pl.ds(i * band, band)], table.at[pl.ds(i * band, band)], fill_sem.at[i]
        )
        for i in range(cuts)
    ]
    gathers = [
        pltpu.make_async_copy(source, target, own_sem.at[2 + index])
        for index, (source, target) in enumerate(
            ((rows_hbm, rows_ref), (masks_hbm, masks_ref), (start_hbm, start_ref))
        )
    ]
    for copy in gathers:
        copy.start()
    own.start()
    for copy in fills:
        copy.start()

    hour = lax.axis_index("hours")
    chips = lax.axis_size("hours") // 2
    core, chip = lax.rem(hour, 2), lax.div(hour, 2)
    twin = {"hours": hour + 1 - 2 * core}
    across, other_side, offsets = torus_offsets(chips)
    row, column = lax.div(chip, across), lax.rem(chip, across)
    places_from = [(dx, dy, flip) for dx, dy in offsets + [(0, 0)] for flip in range(2)][:-2]
    places_from.append((0, 0, 1))

    def device(place):
        dx, dy, flip = place
        goal = across * lax.rem(row + dx, other_side) + lax.rem(column + dy, across)
        return {"hours": 2 * goal + (core if flip == 0 else 1 - core)}

    barrier = pltpu.get_barrier_semaphore()
    partners = [{"pairs": before}, {"pairs": after}]
    partners += [device(place) for place in places_from]
    for other in partners:
        pl.semaphore_signal(barrier, inc=1, device_id=other, device_id_type=MESH)

    gathers[0].wait()
    keys = []
    for p in range(pairs):
        second = rows_ref[1, p]
        relative = lax.rem(lax.div(second, stations) - me + 1 + ring, ring)
        keys.append(relative * stations + lax.rem(second, stations))
    place = []
    for side in range(2):
        taken, slots_of = 0, []
        picks = [0] * some
        for j in range(stations):
            found = keys[0] == 2 * side * stations + j
            for key in keys[1:]:
                found = found | (key == 2 * side * stations + j)
            used = found.astype(jnp.int32)
            slots_of.append(taken)
            for t in range(some):
                picks[t] = picks[t] + jnp.where(found & (taken == t), j, 0)
            taken = taken + used
        place.append(slots_of)
        for t in range(some):
            wants[side, t] = picks[t]
    pl.semaphore_wait(barrier, len(partners))
    asks = []
    for side, other in ((0, before), (1, after)):
        copy = pltpu.make_async_remote_copy(
            src_ref=wants.at[side], dst_ref=asked.at[1 - side],
            send_sem=list_send.at[side], recv_sem=list_recv.at[1 - side],
            device_id={"pairs": other}, device_id_type=MESH,
        )
        copy.start()
        asks.append(copy)

    own.wait()
    for copy in gathers[1:]:
        copy.wait()
    ones = jnp.where(
        lax.div(lax.broadcasted_iota(jnp.int32, (128, 128), 0), BAND)
        == lax.div(lax.broadcasted_iota(jnp.int32, (128, 128), 1), BAND),
        1.0, 0.0,
    ).astype(BF16)
    diagonal = lax.rem(
        lax.broadcasted_iota(jnp.int32, (block, segments), 0), segments
    ) == lax.broadcasted_iota(jnp.int32, (block, segments), 1)

    def station_body(s, carry):
        flags = masks_ref[s].astype(F32)
        lines = jnp.concatenate(
            [jnp.broadcast_to(flags[w : w + 1], (segments, segments)) for w in range(windows)], 0
        )
        mask = jnp.sum(jnp.where(diagonal, lines, 0.0), axis=1, keepdims=True)
        x = jnp.swapaxes(raw[s].astype(F32), 0, 1)
        re, im = whiten(x, mask, ones)
        mine[s, 0], mine[s, 1] = re, im
        near[some + s, 0], near[some + s, 1] = re, im
        return carry

    lax.fori_loop(0, stations, station_body, 0, unroll=2)
    sends = []
    for side, other in ((1, after), (0, before)):
        asks[1 - side].wait_recv()
        slot = 0 if side == 1 else some + stations
        for t in range(some):
            packed[side, t] = mine[jnp.clip(asked[side, t], 0, stations - 1)]
            copy = pltpu.make_async_remote_copy(
                src_ref=packed.at[side, t], dst_ref=near.at[slot + t],
                send_sem=halo_send.at[side, t], recv_sem=halo_recv.at[side, t],
                device_id={"pairs": other}, device_id_type=MESH,
            )
            copy.start()
            sends.append(copy)
    for copy in asks:
        copy.wait_send()

    coef[...] = jnp.zeros_like(coef)
    extra = held_rows.shape[0] - count
    held_rows[count:, :] = jnp.concatenate(
        [start_ref[...], jnp.zeros((extra - RANK, lags), F32)], 0
    ).astype(BF16)
    for p in range(pairs):
        local = lax.rem(rows_ref[1, p], stations)
        relative = lax.div(keys[p], stations)
        low, high = place[0][0], some + stations + place[1][0]
        for j in range(1, stations):
            low = jnp.where(local == j, place[0][j], low)
            high = jnp.where(local == j, some + stations + place[1][j], high)
        at_b = jnp.where(relative == 0, low, jnp.where(relative == 1, some + local, high))
        places[0, p] = some + lax.rem(rows_ref[0, p], stations)
        places[1, p] = jnp.clip(at_b, 0, 2 * stations - 1)
    turn = lax.rem(lax.broadcasted_iota(jnp.int32, (block, freq), 1), 4)
    swap_lanes = lax.rem(turn, 2) == 0
    sign_re = jnp.where((turn == 0) | (turn == 3), 1.0, -1.0)[:1].astype(BF16)
    sign_im = jnp.where(turn >= 2, 1.0, -1.0)[:1].astype(BF16)
    for copy in sends:
        copy.wait()

    def pair_body(p, carry):
        a = near[places[0, p]].astype(F32)
        b = near[places[1, p]].astype(F32)
        re = a[0] * b[0] + a[1] * b[1]
        im = a[1] * b[0] - a[0] * b[1]
        re, im = re.astype(BF16), im.astype(BF16)
        low = pl.ds(pl.multiple_of(p * block, block), block)
        high = pl.ds(pl.multiple_of(count + p * block, block), block)
        cross[high, :freq] = re
        cross[high, freq:] = im
        cross[low, :freq] = jnp.where(swap_lanes, im, re) * sign_re
        cross[low, freq:] = jnp.where(swap_lanes, re, im) * sign_im
        return carry

    lax.fori_loop(0, pairs, pair_body, 0, unroll=3)
    for copy in fills:
        copy.wait()
    tile = 256

    def lag_body(n, carry):
        y = jnp.dot(
            cross[...],
            table[:, pl.ds(pl.multiple_of(n * tile, tile), tile)],
            preferred_element_type=F32,
        ).astype(BF16)
        held_rows[:count, pl.ds(pl.multiple_of(n * tile, tile), tile)] = y[:count]
        held_rows[:count, pl.ds(pl.multiple_of(half + n * tile, tile), tile)] = y[count:]
        return carry

    lax.fori_loop(0, half // tile, lag_body, 0)
    gram = nt(held_rows[: count + 16], held_rows[...])
    lane = lax.broadcasted_iota(jnp.int32, (1, 128), 1)
    group = lax.div(lax.broadcasted_iota(jnp.int32, (1, 256), 1), 8)
    row_batch = lax.div(lax.broadcasted_iota(jnp.int32, (count, 1), 0), 8)
    batch = lax.broadcasted_iota(jnp.int32, (batches, 1), 0)
    mixed = lane >= segments
    near_lanes = lane < segments
    both = lane < segments + RANK
    shift = (128 - (count - 128) + segments) % 128

    def twelve(folded, tail):
        moved = pltpu.roll(tail, shift, 1)
        return jnp.where(near_lanes, folded, jnp.where(both, moved, 0.0))

    square[...] = twelve(fold8(gram[:count], group, row_batch), gram[:count, 128:])
    rows12 = [square[pl.ds(g, batches, stride=segments), :] for g in range(segments)]
    for r in range(RANK):
        line = jnp.broadcast_to(gram[count + r : count + r + 1], (batches, 256))
        rows12.append(twelve(fold8(line, group, batch), line[:, 128:]))

    def product(vectors):
        out = []
        for vector in vectors:
            total = vector[:, 0:1] * rows12[0]
            for j in range(1, segments + RANK):
                total = total + vector[:, j : j + 1] * rows12[j]
            out.append(total)
        return out

    weight = float(lags)
    held = [jnp.where(lane == segments + r, 1.0, 0.0) for r in range(RANK)]
    seen = [rows12[segments + r] for r in range(RANK)]
    for _ in range(TURNS):
        stepped = [weight * held[r] + jnp.where(near_lanes, seen[r], 0.0) for r in range(RANK)]
        image = product(stepped)
        small = [
            [jnp.sum(image[i] * stepped[j], axis=1, keepdims=True) for j in range(i + 1)]
            for i in range(RANK)
        ]
        lower = cholesky(small)
        held = solve(lower, stepped)
        seen = solve(lower, image)
    onto = [jnp.where(near_lanes, seen[r], 0.0) for r in range(RANK)]
    final = [weight * held[r] + onto[r] for r in range(RANK)]
    window = None
    for r in range(RANK):
        term = jnp.sum(onto[r], axis=1, keepdims=True) * held[r]
        window = term if window is None else window + term
    window = window * (1.0 / math.sqrt(segments))

    def spread(x):
        tail = pltpu.roll(jnp.where(mixed, x, 0.0), 128 - shift, 1)
        base = jnp.where(near_lanes, x, 0.0)
        for step in (8, 16, 32, 64):
            base = base + pltpu.roll(base, step, 1)
        left = jnp.where(group[:, :128] == batch, base, 0.0)
        right = jnp.where(group[:, 128:] == batch, base, 0.0) + tail
        return jnp.concatenate([left, right], 1)

    shown = spread(window)
    coef[:batches] = shown
    hours = lax.axis_size("hours")
    units = [spread(x) for x in final] + [shown * (1.0 / math.sqrt(windows * hours))]
    each = pairs // 2
    for r, unit in enumerate(units):
        for side in range(2):
            wide[side] = unit[:, side * 128 : (side + 1) * 128]
            total = wide.at[side][pl.ds(0, pairs, stride=windows), :]
            for w in range(1, windows):
                total = total + wide.at[side][pl.ds(w, pairs, stride=windows), :]
            for c in range(2):
                start = batches + c * slots + r * each
                columns = slice(side * 128, (side + 1) * 128)
                coef[start : start + each, columns] = total[c * each : (c + 1) * each]

    coefs = jnp.concatenate(split(coef[...]), 0)
    size = coef.shape[0]
    width = lags // chips
    chunk = across * width
    rows_order = sorted(range(other_side), key=lambda d: -min(d, other_side - d))
    columns_order = sorted(range(across), key=lambda d: -min(d, across - d))
    sends = []
    for i, dx in enumerate(rows_order):
        goal_row = lax.rem(row + dx, other_side)
        columns = pl.ds(pl.multiple_of(goal_row * chunk, chunk), chunk)
        out = jnp.dot(coefs, held_rows[:, columns], preferred_element_type=F32)
        out = out[:size] + out[size:]
        for c in range(2):
            block_rows = out[batches + c * slots : batches + (c + 1) * slots].astype(BF16)
            for y in range(across):
                part[i, c, y] = block_rows[:, y * width : (y + 1) * width]
        for dy in columns_order:
            for flip in range(2):
                if (dx, dy, flip) == (0, 0, 0):
                    continue
                index = places_from.index((dx, dy, flip))
                copy = pltpu.make_async_remote_copy(
                    src_ref=part.at[
                        i, core if flip == 0 else 1 - core, lax.rem(column + dy, across)
                    ],
                    dst_ref=incoming.at[index],
                    send_sem=out_send.at[index], recv_sem=in_recv.at[index],
                    device_id=device((dx, dy, flip)), device_id_type=MESH,
                )
                copy.start()
                sends.append((index, copy))
        ws_ref[:, columns] = out[:batches]
    merged = part[other_side - 1, core, column].astype(F32)
    for index, copy in reversed(sends):
        copy.wait_recv()
        merged = merged + incoming[index].astype(F32)
    summed_rows[...] = merged

    swap = pltpu.make_async_remote_copy(
        src_ref=summed_rows, dst_ref=theirs, send_sem=send_sem.at[0], recv_sem=recv_sem.at[0],
        device_id=twin, device_id_type=MESH,
    )
    swap.start()
    vectors = [summed_rows[r * each : (r + 1) * each] for r in range(RANK)]
    order = [(i, j) for i in range(RANK) for j in range(i + 1)]
    line = lax.broadcasted_iota(jnp.int32, (each, 128), 1)
    pair_of = lax.broadcasted_iota(jnp.int32, (each, 128), 0)
    marks = [line == 8 * index + pair_of for index in range(len(order))]
    tile = jnp.zeros((each, 128), F32)
    for mark, (i, j) in zip(marks, order):
        tile = jnp.where(mark, jnp.sum(vectors[i] * vectors[j], axis=1, keepdims=True), tile)
    own_gram[...] = jnp.sum(tile, axis=0, keepdims=True)
    tells = []
    for index, place in enumerate(places_from):
        copy = pltpu.make_async_remote_copy(
            src_ref=own_gram, dst_ref=grams.at[index],
            send_sem=gram_send.at[index], recv_sem=gram_recv.at[index],
            device_id=device(place), device_id_type=MESH,
        )
        copy.start()
        tells.append(copy)
    swap.wait()
    for _, copy in sends:
        copy.wait_send()
    gram_sums = [own_gram[...], None]
    for index in reversed(range(len(tells))):
        tells[index].wait_recv()
        flip = places_from[index][2]
        value = grams[index]
        gram_sums[flip] = value if gram_sums[flip] is None else gram_sums[flip] + value
    own_half = width // 2

    def halved(x):
        return jnp.where(core == 0, x[:, :own_half], x[:, own_half:])

    for flip, source in enumerate((summed_rows, theirs)):
        target = core if flip == 0 else 1 - core
        small = [[None] * RANK for _ in range(RANK)]
        for mark, (i, j) in zip(marks, order):
            small[i][j] = jnp.sum(
                jnp.where(mark, gram_sums[flip], 0.0), axis=1, keepdims=True
            )
        pieces = [halved(source[r * each : (r + 1) * each]) for r in range(RANK)]
        for r, value in enumerate(solve(cholesky(small), pieces)):
            out_ref[target, r * each : (r + 1) * each] = value * math.sqrt(lags)
        out_ref[target, RANK * each :] = halved(source[RANK * each :])
    for copy in tells:
        copy.wait_send()


def finish_kernel(pairs, windows, windows_ref, merged_ref, ws_ref, stack_ref, basis_ref):
    each = pairs // 2
    for p in range(pairs):
        ws_ref[p] = windows_ref[windows * p : windows * (p + 1)]
    rows = merged_ref[...]
    stack_ref[...] = jnp.concatenate(
        [rows[c, RANK * each : (RANK + 1) * each] for c in range(2)], 0
    )
    for p in range(pairs):
        c, q = divmod(p, each)
        for r in range(RANK):
            basis_ref[p, r : r + 1] = rows[c, r * each + q : r * each + q + 1]


def on_device(table, spectra, masks, pair_rows, start_basis):
    stations, windows, segments, _, freq = spectra.shape
    lags = start_basis.shape[1]
    half = lags // 2
    pairs = pair_rows.shape[0]
    block = windows * segments
    count = pairs * block
    batches = pairs * windows
    each = pairs // 2
    slots = 32
    chips = lax.axis_size("hours") // 2
    width = lags // chips
    rows_of_chips = torus_offsets(chips)[1]
    raw = spectra.reshape(stations, block, 2, freq)
    vmem = pl.BlockSpec(memory_space=pltpu.VMEM)
    windows_out, merged = pl.pallas_call(
        functools.partial(station_kernel, stations, segments, windows, pairs, freq, half),
        out_shape=(
            pltpu.VMEM((batches, lags), F32),
            pltpu.VMEM((2, slots, width // 2), F32),
        ),
        in_specs=[
            pl.BlockSpec(memory_space=pltpu.HBM),
        ]
        * 5,
        out_specs=(vmem, vmem),
        scratch_shapes=[
            pltpu.SMEM((2, pairs), jnp.int32),
            pltpu.VMEM((stations, windows, segments), jnp.int32),
            pltpu.VMEM((RANK, lags), F32),
            pltpu.VMEM((stations, block, 2, freq), BF16),
            pltpu.VMEM((stations, 2, block, freq), BF16),
            pltpu.VMEM((2, stations // 2, 2, block, freq), BF16),
            pltpu.SMEM((2, stations // 2), jnp.int32),
            pltpu.SMEM((2, stations // 2), jnp.int32),
            pltpu.SMEM((2, pairs), jnp.int32),
            pltpu.VMEM((2 * stations, 2, block, freq), BF16),
            pltpu.VMEM((2 * count, 2 * freq), BF16),
            pltpu.VMEM((2 * freq, half), BF16),
            pltpu.VMEM((256, lags), BF16),
            pltpu.VMEM((count, 128), F32),
            pltpu.VMEM((2, batches, 128), F32),
            pltpu.VMEM((batches + 2 * slots, 256), F32),
            pltpu.VMEM((rows_of_chips, 2, chips // rows_of_chips, slots, width), BF16),
            pltpu.VMEM((2 * chips - 1, slots, width), BF16),
            pltpu.VMEM((slots, width), F32),
            pltpu.VMEM((slots, width), F32),
            pltpu.VMEM((1, 128), F32),
            pltpu.VMEM((2 * chips - 1, 1, 128), F32),
            pltpu.SemaphoreType.DMA((2,)),
            pltpu.SemaphoreType.DMA((2,)),
            pltpu.SemaphoreType.DMA((2, stations // 2)),
            pltpu.SemaphoreType.DMA((2, stations // 2)),
            pltpu.SemaphoreType.DMA((1,)),
            pltpu.SemaphoreType.DMA((1,)),
            pltpu.SemaphoreType.DMA((5,)),
            pltpu.SemaphoreType.DMA((4,)),
            pltpu.SemaphoreType.DMA((2 * chips - 1,)),
            pltpu.SemaphoreType.DMA((2 * chips - 1,)),
            pltpu.SemaphoreType.DMA((2 * chips - 1,)),
            pltpu.SemaphoreType.DMA((2 * chips - 1,)),
        ],
        compiler_params=pltpu.CompilerParams(
            collective_id=0, has_side_effects=True, vmem_limit_bytes=60 << 20
        ),
        name="station_pairs",
    )(pair_rows.T, masks, raw, table, start_basis)
    return pl.pallas_call(
        functools.partial(finish_kernel, pairs, windows),
        out_shape=(
            jax.ShapeDtypeStruct((pairs, windows, lags), F32),
            jax.ShapeDtypeStruct((pairs, width // 2), F32),
            jax.ShapeDtypeStruct((pairs, RANK, width // 2), F32),
        ),
        in_specs=[vmem, vmem],
        out_specs=(vmem, vmem, vmem),
        compiler_params=pltpu.CompilerParams(vmem_limit_bytes=4 << 20),
        name="outputs",
    )(windows_out, merged)


def solution(mesh):
    in_specs = (
        P("pairs", "hours", None, None, None),
        P("pairs", "hours", None),
        P("pairs", None),
        P(),
    )
    out_specs = (P("pairs", "hours", None), P("pairs", "hours"), P("pairs", None, "hours"))

    def whole(spectra, masks, pair_rows, start_basis):
        table = jnp.asarray(half_table(spectra.shape[4], start_basis.shape[1] // 2))
        return jax.shard_map(
            on_device, mesh=mesh, in_specs=(P(), *in_specs), out_specs=out_specs, check_vma=False
        )(table, spectra, masks, pair_rows, start_basis)

    return whole
```

```python
import functools
import math

import jax
import jax.numpy as jnp
import numpy as np
from jax import lax
from jax.experimental import pallas as pl
from jax.experimental.pallas import tpu as pltpu
from jax.sharding import PartitionSpec as P

BAND = 64
TURNS = 2
RANK = 4
MESH = pl.DeviceIdType.MESH
F32 = jnp.float32
BF16 = jnp.bfloat16


def half_table(freq, half):
    bins = np.arange(1, freq + 1, dtype=np.int64)[:, None]
    shifts = np.arange(half, dtype=np.int64)[None, :]
    phase = np.mod(bins * shifts, 4 * half).astype(np.float64) * (math.pi / (2 * half))
    scale = freq ** (-0.5)
    table = np.concatenate([np.cos(phase) * scale, -np.sin(phase) * scale], 0)
    return table.astype(np.float32).astype(jnp.bfloat16)


def whiten(x, mask, ones):
    rows, freq = x.shape[1:]
    square = x[0] * x[0] + x[1] * x[1]
    tiles = freq // 128
    stacked = jnp.concatenate([square[:, t * 128 : (t + 1) * 128] for t in range(tiles)], 0)
    hi, lo = split(stacked)
    power = jnp.dot(hi, ones, preferred_element_type=F32) + jnp.dot(
        lo, ones, preferred_element_type=F32
    )
    scale = lax.rsqrt(power * (0.5 / BAND) + 1e-06)
    scale = jnp.concatenate([scale[t * rows : (t + 1) * rows] for t in range(tiles)], 1) * mask
    return (x[0] * scale).astype(BF16), (x[1] * scale).astype(BF16)


def nt(a, b):
    return lax.dot_general(a, b, (((1,), (1,)), ((), ())), preferred_element_type=F32)


def split(x):
    hi = x.astype(BF16)
    return hi, (x - hi.astype(F32)).astype(BF16)


def cholesky(gram):
    lower = [[None] * RANK for _ in range(RANK)]
    for row in range(RANK):
        for col in range(row + 1):
            total = gram[row][col]
            for inner in range(col):
                total = total - lower[row][inner] * lower[col][inner]
            lower[row][col] = 1.0 / jnp.sqrt(total) if row == col else total * lower[col][col]
    return lower


def solve(lower, vectors):
    result = []
    for row in range(RANK):
        current = vectors[row]
        for inner in range(row):
            current = current - lower[row][inner] * result[inner]
        result.append(current * lower[row][row])
    return result


def fold8(x, batch_of_lane, batch):
    kept = jnp.where(batch_of_lane == batch, x, 0.0)
    total = kept[:, :128] + kept[:, 128:]
    for shift in (64, 32, 16, 8):
        total = total + pltpu.roll(total, shift, 1)
    return total


def torus_offsets(chips):
    side = math.isqrt(chips)
    side = side if side * side == chips else 1
    other = chips // side
    offsets = [(dx, dy) for dx in range(other) for dy in range(side) if dx or dy]
    return side, other, sorted(
        offsets, key=lambda o: -(min(o[0], other - o[0]) + min(o[1], side - o[1]))
    )


def station_kernel(
    stations, segments, windows, pairs, freq, half,
    rows_hbm, masks_hbm, raw_ref, table_ref, start_hbm,
    ws_ref, out_ref,
    rows_ref, masks_ref, start_ref, raw, mine, packed, wants, asked, places, near,
    cross, table, held_rows, square, wide, coef,
    part, sib, outgoing, incoming, summed_rows, theirs, own_gram, grams,
    list_send, list_recv, halo_send, halo_recv, send_sem, recv_sem, own_sem, fill_sem,
    out_send, in_recv, gram_send, gram_recv,
):
    me, ring = lax.axis_index("pairs"), lax.axis_size("pairs")
    after, before = lax.rem(me + 1, ring), lax.rem(me + ring - 1, ring)
    block = windows * segments
    count = pairs * block
    batches = pairs * windows
    lags = 2 * half
    slots = coef.shape[0] // 2 - batches // 2
    some = stations // 2
    own = pltpu.make_async_copy(raw_ref, raw, own_sem.at[0])
    cuts = 4
    band = 2 * freq // cuts
    fills = [
        pltpu.make_async_copy(
            table_ref.at[pl.ds(i * band, band)], table.at[pl.ds(i * band, band)], fill_sem.at[i]
        )
        for i in range(cuts)
    ]
    gathers = [
        pltpu.make_async_copy(source, target, own_sem.at[2 + index])
        for index, (source, target) in enumerate(
            ((rows_hbm, rows_ref), (masks_hbm, masks_ref), (start_hbm, start_ref))
        )
    ]
    for copy in gathers:
        copy.start()
    own.start()
    for copy in fills:
        copy.start()

    hour = lax.axis_index("hours")
    chips = lax.axis_size("hours") // 2
    core, chip = lax.rem(hour, 2), lax.div(hour, 2)
    twin = {"hours": hour + 1 - 2 * core}
    across, other_side, offsets = torus_offsets(chips)
    row, column = lax.div(chip, across), lax.rem(chip, across)
    places_from = [(dx, dy, flip) for dx, dy in offsets + [(0, 0)] for flip in range(2)][:-2]
    places_from.append((0, 0, 1))

    def device(place):
        dx, dy, flip = place
        goal = across * lax.rem(row + dx, other_side) + lax.rem(column + dy, across)
        return {"hours": 2 * goal + (core if flip == 0 else 1 - core)}

    barrier = pltpu.get_barrier_semaphore()
    partners = [{"pairs": before}, {"pairs": after}]
    partners += [device(place) for place in places_from]
    for other in partners:
        pl.semaphore_signal(barrier, inc=1, device_id=other, device_id_type=MESH)

    gathers[0].wait()
    keys = []
    for p in range(pairs):
        second = rows_ref[1, p]
        relative = lax.rem(lax.div(second, stations) - me + 1 + ring, ring)
        keys.append(relative * stations + lax.rem(second, stations))
    place = []
    for side in range(2):
        taken, slots_of = 0, []
        picks = [0] * some
        for j in range(stations):
            found = keys[0] == 2 * side * stations + j
            for key in keys[1:]:
                found = found | (key == 2 * side * stations + j)
            used = found.astype(jnp.int32)
            slots_of.append(taken)
            for t in range(some):
                picks[t] = picks[t] + jnp.where(found & (taken == t), j, 0)
            taken = taken + used
        place.append(slots_of)
        for t in range(some):
            wants[side, t] = picks[t]
    pl.semaphore_wait(barrier, len(partners))
    asks = []
    for side, other in ((0, before), (1, after)):
        copy = pltpu.make_async_remote_copy(
            src_ref=wants.at[side], dst_ref=asked.at[1 - side],
            send_sem=list_send.at[side], recv_sem=list_recv.at[1 - side],
            device_id={"pairs": other}, device_id_type=MESH,
        )
        copy.start()
        asks.append(copy)

    own.wait()
    for copy in gathers[1:]:
        copy.wait()
    ones = jnp.where(
        lax.div(lax.broadcasted_iota(jnp.int32, (128, 128), 0), BAND)
        == lax.div(lax.broadcasted_iota(jnp.int32, (128, 128), 1), BAND),
        1.0, 0.0,
    ).astype(BF16)
    diagonal = lax.rem(
        lax.broadcasted_iota(jnp.int32, (block, segments), 0), segments
    ) == lax.broadcasted_iota(jnp.int32, (block, segments), 1)

    def station_body(s, carry):
        flags = masks_ref[s].astype(F32)
        lines = jnp.concatenate(
            [jnp.broadcast_to(flags[w : w + 1], (segments, segments)) for w in range(windows)], 0
        )
        mask = jnp.sum(jnp.where(diagonal, lines, 0.0), axis=1, keepdims=True)
        x = jnp.swapaxes(raw[s].astype(F32), 0, 1)
        re, im = whiten(x, mask, ones)
        mine[s, 0], mine[s, 1] = re, im
        near[some + s, 0], near[some + s, 1] = re, im
        return carry

    lax.fori_loop(0, stations, station_body, 0, unroll=2)
    sends = []
    for side, other in ((1, after), (0, before)):
        asks[1 - side].wait_recv()
        slot = 0 if side == 1 else some + stations
        for t in range(some):
            packed[side, t] = mine[jnp.clip(asked[side, t], 0, stations - 1)]
            copy = pltpu.make_async_remote_copy(
                src_ref=packed.at[side, t], dst_ref=near.at[slot + t],
                send_sem=halo_send.at[side, t], recv_sem=halo_recv.at[side, t],
                device_id={"pairs": other}, device_id_type=MESH,
            )
            copy.start()
            sends.append(copy)
    for copy in asks:
        copy.wait_send()

    coef[...] = jnp.zeros_like(coef)
    extra = held_rows.shape[0] - count
    held_rows[count:, :] = jnp.concatenate(
        [start_ref[...], jnp.zeros((extra - RANK, lags), F32)], 0
    ).astype(BF16)
    for p in range(pairs):
        local = lax.rem(rows_ref[1, p], stations)
        relative = lax.div(keys[p], stations)
        low, high = place[0][0], some + stations + place[1][0]
        for j in range(1, stations):
            low = jnp.where(local == j, place[0][j], low)
            high = jnp.where(local == j, some + stations + place[1][j], high)
        at_b = jnp.where(relative == 0, low, jnp.where(relative == 1, some + local, high))
        places[0, p] = some + lax.rem(rows_ref[0, p], stations)
        places[1, p] = jnp.clip(at_b, 0, 2 * stations - 1)
    turn = lax.rem(lax.broadcasted_iota(jnp.int32, (block, freq), 1), 4)
    swap_lanes = lax.rem(turn, 2) == 0
    sign_re = jnp.where((turn == 0) | (turn == 3), 1.0, -1.0)[:1].astype(BF16)
    sign_im = jnp.where(turn >= 2, 1.0, -1.0)[:1].astype(BF16)
    for copy in sends:
        copy.wait()

    def pair_body(p, carry):
        a = near[places[0, p]].astype(F32)
        b = near[places[1, p]].astype(F32)
        re = a[0] * b[0] + a[1] * b[1]
        im = a[1] * b[0] - a[0] * b[1]
        re, im = re.astype(BF16), im.astype(BF16)
        low = pl.ds(pl.multiple_of(p * block, block), block)
        high = pl.ds(pl.multiple_of(count + p * block, block), block)
        cross[high, :freq] = re
        cross[high, freq:] = im
        cross[low, :freq] = jnp.where(swap_lanes, im, re) * sign_re
        cross[low, freq:] = jnp.where(swap_lanes, re, im) * sign_im
        return carry

    lax.fori_loop(0, pairs, pair_body, 0, unroll=3)
    for copy in fills:
        copy.wait()
    tile = 512

    def lag_body(n, carry):
        y = jnp.dot(
            cross[...],
            table[:, pl.ds(pl.multiple_of(n * tile, tile), tile)],
            preferred_element_type=F32,
        ).astype(BF16)
        held_rows[:count, pl.ds(pl.multiple_of(n * tile, tile), tile)] = y[:count]
        held_rows[:count, pl.ds(pl.multiple_of(half + n * tile, tile), tile)] = y[count:]
        return carry

    lax.fori_loop(0, half // tile, lag_body, 0)
    gram = nt(held_rows[: count + 16], held_rows[...])
    lane = lax.broadcasted_iota(jnp.int32, (1, 128), 1)
    group = lax.div(lax.broadcasted_iota(jnp.int32, (1, 256), 1), 8)
    row_batch = lax.div(lax.broadcasted_iota(jnp.int32, (count, 1), 0), 8)
    batch = lax.broadcasted_iota(jnp.int32, (batches, 1), 0)
    mixed = lane >= segments
    near_lanes = lane < segments
    both = lane < segments + RANK
    shift = (128 - (count - 128) + segments) % 128

    def twelve(folded, tail):
        moved = pltpu.roll(tail, shift, 1)
        return jnp.where(near_lanes, folded, jnp.where(both, moved, 0.0))

    square[...] = twelve(fold8(gram[:count], group, row_batch), gram[:count, 128:])
    rows12 = [square[pl.ds(g, batches, stride=segments), :] for g in range(segments)]
    for r in range(RANK):
        line = jnp.broadcast_to(gram[count + r : count + r + 1], (batches, 256))
        rows12.append(twelve(fold8(line, group, batch), line[:, 128:]))

    def product(vectors):
        out = []
        for vector in vectors:
            total = vector[:, 0:1] * rows12[0]
            for j in range(1, segments + RANK):
                total = total + vector[:, j : j + 1] * rows12[j]
            out.append(total)
        return out

    weight = float(lags)
    held = [jnp.where(lane == segments + r, 1.0, 0.0) for r in range(RANK)]
    seen = [rows12[segments + r] for r in range(RANK)]
    for _ in range(TURNS):
        stepped = [weight * held[r] + jnp.where(near_lanes, seen[r], 0.0) for r in range(RANK)]
        image = product(stepped)
        small = [
            [jnp.sum(image[i] * stepped[j], axis=1, keepdims=True) for j in range(i + 1)]
            for i in range(RANK)
        ]
        lower = cholesky(small)
        held = solve(lower, stepped)
        seen = solve(lower, image)
    onto = [jnp.where(near_lanes, seen[r], 0.0) for r in range(RANK)]
    final = [weight * held[r] + onto[r] for r in range(RANK)]
    window = None
    for r in range(RANK):
        term = jnp.sum(onto[r], axis=1, keepdims=True) * held[r]
        window = term if window is None else window + term
    window = window * (1.0 / math.sqrt(segments))

    def spread(x):
        tail = pltpu.roll(jnp.where(mixed, x, 0.0), 128 - shift, 1)
        base = jnp.where(near_lanes, x, 0.0)
        for step in (8, 16, 32, 64):
            base = base + pltpu.roll(base, step, 1)
        left = jnp.where(group[:, :128] == batch, base, 0.0)
        right = jnp.where(group[:, 128:] == batch, base, 0.0) + tail
        return jnp.concatenate([left, right], 1)

    shown = spread(window)
    coef[:batches] = shown
    hours = lax.axis_size("hours")
    units = [spread(x) for x in final] + [shown * (1.0 / math.sqrt(windows * hours))]
    each = pairs // 2
    for r, unit in enumerate(units):
        for side in range(2):
            wide[side] = unit[:, side * 128 : (side + 1) * 128]
            total = wide.at[side][pl.ds(0, pairs, stride=windows), :]
            for w in range(1, windows):
                total = total + wide.at[side][pl.ds(w, pairs, stride=windows), :]
            for c in range(2):
                start = batches + c * slots + r * each
                columns = slice(side * 128, (side + 1) * 128)
                coef[start : start + each, columns] = total[c * each : (c + 1) * each]

    coefs = jnp.concatenate(split(coef[...]), 0)
    size = coef.shape[0]
    width = lags // chips
    chunk = across * width
    rows_order = sorted(range(other_side), key=lambda d: -min(d, other_side - d))
    columns_order = sorted(range(across), key=lambda d: -min(d, across - d))
    swaps, sends = [], []

    def scatter(i):
        kept = None
        swaps[i].wait_recv()
        for dy in columns_order:
            goal_column = lax.rem(column + dy, across)
            lanes = pl.ds(pl.multiple_of(goal_column * width, width), width)
            block_sum = part[i, core, :, lanes] + sib[i, :, lanes]
            if rows_order[i] == 0 and dy == 0:
                kept = block_sum
                continue
            index = len(sends)
            outgoing[index] = block_sum.astype(BF16)
            copy = pltpu.make_async_remote_copy(
                src_ref=outgoing.at[index], dst_ref=incoming.at[index],
                send_sem=out_send.at[index], recv_sem=in_recv.at[index],
                device_id=device((rows_order[i], dy, 0)), device_id_type=MESH,
            )
            copy.start()
            sends.append(copy)
        return kept

    for i, dx in enumerate(rows_order):
        goal_row = lax.rem(row + dx, other_side)
        columns = pl.ds(pl.multiple_of(goal_row * chunk, chunk), chunk)
        out = jnp.dot(coefs, held_rows[:, columns], preferred_element_type=F32)
        out = out[:size] + out[size:]
        for c in range(2):
            part[i, c] = out[batches + c * slots : batches + (c + 1) * slots]
        copy = pltpu.make_async_remote_copy(
            src_ref=part.at[i, 1 - core], dst_ref=sib.at[i],
            send_sem=send_sem.at[i], recv_sem=recv_sem.at[i],
            device_id=twin, device_id_type=MESH,
        )
        copy.start()
        swaps.append(copy)
        ws_ref[:, columns] = out[:batches]
        if i > 0:
            scatter(i - 1)
    merged = scatter(other_side - 1)
    for index in reversed(range(len(sends))):
        sends[index].wait_recv()
        merged = merged + incoming[index].astype(F32)
    summed_rows[...] = merged

    swap = pltpu.make_async_remote_copy(
        src_ref=summed_rows, dst_ref=theirs, send_sem=send_sem.at[other_side], recv_sem=recv_sem.at[other_side],
        device_id=twin, device_id_type=MESH,
    )
    swap.start()
    vectors = [summed_rows[r * each : (r + 1) * each] for r in range(RANK)]
    order = [(i, j) for i in range(RANK) for j in range(i + 1)]
    line = lax.broadcasted_iota(jnp.int32, (each, 128), 1)
    pair_of = lax.broadcasted_iota(jnp.int32, (each, 128), 0)
    marks = [line == 8 * index + pair_of for index in range(len(order))]
    tile = jnp.zeros((each, 128), F32)
    for mark, (i, j) in zip(marks, order):
        tile = jnp.where(mark, jnp.sum(vectors[i] * vectors[j], axis=1, keepdims=True), tile)
    own_gram[...] = jnp.sum(tile, axis=0, keepdims=True)
    tells = []
    for index, place in enumerate(places_from):
        copy = pltpu.make_async_remote_copy(
            src_ref=own_gram, dst_ref=grams.at[index],
            send_sem=gram_send.at[index], recv_sem=gram_recv.at[index],
            device_id=device(place), device_id_type=MESH,
        )
        copy.start()
        tells.append(copy)
    swap.wait()
    for copy in swaps + sends:
        copy.wait_send()
    gram_sums = [own_gram[...], None]
    for index in reversed(range(len(tells))):
        tells[index].wait_recv()
        flip = places_from[index][2]
        value = grams[index]
        gram_sums[flip] = value if gram_sums[flip] is None else gram_sums[flip] + value
    own_half = width // 2

    def halved(x):
        return jnp.where(core == 0, x[:, :own_half], x[:, own_half:])

    for flip, source in enumerate((summed_rows, theirs)):
        target = core if flip == 0 else 1 - core
        small = [[None] * RANK for _ in range(RANK)]
        for mark, (i, j) in zip(marks, order):
            small[i][j] = jnp.sum(
                jnp.where(mark, gram_sums[flip], 0.0), axis=1, keepdims=True
            )
        pieces = [halved(source[r * each : (r + 1) * each]) for r in range(RANK)]
        for r, value in enumerate(solve(cholesky(small), pieces)):
            out_ref[target, r * each : (r + 1) * each] = value * math.sqrt(lags)
        out_ref[target, RANK * each :] = halved(source[RANK * each :])
    for copy in tells:
        copy.wait_send()


def finish_kernel(pairs, windows, windows_ref, merged_ref, ws_ref, stack_ref, basis_ref):
    each = pairs // 2
    for p in range(pairs):
        ws_ref[p] = windows_ref[windows * p : windows * (p + 1)]
    rows = merged_ref[...]
    stack_ref[...] = jnp.concatenate(
        [rows[c, RANK * each : (RANK + 1) * each] for c in range(2)], 0
    )
    for p in range(pairs):
        c, q = divmod(p, each)
        for r in range(RANK):
            basis_ref[p, r : r + 1] = rows[c, r * each + q : r * each + q + 1]


def on_device(table, spectra, masks, pair_rows, start_basis):
    stations, windows, segments, _, freq = spectra.shape
    lags = start_basis.shape[1]
    half = lags // 2
    pairs = pair_rows.shape[0]
    block = windows * segments
    count = pairs * block
    batches = pairs * windows
    each = pairs // 2
    slots = 32
    chips = lax.axis_size("hours") // 2
    width = lags // chips
    rows_of_chips = torus_offsets(chips)[1]
    raw = spectra.reshape(stations, block, 2, freq)
    vmem = pl.BlockSpec(memory_space=pltpu.VMEM)
    windows_out, merged = pl.pallas_call(
        functools.partial(station_kernel, stations, segments, windows, pairs, freq, half),
        out_shape=(
            pltpu.VMEM((batches, lags), F32),
            pltpu.VMEM((2, slots, width // 2), F32),
        ),
        in_specs=[
            pl.BlockSpec(memory_space=pltpu.HBM),
        ]
        * 5,
        out_specs=(vmem, vmem),
        scratch_shapes=[
            pltpu.SMEM((2, pairs), jnp.int32),
            pltpu.VMEM((stations, windows, segments), jnp.int32),
            pltpu.VMEM((RANK, lags), F32),
            pltpu.VMEM((stations, block, 2, freq), BF16),
            pltpu.VMEM((stations, 2, block, freq), BF16),
            pltpu.VMEM((2, stations // 2, 2, block, freq), BF16),
            pltpu.SMEM((2, stations // 2), jnp.int32),
            pltpu.SMEM((2, stations // 2), jnp.int32),
            pltpu.SMEM((2, pairs), jnp.int32),
            pltpu.VMEM((2 * stations, 2, block, freq), BF16),
            pltpu.VMEM((2 * count, 2 * freq), BF16),
            pltpu.VMEM((2 * freq, half), BF16),
            pltpu.VMEM((256, lags), BF16),
            pltpu.VMEM((count, 128), F32),
            pltpu.VMEM((2, batches, 128), F32),
            pltpu.VMEM((batches + 2 * slots, 256), F32),
            pltpu.VMEM((rows_of_chips, 2, slots, lags // rows_of_chips), F32),
            pltpu.VMEM((rows_of_chips, slots, lags // rows_of_chips), F32),
            pltpu.VMEM((chips - 1, slots, width), BF16),
            pltpu.VMEM((chips - 1, slots, width), BF16),
            pltpu.VMEM((slots, width), F32),
            pltpu.VMEM((slots, width), F32),
            pltpu.VMEM((1, 128), F32),
            pltpu.VMEM((2 * chips - 1, 1, 128), F32),
            pltpu.SemaphoreType.DMA((2,)),
            pltpu.SemaphoreType.DMA((2,)),
            pltpu.SemaphoreType.DMA((2, stations // 2)),
            pltpu.SemaphoreType.DMA((2, stations // 2)),
            pltpu.SemaphoreType.DMA((rows_of_chips + 1,)),
            pltpu.SemaphoreType.DMA((rows_of_chips + 1,)),
            pltpu.SemaphoreType.DMA((5,)),
            pltpu.SemaphoreType.DMA((4,)),
            pltpu.SemaphoreType.DMA((chips - 1,)),
            pltpu.SemaphoreType.DMA((chips - 1,)),
            pltpu.SemaphoreType.DMA((2 * chips - 1,)),
            pltpu.SemaphoreType.DMA((2 * chips - 1,)),
        ],
        compiler_params=pltpu.CompilerParams(
            collective_id=0, has_side_effects=True, vmem_limit_bytes=60 << 20
        ),
        name="station_pairs",
    )(pair_rows.T, masks, raw, table, start_basis)
    return pl.pallas_call(
        functools.partial(finish_kernel, pairs, windows),
        out_shape=(
            jax.ShapeDtypeStruct((pairs, windows, lags), F32),
            jax.ShapeDtypeStruct((pairs, width // 2), F32),
            jax.ShapeDtypeStruct((pairs, RANK, width // 2), F32),
        ),
        in_specs=[vmem, vmem],
        out_specs=(vmem, vmem, vmem),
        compiler_params=pltpu.CompilerParams(vmem_limit_bytes=4 << 20),
        name="outputs",
    )(windows_out, merged)


def solution(mesh):
    in_specs = (
        P("pairs", "hours", None, None, None),
        P("pairs", "hours", None),
        P("pairs", None),
        P(),
    )
    out_specs = (P("pairs", "hours", None), P("pairs", "hours"), P("pairs", None, "hours"))

    def whole(spectra, masks, pair_rows, start_basis):
        table = jnp.asarray(half_table(spectra.shape[4], start_basis.shape[1] // 2))
        return jax.shard_map(
            on_device, mesh=mesh, in_specs=(P(), *in_specs), out_specs=out_specs, check_vma=False
        )(table, spectra, masks, pair_rows, start_basis)

    return whole
```

```python
import functools
import math

import jax
import jax.numpy as jnp
import numpy as np
from jax import lax
from jax.experimental import pallas as pl
from jax.experimental.pallas import tpu as pltpu
from jax.sharding import PartitionSpec as P

BAND = 64
TURNS = 2
RANK = 4
MESH = pl.DeviceIdType.MESH
F32 = jnp.float32
BF16 = jnp.bfloat16


def half_table(freq, half):
    bins = np.arange(1, freq + 1, dtype=np.int64)[:, None]
    shifts = np.arange(half, dtype=np.int64)[None, :]
    phase = np.mod(bins * shifts, 4 * half).astype(np.float64) * (math.pi / (2 * half))
    scale = freq ** (-0.5)
    table = np.concatenate([np.cos(phase) * scale, -np.sin(phase) * scale], 0)
    return table.astype(np.float32).astype(jnp.bfloat16)


def whiten(x, mask, ones):
    rows, freq = x.shape[1:]
    square = x[0] * x[0] + x[1] * x[1]
    tiles = freq // 128
    stacked = jnp.concatenate([square[:, t * 128 : (t + 1) * 128] for t in range(tiles)], 0)
    hi, lo = split(stacked)
    power = jnp.dot(hi, ones, preferred_element_type=F32) + jnp.dot(
        lo, ones, preferred_element_type=F32
    )
    scale = lax.rsqrt(power * (0.5 / BAND) + 1e-06)
    scale = jnp.concatenate([scale[t * rows : (t + 1) * rows] for t in range(tiles)], 1) * mask
    return (x[0] * scale).astype(BF16), (x[1] * scale).astype(BF16)


def nt(a, b):
    return lax.dot_general(a, b, (((1,), (1,)), ((), ())), preferred_element_type=F32)


def split(x):
    hi = x.astype(BF16)
    return hi, (x - hi.astype(F32)).astype(BF16)


def cholesky(gram):
    lower = [[None] * RANK for _ in range(RANK)]
    for row in range(RANK):
        for col in range(row + 1):
            total = gram[row][col]
            for inner in range(col):
                total = total - lower[row][inner] * lower[col][inner]
            lower[row][col] = 1.0 / jnp.sqrt(total) if row == col else total * lower[col][col]
    return lower


def solve(lower, vectors):
    result = []
    for row in range(RANK):
        current = vectors[row]
        for inner in range(row):
            current = current - lower[row][inner] * result[inner]
        result.append(current * lower[row][row])
    return result


def fold8(x, batch_of_lane, batch):
    kept = jnp.where(batch_of_lane == batch, x, 0.0)
    total = kept[:, :128] + kept[:, 128:]
    for shift in (64, 32, 16, 8):
        total = total + pltpu.roll(total, shift, 1)
    return total


def torus_offsets(chips):
    side = math.isqrt(chips)
    side = side if side * side == chips else 1
    other = chips // side
    offsets = [(dx, dy) for dx in range(other) for dy in range(side) if dx or dy]
    return side, other, sorted(
        offsets, key=lambda o: -(min(o[0], other - o[0]) + min(o[1], side - o[1]))
    )


def station_kernel(
    stations, segments, windows, pairs, freq, half,
    rows_hbm, masks_hbm, raw_ref, table_ref, start_hbm,
    ws_ref, out_ref,
    rows_ref, masks_ref, start_ref, raw, mine, packed, wants, asked, places, near,
    cross, table, held_rows, square, wide, coef,
    part, incoming, summed_rows, theirs, own_gram, grams,
    list_send, list_recv, halo_send, halo_recv, send_sem, recv_sem, own_sem, fill_sem,
    out_send, in_recv, gram_send, gram_recv,
):
    me, ring = lax.axis_index("pairs"), lax.axis_size("pairs")
    after, before = lax.rem(me + 1, ring), lax.rem(me + ring - 1, ring)
    block = windows * segments
    count = pairs * block
    batches = pairs * windows
    lags = 2 * half
    slots = coef.shape[0] // 2 - batches // 2
    some = stations // 2
    own = pltpu.make_async_copy(raw_ref, raw, own_sem.at[0])
    cuts = 4
    band = 2 * freq // cuts
    fills = [
        pltpu.make_async_copy(
            table_ref.at[pl.ds(i * band, band)], table.at[pl.ds(i * band, band)], fill_sem.at[i]
        )
        for i in range(cuts)
    ]
    gathers = [
        pltpu.make_async_copy(source, target, own_sem.at[2 + index])
        for index, (source, target) in enumerate(
            ((rows_hbm, rows_ref), (masks_hbm, masks_ref), (start_hbm, start_ref))
        )
    ]
    for copy in gathers:
        copy.start()
    own.start()
    for copy in fills:
        copy.start()

    hour = lax.axis_index("hours")
    chips = lax.axis_size("hours") // 2
    core, chip = lax.rem(hour, 2), lax.div(hour, 2)
    twin = {"hours": hour + 1 - 2 * core}
    across, other_side, offsets = torus_offsets(chips)
    row, column = lax.div(chip, across), lax.rem(chip, across)
    places_from = [(dx, dy, flip) for dx, dy in offsets + [(0, 0)] for flip in range(2)][:-2]
    places_from.append((0, 0, 1))

    def device(place):
        dx, dy, flip = place
        goal = across * lax.rem(row + dx, other_side) + lax.rem(column + dy, across)
        return {"hours": 2 * goal + (core if flip == 0 else 1 - core)}

    barrier = pltpu.get_barrier_semaphore()
    partners = [{"pairs": before}, {"pairs": after}]
    partners += [device(place) for place in places_from]
    for other in partners:
        pl.semaphore_signal(barrier, inc=1, device_id=other, device_id_type=MESH)

    gathers[0].wait()
    keys = []
    for p in range(pairs):
        second = rows_ref[1, p]
        relative = lax.rem(lax.div(second, stations) - me + 1 + ring, ring)
        keys.append(relative * stations + lax.rem(second, stations))
    place = []
    for side in range(2):
        taken, slots_of = 0, []
        picks = [0] * some
        for j in range(stations):
            found = keys[0] == 2 * side * stations + j
            for key in keys[1:]:
                found = found | (key == 2 * side * stations + j)
            used = found.astype(jnp.int32)
            slots_of.append(taken)
            for t in range(some):
                picks[t] = picks[t] + jnp.where(found & (taken == t), j, 0)
            taken = taken + used
        place.append(slots_of)
        for t in range(some):
            wants[side, t] = picks[t]
    pl.semaphore_wait(barrier, len(partners))
    asks = []
    for side, other in ((0, before), (1, after)):
        copy = pltpu.make_async_remote_copy(
            src_ref=wants.at[side], dst_ref=asked.at[1 - side],
            send_sem=list_send.at[side], recv_sem=list_recv.at[1 - side],
            device_id={"pairs": other}, device_id_type=MESH,
        )
        copy.start()
        asks.append(copy)

    own.wait()
    for copy in gathers[1:]:
        copy.wait()
    ones = jnp.where(
        lax.div(lax.broadcasted_iota(jnp.int32, (128, 128), 0), BAND)
        == lax.div(lax.broadcasted_iota(jnp.int32, (128, 128), 1), BAND),
        1.0, 0.0,
    ).astype(BF16)
    diagonal = lax.rem(
        lax.broadcasted_iota(jnp.int32, (block, segments), 0), segments
    ) == lax.broadcasted_iota(jnp.int32, (block, segments), 1)

    def station_body(s, carry):
        flags = masks_ref[s].astype(F32)
        lines = jnp.concatenate(
            [jnp.broadcast_to(flags[w : w + 1], (segments, segments)) for w in range(windows)], 0
        )
        mask = jnp.sum(jnp.where(diagonal, lines, 0.0), axis=1, keepdims=True)
        x = jnp.swapaxes(raw[s].astype(F32), 0, 1)
        re, im = whiten(x, mask, ones)
        mine[s, 0], mine[s, 1] = re, im
        near[some + s, 0], near[some + s, 1] = re, im
        return carry

    lax.fori_loop(0, stations, station_body, 0, unroll=2)
    sends = []
    for side, other in ((1, after), (0, before)):
        asks[1 - side].wait_recv()
        slot = 0 if side == 1 else some + stations
        for t in range(some):
            packed[side, t] = mine[jnp.clip(asked[side, t], 0, stations - 1)]
            copy = pltpu.make_async_remote_copy(
                src_ref=packed.at[side, t], dst_ref=near.at[slot + t],
                send_sem=halo_send.at[side, t], recv_sem=halo_recv.at[side, t],
                device_id={"pairs": other}, device_id_type=MESH,
            )
            copy.start()
            sends.append(copy)
    for copy in asks:
        copy.wait_send()

    coef[...] = jnp.zeros_like(coef)
    extra = held_rows.shape[0] - count
    held_rows[count:, :] = jnp.concatenate(
        [start_ref[...], jnp.zeros((extra - RANK, lags), F32)], 0
    ).astype(BF16)
    for p in range(pairs):
        local = lax.rem(rows_ref[1, p], stations)
        relative = lax.div(keys[p], stations)
        low, high = place[0][0], some + stations + place[1][0]
        for j in range(1, stations):
            low = jnp.where(local == j, place[0][j], low)
            high = jnp.where(local == j, some + stations + place[1][j], high)
        at_b = jnp.where(relative == 0, low, jnp.where(relative == 1, some + local, high))
        places[0, p] = some + lax.rem(rows_ref[0, p], stations)
        places[1, p] = jnp.clip(at_b, 0, 2 * stations - 1)
    turn = lax.rem(lax.broadcasted_iota(jnp.int32, (block, freq), 1), 4)
    swap_lanes = lax.rem(turn, 2) == 0
    sign_re = jnp.where((turn == 0) | (turn == 3), 1.0, -1.0)[:1].astype(BF16)
    sign_im = jnp.where(turn >= 2, 1.0, -1.0)[:1].astype(BF16)
    for copy in sends:
        copy.wait_recv()
    halos = sends

    def pair_body(p, carry):
        a = near[places[0, p]].astype(F32)
        b = near[places[1, p]].astype(F32)
        re = a[0] * b[0] + a[1] * b[1]
        im = a[1] * b[0] - a[0] * b[1]
        re, im = re.astype(BF16), im.astype(BF16)
        low = pl.ds(pl.multiple_of(p * block, block), block)
        high = pl.ds(pl.multiple_of(count + p * block, block), block)
        cross[high, :freq] = re
        cross[high, freq:] = im
        cross[low, :freq] = jnp.where(swap_lanes, im, re) * sign_re
        cross[low, freq:] = jnp.where(swap_lanes, re, im) * sign_im
        return carry

    lax.fori_loop(0, pairs, pair_body, 0, unroll=3)
    for copy in fills:
        copy.wait()
    tile = 512

    def lag_body(n, carry):
        y = jnp.dot(
            cross[...],
            table[:, pl.ds(pl.multiple_of(n * tile, tile), tile)],
            preferred_element_type=F32,
        ).astype(BF16)
        held_rows[:count, pl.ds(pl.multiple_of(n * tile, tile), tile)] = y[:count]
        held_rows[:count, pl.ds(pl.multiple_of(half + n * tile, tile), tile)] = y[count:]
        return carry

    lax.fori_loop(0, half // tile, lag_body, 0)
    gram = nt(held_rows[: count + 16], held_rows[...])
    lane = lax.broadcasted_iota(jnp.int32, (1, 128), 1)
    group = lax.div(lax.broadcasted_iota(jnp.int32, (1, 256), 1), 8)
    row_batch = lax.div(lax.broadcasted_iota(jnp.int32, (count, 1), 0), 8)
    batch = lax.broadcasted_iota(jnp.int32, (batches, 1), 0)
    mixed = lane >= segments
    near_lanes = lane < segments
    both = lane < segments + RANK
    shift = (128 - (count - 128) + segments) % 128

    def twelve(folded, tail):
        moved = pltpu.roll(tail, shift, 1)
        return jnp.where(near_lanes, folded, jnp.where(both, moved, 0.0))

    square[...] = twelve(fold8(gram[:count], group, row_batch), gram[:count, 128:])
    rows12 = [square[pl.ds(g, batches, stride=segments), :] for g in range(segments)]
    for r in range(RANK):
        line = jnp.broadcast_to(gram[count + r : count + r + 1], (batches, 256))
        rows12.append(twelve(fold8(line, group, batch), line[:, 128:]))

    def product(vectors):
        out = []
        for vector in vectors:
            total = vector[:, 0:1] * rows12[0]
            for j in range(1, segments + RANK):
                total = total + vector[:, j : j + 1] * rows12[j]
            out.append(total)
        return out

    weight = float(lags)
    held = [jnp.where(lane == segments + r, 1.0, 0.0) for r in range(RANK)]
    seen = [rows12[segments + r] for r in range(RANK)]
    for _ in range(TURNS):
        stepped = [weight * held[r] + jnp.where(near_lanes, seen[r], 0.0) for r in range(RANK)]
        image = product(stepped)
        small = [
            [jnp.sum(image[i] * stepped[j], axis=1, keepdims=True) for j in range(i + 1)]
            for i in range(RANK)
        ]
        lower = cholesky(small)
        held = solve(lower, stepped)
        seen = solve(lower, image)
    onto = [jnp.where(near_lanes, seen[r], 0.0) for r in range(RANK)]
    final = [weight * held[r] + onto[r] for r in range(RANK)]
    window = None
    for r in range(RANK):
        term = jnp.sum(onto[r], axis=1, keepdims=True) * held[r]
        window = term if window is None else window + term
    window = window * (1.0 / math.sqrt(segments))

    def spread(x):
        tail = pltpu.roll(jnp.where(mixed, x, 0.0), 128 - shift, 1)
        base = jnp.where(near_lanes, x, 0.0)
        for step in (8, 16, 32, 64):
            base = base + pltpu.roll(base, step, 1)
        left = jnp.where(group[:, :128] == batch, base, 0.0)
        right = jnp.where(group[:, 128:] == batch, base, 0.0) + tail
        return jnp.concatenate([left, right], 1)

    shown = spread(window)
    coef[:batches] = shown
    hours = lax.axis_size("hours")
    units = [spread(x) for x in final] + [shown * (1.0 / math.sqrt(windows * hours))]
    each = pairs // 2
    for r, unit in enumerate(units):
        for side in range(2):
            wide[side] = unit[:, side * 128 : (side + 1) * 128]
            total = wide.at[side][pl.ds(0, pairs, stride=windows), :]
            for w in range(1, windows):
                total = total + wide.at[side][pl.ds(w, pairs, stride=windows), :]
            for c in range(2):
                start = batches + c * slots + r * each
                columns = slice(side * 128, (side + 1) * 128)
                coef[start : start + each, columns] = total[c * each : (c + 1) * each]

    coefs = jnp.concatenate(split(coef[batches:]), 0)
    size = coef.shape[0] - batches
    width = lags // chips
    chunk = across * width
    rows_order = sorted(range(other_side), key=lambda d: -min(d, other_side - d))
    columns_order = sorted(range(across), key=lambda d: -min(d, across - d))
    sends = []
    for i, dx in enumerate(rows_order):
        goal_row = lax.rem(row + dx, other_side)
        columns = pl.ds(pl.multiple_of(goal_row * chunk, chunk), chunk)
        out = jnp.dot(coefs, held_rows[:, columns], preferred_element_type=F32)
        out = out[:size] + out[size:]
        for c in range(2):
            block_rows = out[c * slots : (c + 1) * slots].astype(BF16)
            for y in range(across):
                part[i, c, y] = block_rows[:, y * width : (y + 1) * width]
        for dy in columns_order:
            for flip in range(2):
                if (dx, dy, flip) == (0, 0, 0):
                    continue
                index = places_from.index((dx, dy, flip))
                copy = pltpu.make_async_remote_copy(
                    src_ref=part.at[
                        i, core if flip == 0 else 1 - core, lax.rem(column + dy, across)
                    ],
                    dst_ref=incoming.at[index],
                    send_sem=out_send.at[index], recv_sem=in_recv.at[index],
                    device_id=device((dx, dy, flip)), device_id_type=MESH,
                )
                copy.start()
                sends.append((index, copy))
    coefs = jnp.concatenate(split(coef[:batches]), 0)
    for i in range(other_side):
        columns = slice(i * chunk, (i + 1) * chunk)
        out = jnp.dot(coefs, held_rows[:, columns], preferred_element_type=F32)
        ws_ref[:, columns] = out[:batches] + out[batches:]
    merged = part[other_side - 1, core, column].astype(F32)
    for index, copy in reversed(sends):
        copy.wait_recv()
        merged = merged + incoming[index].astype(F32)
    summed_rows[...] = merged

    swap = pltpu.make_async_remote_copy(
        src_ref=summed_rows, dst_ref=theirs, send_sem=send_sem.at[0], recv_sem=recv_sem.at[0],
        device_id=twin, device_id_type=MESH,
    )
    swap.start()
    vectors = [summed_rows[r * each : (r + 1) * each] for r in range(RANK)]
    order = [(i, j) for i in range(RANK) for j in range(i + 1)]
    line = lax.broadcasted_iota(jnp.int32, (each, 128), 1)
    pair_of = lax.broadcasted_iota(jnp.int32, (each, 128), 0)
    marks = [line == 8 * index + pair_of for index in range(len(order))]
    tile = jnp.zeros((each, 128), F32)
    for mark, (i, j) in zip(marks, order):
        tile = jnp.where(mark, jnp.sum(vectors[i] * vectors[j], axis=1, keepdims=True), tile)
    own_gram[...] = jnp.sum(tile, axis=0, keepdims=True)
    tells = []
    for index, place in enumerate(places_from):
        copy = pltpu.make_async_remote_copy(
            src_ref=own_gram, dst_ref=grams.at[index],
            send_sem=gram_send.at[index], recv_sem=gram_recv.at[index],
            device_id=device(place), device_id_type=MESH,
        )
        copy.start()
        tells.append(copy)
    swap.wait()
    for copy in halos:
        copy.wait_send()
    for _, copy in sends:
        copy.wait_send()
    gram_sums = [own_gram[...], None]
    for index in reversed(range(len(tells))):
        tells[index].wait_recv()
        flip = places_from[index][2]
        value = grams[index]
        gram_sums[flip] = value if gram_sums[flip] is None else gram_sums[flip] + value
    own_half = width // 2

    def halved(x):
        return jnp.where(core == 0, x[:, :own_half], x[:, own_half:])

    for flip, source in enumerate((summed_rows, theirs)):
        target = core if flip == 0 else 1 - core
        small = [[None] * RANK for _ in range(RANK)]
        for mark, (i, j) in zip(marks, order):
            small[i][j] = jnp.sum(
                jnp.where(mark, gram_sums[flip], 0.0), axis=1, keepdims=True
            )
        pieces = [halved(source[r * each : (r + 1) * each]) for r in range(RANK)]
        for r, value in enumerate(solve(cholesky(small), pieces)):
            out_ref[target, r * each : (r + 1) * each] = value * math.sqrt(lags)
        out_ref[target, RANK * each :] = halved(source[RANK * each :])
    for copy in tells:
        copy.wait_send()


def finish_kernel(pairs, windows, windows_ref, merged_ref, ws_ref, stack_ref, basis_ref):
    each = pairs // 2
    for p in range(pairs):
        ws_ref[p] = windows_ref[windows * p : windows * (p + 1)]
    rows = merged_ref[...]
    stack_ref[...] = jnp.concatenate(
        [rows[c, RANK * each : (RANK + 1) * each] for c in range(2)], 0
    )
    for p in range(pairs):
        c, q = divmod(p, each)
        for r in range(RANK):
            basis_ref[p, r : r + 1] = rows[c, r * each + q : r * each + q + 1]


def on_device(table, spectra, masks, pair_rows, start_basis):
    stations, windows, segments, _, freq = spectra.shape
    lags = start_basis.shape[1]
    half = lags // 2
    pairs = pair_rows.shape[0]
    block = windows * segments
    count = pairs * block
    batches = pairs * windows
    each = pairs // 2
    slots = 32
    chips = lax.axis_size("hours") // 2
    width = lags // chips
    rows_of_chips = torus_offsets(chips)[1]
    raw = spectra.reshape(stations, block, 2, freq)
    vmem = pl.BlockSpec(memory_space=pltpu.VMEM)
    windows_out, merged = pl.pallas_call(
        functools.partial(station_kernel, stations, segments, windows, pairs, freq, half),
        out_shape=(
            pltpu.VMEM((batches, lags), F32),
            pltpu.VMEM((2, slots, width // 2), F32),
        ),
        in_specs=[
            pl.BlockSpec(memory_space=pltpu.HBM),
        ]
        * 5,
        out_specs=(vmem, vmem),
        scratch_shapes=[
            pltpu.SMEM((2, pairs), jnp.int32),
            pltpu.VMEM((stations, windows, segments), jnp.int32),
            pltpu.VMEM((RANK, lags), F32),
            pltpu.VMEM((stations, block, 2, freq), BF16),
            pltpu.VMEM((stations, 2, block, freq), BF16),
            pltpu.VMEM((2, stations // 2, 2, block, freq), BF16),
            pltpu.SMEM((2, stations // 2), jnp.int32),
            pltpu.SMEM((2, stations // 2), jnp.int32),
            pltpu.SMEM((2, pairs), jnp.int32),
            pltpu.VMEM((2 * stations, 2, block, freq), BF16),
            pltpu.VMEM((2 * count, 2 * freq), BF16),
            pltpu.VMEM((2 * freq, half), BF16),
            pltpu.VMEM((256, lags), BF16),
            pltpu.VMEM((count, 128), F32),
            pltpu.VMEM((2, batches, 128), F32),
            pltpu.VMEM((batches + 2 * slots, 256), F32),
            pltpu.VMEM((rows_of_chips, 2, chips // rows_of_chips, slots, width), BF16),
            pltpu.VMEM((2 * chips - 1, slots, width), BF16),
            pltpu.VMEM((slots, width), F32),
            pltpu.VMEM((slots, width), F32),
            pltpu.VMEM((1, 128), F32),
            pltpu.VMEM((2 * chips - 1, 1, 128), F32),
            pltpu.SemaphoreType.DMA((2,)),
            pltpu.SemaphoreType.DMA((2,)),
            pltpu.SemaphoreType.DMA((2, stations // 2)),
            pltpu.SemaphoreType.DMA((2, stations // 2)),
            pltpu.SemaphoreType.DMA((1,)),
            pltpu.SemaphoreType.DMA((1,)),
            pltpu.SemaphoreType.DMA((5,)),
            pltpu.SemaphoreType.DMA((4,)),
            pltpu.SemaphoreType.DMA((2 * chips - 1,)),
            pltpu.SemaphoreType.DMA((2 * chips - 1,)),
            pltpu.SemaphoreType.DMA((2 * chips - 1,)),
            pltpu.SemaphoreType.DMA((2 * chips - 1,)),
        ],
        compiler_params=pltpu.CompilerParams(
            collective_id=0, has_side_effects=True, vmem_limit_bytes=60 << 20
        ),
        name="station_pairs",
    )(pair_rows.T, masks, raw, table, start_basis)
    return pl.pallas_call(
        functools.partial(finish_kernel, pairs, windows),
        out_shape=(
            jax.ShapeDtypeStruct((pairs, windows, lags), F32),
            jax.ShapeDtypeStruct((pairs, width // 2), F32),
            jax.ShapeDtypeStruct((pairs, RANK, width // 2), F32),
        ),
        in_specs=[vmem, vmem],
        out_specs=(vmem, vmem, vmem),
        compiler_params=pltpu.CompilerParams(vmem_limit_bytes=4 << 20),
        name="outputs",
    )(windows_out, merged)


def solution(mesh):
    in_specs = (
        P("pairs", "hours", None, None, None),
        P("pairs", "hours", None),
        P("pairs", None),
        P(),
    )
    out_specs = (P("pairs", "hours", None), P("pairs", "hours"), P("pairs", None, "hours"))

    def whole(spectra, masks, pair_rows, start_basis):
        table = jnp.asarray(half_table(spectra.shape[4], start_basis.shape[1] // 2))
        return jax.shard_map(
            on_device, mesh=mesh, in_specs=(P(), *in_specs), out_specs=out_specs, check_vma=False
        )(table, spectra, masks, pair_rows, start_basis)

    return whole
```

```python
import functools
import math

import jax
import jax.numpy as jnp
import numpy as np
from jax import lax
from jax.experimental import pallas as pl
from jax.experimental.pallas import tpu as pltpu
from jax.sharding import PartitionSpec as P

BAND = 64
TURNS = 2
RANK = 4
MESH = pl.DeviceIdType.MESH
F32 = jnp.float32
BF16 = jnp.bfloat16


def half_table(freq, half):
    bins = np.arange(1, freq + 1, dtype=np.int64)[:, None]
    shifts = np.arange(half, dtype=np.int64)[None, :]
    phase = np.mod(bins * shifts, 4 * half).astype(np.float64) * (math.pi / (2 * half))
    scale = freq ** (-0.5)
    table = np.stack([np.cos(phase) * scale, -np.sin(phase) * scale], 0)
    table = table.reshape(2, 2, freq // 2, half).transpose(1, 0, 2, 3).reshape(2 * freq, half)
    return table.astype(np.float32).astype(jnp.bfloat16)


def whiten(x, mask, ones):
    rows, freq = x.shape[1:]
    square = x[0] * x[0] + x[1] * x[1]
    tiles = freq // 128
    stacked = jnp.concatenate([square[:, t * 128 : (t + 1) * 128] for t in range(tiles)], 0)
    hi, lo = split(stacked)
    power = jnp.dot(hi, ones, preferred_element_type=F32) + jnp.dot(
        lo, ones, preferred_element_type=F32
    )
    scale = lax.rsqrt(power * (0.5 / BAND) + 1e-06)
    scale = jnp.concatenate([scale[t * rows : (t + 1) * rows] for t in range(tiles)], 1) * mask
    return (x[0] * scale).astype(BF16), (x[1] * scale).astype(BF16)


def nt(a, b):
    return lax.dot_general(a, b, (((1,), (1,)), ((), ())), preferred_element_type=F32)


def split(x):
    hi = x.astype(BF16)
    return hi, (x - hi.astype(F32)).astype(BF16)


def cholesky(gram):
    lower = [[None] * RANK for _ in range(RANK)]
    for row in range(RANK):
        for col in range(row + 1):
            total = gram[row][col]
            for inner in range(col):
                total = total - lower[row][inner] * lower[col][inner]
            lower[row][col] = 1.0 / jnp.sqrt(total) if row == col else total * lower[col][col]
    return lower


def solve(lower, vectors):
    result = []
    for row in range(RANK):
        current = vectors[row]
        for inner in range(row):
            current = current - lower[row][inner] * result[inner]
        result.append(current * lower[row][row])
    return result


def fold8(x, batch_of_lane, batch):
    kept = jnp.where(batch_of_lane == batch, x, 0.0)
    total = kept[:, :128] + kept[:, 128:]
    for shift in (64, 32, 16, 8):
        total = total + pltpu.roll(total, shift, 1)
    return total


def torus_offsets(chips):
    side = math.isqrt(chips)
    side = side if side * side == chips else 1
    other = chips // side
    offsets = [(dx, dy) for dx in range(other) for dy in range(side) if dx or dy]
    return side, other, sorted(
        offsets, key=lambda o: -(min(o[0], other - o[0]) + min(o[1], side - o[1]))
    )


def station_kernel(
    stations, segments, windows, pairs, freq, half,
    rows_hbm, masks_hbm, raw_ref, table_ref, start_hbm,
    ws_ref, out_ref,
    rows_ref, masks_ref, start_ref, raw, mine, packed, wants, asked, places, near_low, near_high,
    cross, first_sum, table, held_rows, square, wide, coef,
    part, incoming, summed_rows, theirs, own_gram, grams,
    list_send, list_recv, halo_send, halo_recv, send_sem, recv_sem, own_sem, fill_sem,
    out_send, in_recv, gram_send, gram_recv,
):
    me, ring = lax.axis_index("pairs"), lax.axis_size("pairs")
    after, before = lax.rem(me + 1, ring), lax.rem(me + ring - 1, ring)
    block = windows * segments
    count = pairs * block
    batches = pairs * windows
    lags = 2 * half
    slots = coef.shape[0] // 2 - batches // 2
    some = stations // 2
    own = pltpu.make_async_copy(raw_ref, raw, own_sem.at[0])
    cuts = 4
    band = 2 * freq // cuts
    fills = [
        pltpu.make_async_copy(
            table_ref.at[pl.ds(i * band, band)], table.at[pl.ds(i * band, band)], fill_sem.at[i]
        )
        for i in range(cuts)
    ]
    gathers = [
        pltpu.make_async_copy(source, target, own_sem.at[2 + index])
        for index, (source, target) in enumerate(
            ((rows_hbm, rows_ref), (masks_hbm, masks_ref), (start_hbm, start_ref))
        )
    ]
    for copy in gathers:
        copy.start()
    own.start()
    for copy in fills:
        copy.start()

    hour = lax.axis_index("hours")
    chips = lax.axis_size("hours") // 2
    core, chip = lax.rem(hour, 2), lax.div(hour, 2)
    twin = {"hours": hour + 1 - 2 * core}
    across, other_side, offsets = torus_offsets(chips)
    row, column = lax.div(chip, across), lax.rem(chip, across)
    places_from = [(dx, dy, flip) for dx, dy in offsets + [(0, 0)] for flip in range(2)][:-2]
    places_from.append((0, 0, 1))

    def device(place):
        dx, dy, flip = place
        goal = across * lax.rem(row + dx, other_side) + lax.rem(column + dy, across)
        return {"hours": 2 * goal + (core if flip == 0 else 1 - core)}

    barrier = pltpu.get_barrier_semaphore()
    partners = [{"pairs": before}, {"pairs": after}]
    partners += [device(place) for place in places_from]
    for other in partners:
        pl.semaphore_signal(barrier, inc=1, device_id=other, device_id_type=MESH)

    gathers[0].wait()
    keys = []
    for p in range(pairs):
        second = rows_ref[1, p]
        relative = lax.rem(lax.div(second, stations) - me + 1 + ring, ring)
        keys.append(relative * stations + lax.rem(second, stations))
    place = []
    for side in range(2):
        taken, slots_of = 0, []
        picks = [0] * some
        for j in range(stations):
            found = keys[0] == 2 * side * stations + j
            for key in keys[1:]:
                found = found | (key == 2 * side * stations + j)
            used = found.astype(jnp.int32)
            slots_of.append(taken)
            for t in range(some):
                picks[t] = picks[t] + jnp.where(found & (taken == t), j, 0)
            taken = taken + used
        place.append(slots_of)
        for t in range(some):
            wants[side, t] = picks[t]
    pl.semaphore_wait(barrier, len(partners))
    asks = []
    for side, other in ((0, before), (1, after)):
        copy = pltpu.make_async_remote_copy(
            src_ref=wants.at[side], dst_ref=asked.at[1 - side],
            send_sem=list_send.at[side], recv_sem=list_recv.at[1 - side],
            device_id={"pairs": other}, device_id_type=MESH,
        )
        copy.start()
        asks.append(copy)

    own.wait()
    for copy in gathers[1:]:
        copy.wait()
    ones = jnp.where(
        lax.div(lax.broadcasted_iota(jnp.int32, (128, 128), 0), BAND)
        == lax.div(lax.broadcasted_iota(jnp.int32, (128, 128), 1), BAND),
        1.0, 0.0,
    ).astype(BF16)
    diagonal = lax.rem(
        lax.broadcasted_iota(jnp.int32, (block, segments), 0), segments
    ) == lax.broadcasted_iota(jnp.int32, (block, segments), 1)

    nears, cut = (near_low, near_high), freq // 2

    def station_body(s, carry):
        flags = masks_ref[s].astype(F32)
        lines = jnp.concatenate(
            [jnp.broadcast_to(flags[w : w + 1], (segments, segments)) for w in range(windows)], 0
        )
        mask = jnp.sum(jnp.where(diagonal, lines, 0.0), axis=1, keepdims=True)
        x = jnp.swapaxes(raw[s].astype(F32), 0, 1)
        re, im = whiten(x, mask, ones)
        for b, near in enumerate(nears):
            bins = slice(b * cut, (b + 1) * cut)
            mine[b, s, 0], mine[b, s, 1] = re[:, bins], im[:, bins]
            near[some + s, 0], near[some + s, 1] = re[:, bins], im[:, bins]
        return carry

    lax.fori_loop(0, stations, station_body, 0, unroll=2)
    halos = [[], []]
    for copy in asks:
        copy.wait_recv()
    for b in range(2):
        for t in range(some):
            for side, other in ((1, after), (0, before)):
                slot = 0 if side == 1 else some + stations
                packed[b, side, t] = mine[b, jnp.clip(asked[side, t], 0, stations - 1)]
                copy = pltpu.make_async_remote_copy(
                    src_ref=packed.at[b, side, t], dst_ref=nears[b].at[slot + t],
                    send_sem=halo_send.at[b, side, t], recv_sem=halo_recv.at[b, side, t],
                    device_id={"pairs": other}, device_id_type=MESH,
                )
                copy.start()
                halos[b].append(copy)
    for copy in asks:
        copy.wait_send()

    coef[...] = jnp.zeros_like(coef)
    extra = held_rows.shape[0] - count
    held_rows[count:, :] = jnp.concatenate(
        [start_ref[...], jnp.zeros((extra - RANK, lags), F32)], 0
    ).astype(BF16)
    for p in range(pairs):
        local = lax.rem(rows_ref[1, p], stations)
        relative = lax.div(keys[p], stations)
        low, high = place[0][0], some + stations + place[1][0]
        for j in range(1, stations):
            low = jnp.where(local == j, place[0][j], low)
            high = jnp.where(local == j, some + stations + place[1][j], high)
        at_b = jnp.where(relative == 0, low, jnp.where(relative == 1, some + local, high))
        places[0, p] = some + lax.rem(rows_ref[0, p], stations)
        places[1, p] = jnp.clip(at_b, 0, 2 * stations - 1)
    turn = lax.rem(lax.broadcasted_iota(jnp.int32, (block, cut), 1), 4)
    swap_lanes = lax.rem(turn, 2) == 0
    sign_re = jnp.where((turn == 0) | (turn == 3), 1.0, -1.0)[:1].astype(BF16)
    sign_im = jnp.where(turn >= 2, 1.0, -1.0)[:1].astype(BF16)
    tile = 512
    for b, near in enumerate(nears):
        for copy in halos[b]:
            copy.wait_recv()

        def pair_body(p, carry, b=b, near=near):
            x = near[places[0, p]].astype(F32)
            y = near[places[1, p]].astype(F32)
            re = (x[0] * y[0] + x[1] * y[1]).astype(BF16)
            im = (x[1] * y[0] - x[0] * y[1]).astype(BF16)
            low = pl.ds(pl.multiple_of(p * block, block), block)
            high = pl.ds(pl.multiple_of(count + p * block, block), block)
            reals, imags = slice(b * freq, b * freq + cut), slice(b * freq + cut, (b + 1) * freq)
            cross[high, reals] = re
            cross[high, imags] = im
            cross[low, reals] = jnp.where(swap_lanes, im, re) * sign_re
            cross[low, imags] = jnp.where(swap_lanes, re, im) * sign_im
            return carry

        lax.fori_loop(0, pairs, pair_body, 0, unroll=3)
        if b == 0:
            for copy in fills:
                copy.wait()

        def lag_body(n, carry, b=b):
            lanes = pl.ds(pl.multiple_of(n * tile, tile), tile)
            y = jnp.dot(
                cross[:, b * freq : (b + 1) * freq],
                table[b * freq : (b + 1) * freq, lanes],
                preferred_element_type=F32,
            )
            if b == 0:
                first_sum[:, lanes] = y
                return carry
            y = (y + first_sum[:, lanes]).astype(BF16)
            held_rows[:count, lanes] = y[:count]
            held_rows[:count, pl.ds(pl.multiple_of(half + n * tile, tile), tile)] = y[count:]
            return carry

        lax.fori_loop(0, half // tile, lag_body, 0)

    gram = nt(held_rows[: count + 16], held_rows[...])
    lane = lax.broadcasted_iota(jnp.int32, (1, 128), 1)
    group = lax.div(lax.broadcasted_iota(jnp.int32, (1, 256), 1), 8)
    row_batch = lax.div(lax.broadcasted_iota(jnp.int32, (count, 1), 0), 8)
    batch = lax.broadcasted_iota(jnp.int32, (batches, 1), 0)
    mixed = lane >= segments
    near_lanes = lane < segments
    both = lane < segments + RANK
    shift = (128 - (count - 128) + segments) % 128

    def twelve(folded, tail):
        moved = pltpu.roll(tail, shift, 1)
        return jnp.where(near_lanes, folded, jnp.where(both, moved, 0.0))

    square[...] = twelve(fold8(gram[:count], group, row_batch), gram[:count, 128:])
    rows12 = [square[pl.ds(g, batches, stride=segments), :] for g in range(segments)]
    for r in range(RANK):
        line = jnp.broadcast_to(gram[count + r : count + r + 1], (batches, 256))
        rows12.append(twelve(fold8(line, group, batch), line[:, 128:]))

    def product(vectors):
        out = []
        for vector in vectors:
            total = vector[:, 0:1] * rows12[0]
            for j in range(1, segments + RANK):
                total = total + vector[:, j : j + 1] * rows12[j]
            out.append(total)
        return out

    weight = float(lags)
    held = [jnp.where(lane == segments + r, 1.0, 0.0) for r in range(RANK)]
    seen = [rows12[segments + r] for r in range(RANK)]
    for _ in range(TURNS):
        stepped = [weight * held[r] + jnp.where(near_lanes, seen[r], 0.0) for r in range(RANK)]
        image = product(stepped)
        small = [
            [jnp.sum(image[i] * stepped[j], axis=1, keepdims=True) for j in range(i + 1)]
            for i in range(RANK)
        ]
        lower = cholesky(small)
        held = solve(lower, stepped)
        seen = solve(lower, image)
    onto = [jnp.where(near_lanes, seen[r], 0.0) for r in range(RANK)]
    final = [weight * held[r] + onto[r] for r in range(RANK)]
    window = None
    for r in range(RANK):
        term = jnp.sum(onto[r], axis=1, keepdims=True) * held[r]
        window = term if window is None else window + term
    window = window * (1.0 / math.sqrt(segments))

    def spread(x):
        tail = pltpu.roll(jnp.where(mixed, x, 0.0), 128 - shift, 1)
        base = jnp.where(near_lanes, x, 0.0)
        for step in (8, 16, 32, 64):
            base = base + pltpu.roll(base, step, 1)
        left = jnp.where(group[:, :128] == batch, base, 0.0)
        right = jnp.where(group[:, 128:] == batch, base, 0.0) + tail
        return jnp.concatenate([left, right], 1)

    shown = spread(window)
    coef[:batches] = shown
    hours = lax.axis_size("hours")
    units = [spread(x) for x in final] + [shown * (1.0 / math.sqrt(windows * hours))]
    each = pairs // 2
    for r, unit in enumerate(units):
        for side in range(2):
            wide[side] = unit[:, side * 128 : (side + 1) * 128]
            total = wide.at[side][pl.ds(0, pairs, stride=windows), :]
            for w in range(1, windows):
                total = total + wide.at[side][pl.ds(w, pairs, stride=windows), :]
            for c in range(2):
                start = batches + c * slots + r * each
                columns = slice(side * 128, (side + 1) * 128)
                coef[start : start + each, columns] = total[c * each : (c + 1) * each]

    coefs = jnp.concatenate(split(coef[batches:]), 0)
    size = coef.shape[0] - batches
    width = lags // chips
    chunk = across * width
    rows_order = sorted(range(other_side), key=lambda d: -min(d, other_side - d))
    columns_order = sorted(range(across), key=lambda d: -min(d, across - d))
    sends = []
    for i, dx in enumerate(rows_order):
        goal_row = lax.rem(row + dx, other_side)
        columns = pl.ds(pl.multiple_of(goal_row * chunk, chunk), chunk)
        out = jnp.dot(coefs, held_rows[:, columns], preferred_element_type=F32)
        out = out[:size] + out[size:]
        for c in range(2):
            block_rows = out[c * slots : (c + 1) * slots].astype(BF16)
            for y in range(across):
                part[i, c, y] = block_rows[:, y * width : (y + 1) * width]
        for dy in columns_order:
            for flip in range(2):
                if (dx, dy, flip) == (0, 0, 0):
                    continue
                index = places_from.index((dx, dy, flip))
                copy = pltpu.make_async_remote_copy(
                    src_ref=part.at[
                        i, core if flip == 0 else 1 - core, lax.rem(column + dy, across)
                    ],
                    dst_ref=incoming.at[index],
                    send_sem=out_send.at[index], recv_sem=in_recv.at[index],
                    device_id=device((dx, dy, flip)), device_id_type=MESH,
                )
                copy.start()
                sends.append((index, copy))
    coefs = jnp.concatenate(split(coef[:batches]), 0)
    for i in range(other_side):
        columns = slice(i * chunk, (i + 1) * chunk)
        out = jnp.dot(coefs, held_rows[:, columns], preferred_element_type=F32)
        ws_ref[:, columns] = out[:batches] + out[batches:]
    merged = part[other_side - 1, core, column].astype(F32)
    for index, copy in reversed(sends):
        copy.wait_recv()
        merged = merged + incoming[index].astype(F32)
    summed_rows[...] = merged

    swap = pltpu.make_async_remote_copy(
        src_ref=summed_rows, dst_ref=theirs, send_sem=send_sem.at[0], recv_sem=recv_sem.at[0],
        device_id=twin, device_id_type=MESH,
    )
    swap.start()
    vectors = [summed_rows[r * each : (r + 1) * each] for r in range(RANK)]
    order = [(i, j) for i in range(RANK) for j in range(i + 1)]
    line = lax.broadcasted_iota(jnp.int32, (each, 128), 1)
    pair_of = lax.broadcasted_iota(jnp.int32, (each, 128), 0)
    marks = [line == 8 * index + pair_of for index in range(len(order))]
    tile = jnp.zeros((each, 128), F32)
    for mark, (i, j) in zip(marks, order):
        tile = jnp.where(mark, jnp.sum(vectors[i] * vectors[j], axis=1, keepdims=True), tile)
    own_gram[...] = jnp.sum(tile, axis=0, keepdims=True)
    tells = []
    for index, place in enumerate(places_from):
        copy = pltpu.make_async_remote_copy(
            src_ref=own_gram, dst_ref=grams.at[index],
            send_sem=gram_send.at[index], recv_sem=gram_recv.at[index],
            device_id=device(place), device_id_type=MESH,
        )
        copy.start()
        tells.append(copy)
    swap.wait()
    for copy in halos[0] + halos[1]:
        copy.wait_send()
    for _, copy in sends:
        copy.wait_send()
    gram_sums = [own_gram[...], None]
    for index in reversed(range(len(tells))):
        tells[index].wait_recv()
        flip = places_from[index][2]
        value = grams[index]
        gram_sums[flip] = value if gram_sums[flip] is None else gram_sums[flip] + value
    own_half = width // 2

    def halved(x):
        return jnp.where(core == 0, x[:, :own_half], x[:, own_half:])

    for flip, source in enumerate((summed_rows, theirs)):
        target = core if flip == 0 else 1 - core
        small = [[None] * RANK for _ in range(RANK)]
        for mark, (i, j) in zip(marks, order):
            small[i][j] = jnp.sum(
                jnp.where(mark, gram_sums[flip], 0.0), axis=1, keepdims=True
            )
        pieces = [halved(source[r * each : (r + 1) * each]) for r in range(RANK)]
        for r, value in enumerate(solve(cholesky(small), pieces)):
            out_ref[target, r * each : (r + 1) * each] = value * math.sqrt(lags)
        out_ref[target, RANK * each :] = halved(source[RANK * each :])
    for copy in tells:
        copy.wait_send()


def finish_kernel(pairs, windows, windows_ref, merged_ref, ws_ref, stack_ref, basis_ref):
    each = pairs // 2
    for p in range(pairs):
        ws_ref[p] = windows_ref[windows * p : windows * (p + 1)]
    rows = merged_ref[...]
    stack_ref[...] = jnp.concatenate(
        [rows[c, RANK * each : (RANK + 1) * each] for c in range(2)], 0
    )
    for p in range(pairs):
        c, q = divmod(p, each)
        for r in range(RANK):
            basis_ref[p, r : r + 1] = rows[c, r * each + q : r * each + q + 1]


def on_device(table, spectra, masks, pair_rows, start_basis):
    stations, windows, segments, _, freq = spectra.shape
    lags = start_basis.shape[1]
    half = lags // 2
    pairs = pair_rows.shape[0]
    block = windows * segments
    count = pairs * block
    batches = pairs * windows
    each = pairs // 2
    slots = 32
    chips = lax.axis_size("hours") // 2
    width = lags // chips
    rows_of_chips = torus_offsets(chips)[1]
    raw = spectra.reshape(stations, block, 2, freq)
    vmem = pl.BlockSpec(memory_space=pltpu.VMEM)
    windows_out, merged = pl.pallas_call(
        functools.partial(station_kernel, stations, segments, windows, pairs, freq, half),
        out_shape=(
            pltpu.VMEM((batches, lags), F32),
            pltpu.VMEM((2, slots, width // 2), F32),
        ),
        in_specs=[
            pl.BlockSpec(memory_space=pltpu.HBM),
        ]
        * 5,
        out_specs=(vmem, vmem),
        scratch_shapes=[
            pltpu.SMEM((2, pairs), jnp.int32),
            pltpu.VMEM((stations, windows, segments), jnp.int32),
            pltpu.VMEM((RANK, lags), F32),
            pltpu.VMEM((stations, block, 2, freq), BF16),
            pltpu.VMEM((2, stations, 2, block, freq // 2), BF16),
            pltpu.VMEM((2, 2, stations // 2, 2, block, freq // 2), BF16),
            pltpu.SMEM((2, stations // 2), jnp.int32),
            pltpu.SMEM((2, stations // 2), jnp.int32),
            pltpu.SMEM((2, pairs), jnp.int32),
            pltpu.VMEM((2 * stations, 2, block, freq // 2), BF16),
            pltpu.VMEM((2 * stations, 2, block, freq // 2), BF16),
            pltpu.VMEM((2 * count, 2 * freq), BF16),
            pltpu.VMEM((2 * count, half), F32),
            pltpu.VMEM((2 * freq, half), BF16),
            pltpu.VMEM((256, lags), BF16),
            pltpu.VMEM((count, 128), F32),
            pltpu.VMEM((2, batches, 128), F32),
            pltpu.VMEM((batches + 2 * slots, 256), F32),
            pltpu.VMEM((rows_of_chips, 2, chips // rows_of_chips, slots, width), BF16),
            pltpu.VMEM((2 * chips - 1, slots, width), BF16),
            pltpu.VMEM((slots, width), F32),
            pltpu.VMEM((slots, width), F32),
            pltpu.VMEM((1, 128), F32),
            pltpu.VMEM((2 * chips - 1, 1, 128), F32),
            pltpu.SemaphoreType.DMA((2,)),
            pltpu.SemaphoreType.DMA((2,)),
            pltpu.SemaphoreType.DMA((2, 2, stations // 2)),
            pltpu.SemaphoreType.DMA((2, 2, stations // 2)),
            pltpu.SemaphoreType.DMA((1,)),
            pltpu.SemaphoreType.DMA((1,)),
            pltpu.SemaphoreType.DMA((5,)),
            pltpu.SemaphoreType.DMA((4,)),
            pltpu.SemaphoreType.DMA((2 * chips - 1,)),
            pltpu.SemaphoreType.DMA((2 * chips - 1,)),
            pltpu.SemaphoreType.DMA((2 * chips - 1,)),
            pltpu.SemaphoreType.DMA((2 * chips - 1,)),
        ],
        compiler_params=pltpu.CompilerParams(
            collective_id=0, has_side_effects=True, vmem_limit_bytes=60 << 20
        ),
        name="station_pairs",
    )(pair_rows.T, masks, raw, table, start_basis)
    return pl.pallas_call(
        functools.partial(finish_kernel, pairs, windows),
        out_shape=(
            jax.ShapeDtypeStruct((pairs, windows, lags), F32),
            jax.ShapeDtypeStruct((pairs, width // 2), F32),
            jax.ShapeDtypeStruct((pairs, RANK, width // 2), F32),
        ),
        in_specs=[vmem, vmem],
        out_specs=(vmem, vmem, vmem),
        compiler_params=pltpu.CompilerParams(vmem_limit_bytes=4 << 20),
        name="outputs",
    )(windows_out, merged)


def solution(mesh):
    in_specs = (
        P("pairs", "hours", None, None, None),
        P("pairs", "hours", None),
        P("pairs", None),
        P(),
    )
    out_specs = (P("pairs", "hours", None), P("pairs", "hours"), P("pairs", None, "hours"))

    def whole(spectra, masks, pair_rows, start_basis):
        table = jnp.asarray(half_table(spectra.shape[4], start_basis.shape[1] // 2))
        return jax.shard_map(
            on_device, mesh=mesh, in_specs=(P(), *in_specs), out_specs=out_specs, check_vma=False
        )(table, spectra, masks, pair_rows, start_basis)

    return whole
```

```python
import functools
import math

import jax
import jax.numpy as jnp
import numpy as np
from jax import lax
from jax.experimental import pallas as pl
from jax.experimental.pallas import tpu as pltpu
from jax.sharding import PartitionSpec as P

BAND = 64
TURNS = 2
CUTS = 4
RANK = 4
MESH = pl.DeviceIdType.MESH
F32 = jnp.float32
BF16 = jnp.bfloat16


def half_table(freq, half):
    bins = np.arange(1, freq + 1, dtype=np.int64)[:, None]
    shifts = np.arange(half, dtype=np.int64)[None, :]
    phase = np.mod(bins * shifts, 4 * half).astype(np.float64) * (math.pi / (2 * half))
    scale = freq ** (-0.5)
    table = np.stack([np.cos(phase) * scale, -np.sin(phase) * scale], 0)
    table = table.reshape(2, CUTS, freq // CUTS, half).transpose(1, 0, 2, 3).reshape(2 * freq, half)
    return table.astype(np.float32).astype(jnp.bfloat16)


def whiten(x, mask, ones):
    rows, freq = x.shape[1:]
    square = x[0] * x[0] + x[1] * x[1]
    tiles = freq // 128
    stacked = jnp.concatenate([square[:, t * 128 : (t + 1) * 128] for t in range(tiles)], 0)
    hi, lo = split(stacked)
    power = jnp.dot(hi, ones, preferred_element_type=F32) + jnp.dot(
        lo, ones, preferred_element_type=F32
    )
    scale = lax.rsqrt(power * (0.5 / BAND) + 1e-06)
    scale = jnp.concatenate([scale[t * rows : (t + 1) * rows] for t in range(tiles)], 1) * mask
    return (x[0] * scale).astype(BF16), (x[1] * scale).astype(BF16)


def nt(a, b):
    return lax.dot_general(a, b, (((1,), (1,)), ((), ())), preferred_element_type=F32)


def split(x):
    hi = x.astype(BF16)
    return hi, (x - hi.astype(F32)).astype(BF16)


def cholesky(gram):
    lower = [[None] * RANK for _ in range(RANK)]
    for row in range(RANK):
        for col in range(row + 1):
            total = gram[row][col]
            for inner in range(col):
                total = total - lower[row][inner] * lower[col][inner]
            lower[row][col] = 1.0 / jnp.sqrt(total) if row == col else total * lower[col][col]
    return lower


def solve(lower, vectors):
    result = []
    for row in range(RANK):
        current = vectors[row]
        for inner in range(row):
            current = current - lower[row][inner] * result[inner]
        result.append(current * lower[row][row])
    return result


def fold8(x, batch_of_lane, batch):
    kept = jnp.where(batch_of_lane == batch, x, 0.0)
    total = kept[:, :128] + kept[:, 128:]
    for shift in (64, 32, 16, 8):
        total = total + pltpu.roll(total, shift, 1)
    return total


def torus_offsets(chips):
    side = math.isqrt(chips)
    side = side if side * side == chips else 1
    other = chips // side
    offsets = [(dx, dy) for dx in range(other) for dy in range(side) if dx or dy]
    return side, other, sorted(
        offsets, key=lambda o: -(min(o[0], other - o[0]) + min(o[1], side - o[1]))
    )


def station_kernel(
    stations, segments, windows, pairs, freq, half,
    rows_hbm, masks_hbm, raw_ref, table_ref, start_hbm,
    ws_ref, out_ref,
    rows_ref, masks_ref, start_ref, raw, mine, packed, wants, asked, places, near_a, near_b, near_c, near_d,
    cross, first_sum, table, held_rows, square, wide, coef,
    part, incoming, summed_rows, theirs, own_gram, grams,
    list_send, list_recv, halo_send, halo_recv, send_sem, recv_sem, own_sem, fill_sem,
    out_send, in_recv, gram_send, gram_recv,
):
    me, ring = lax.axis_index("pairs"), lax.axis_size("pairs")
    after, before = lax.rem(me + 1, ring), lax.rem(me + ring - 1, ring)
    block = windows * segments
    count = pairs * block
    batches = pairs * windows
    lags = 2 * half
    slots = coef.shape[0] // 2 - batches // 2
    some = stations // 2
    own = pltpu.make_async_copy(raw_ref, raw, own_sem.at[0])
    cuts = 4
    band = 2 * freq // cuts
    fills = [
        pltpu.make_async_copy(
            table_ref.at[pl.ds(i * band, band)], table.at[pl.ds(i * band, band)], fill_sem.at[i]
        )
        for i in range(cuts)
    ]
    gathers = [
        pltpu.make_async_copy(source, target, own_sem.at[2 + index])
        for index, (source, target) in enumerate(
            ((rows_hbm, rows_ref), (masks_hbm, masks_ref), (start_hbm, start_ref))
        )
    ]
    for copy in gathers:
        copy.start()
    own.start()
    for copy in fills:
        copy.start()

    hour = lax.axis_index("hours")
    chips = lax.axis_size("hours") // 2
    core, chip = lax.rem(hour, 2), lax.div(hour, 2)
    twin = {"hours": hour + 1 - 2 * core}
    across, other_side, offsets = torus_offsets(chips)
    row, column = lax.div(chip, across), lax.rem(chip, across)
    places_from = [(dx, dy, flip) for dx, dy in offsets + [(0, 0)] for flip in range(2)][:-2]
    places_from.append((0, 0, 1))

    def device(place):
        dx, dy, flip = place
        goal = across * lax.rem(row + dx, other_side) + lax.rem(column + dy, across)
        return {"hours": 2 * goal + (core if flip == 0 else 1 - core)}

    barrier = pltpu.get_barrier_semaphore()
    partners = [{"pairs": before}, {"pairs": after}]
    partners += [device(place) for place in places_from]
    for other in partners:
        pl.semaphore_signal(barrier, inc=1, device_id=other, device_id_type=MESH)

    gathers[0].wait()
    keys = []
    for p in range(pairs):
        second = rows_ref[1, p]
        relative = lax.rem(lax.div(second, stations) - me + 1 + ring, ring)
        keys.append(relative * stations + lax.rem(second, stations))
    place = []
    for side in range(2):
        taken, slots_of = 0, []
        picks = [0] * some
        for j in range(stations):
            found = keys[0] == 2 * side * stations + j
            for key in keys[1:]:
                found = found | (key == 2 * side * stations + j)
            used = found.astype(jnp.int32)
            slots_of.append(taken)
            for t in range(some):
                picks[t] = picks[t] + jnp.where(found & (taken == t), j, 0)
            taken = taken + used
        place.append(slots_of)
        for t in range(some):
            wants[side, t] = picks[t]
    pl.semaphore_wait(barrier, len(partners))
    asks = []
    for side, other in ((0, before), (1, after)):
        copy = pltpu.make_async_remote_copy(
            src_ref=wants.at[side], dst_ref=asked.at[1 - side],
            send_sem=list_send.at[side], recv_sem=list_recv.at[1 - side],
            device_id={"pairs": other}, device_id_type=MESH,
        )
        copy.start()
        asks.append(copy)

    own.wait()
    for copy in gathers[1:]:
        copy.wait()
    ones = jnp.where(
        lax.div(lax.broadcasted_iota(jnp.int32, (128, 128), 0), BAND)
        == lax.div(lax.broadcasted_iota(jnp.int32, (128, 128), 1), BAND),
        1.0, 0.0,
    ).astype(BF16)
    diagonal = lax.rem(
        lax.broadcasted_iota(jnp.int32, (block, segments), 0), segments
    ) == lax.broadcasted_iota(jnp.int32, (block, segments), 1)

    nears, cut = (near_a, near_b, near_c, near_d), freq // CUTS

    def station_body(s, carry):
        flags = masks_ref[s].astype(F32)
        lines = jnp.concatenate(
            [jnp.broadcast_to(flags[w : w + 1], (segments, segments)) for w in range(windows)], 0
        )
        mask = jnp.sum(jnp.where(diagonal, lines, 0.0), axis=1, keepdims=True)
        x = jnp.swapaxes(raw[s].astype(F32), 0, 1)
        re, im = whiten(x, mask, ones)
        for b, near in enumerate(nears):
            bins = slice(b * cut, (b + 1) * cut)
            mine[b, s, 0], mine[b, s, 1] = re[:, bins], im[:, bins]
            near[some + s, 0], near[some + s, 1] = re[:, bins], im[:, bins]
        return carry

    lax.fori_loop(0, stations, station_body, 0, unroll=2)
    halos = [[] for _ in range(CUTS)]
    for copy in asks:
        copy.wait_recv()
    for b in range(CUTS):
        for t in range(some):
            for side, other in ((1, after), (0, before)):
                slot = 0 if side == 1 else some + stations
                packed[b, side, t] = mine[b, jnp.clip(asked[side, t], 0, stations - 1)]
                copy = pltpu.make_async_remote_copy(
                    src_ref=packed.at[b, side, t], dst_ref=nears[b].at[slot + t],
                    send_sem=halo_send.at[b, side, t], recv_sem=halo_recv.at[b, side, t],
                    device_id={"pairs": other}, device_id_type=MESH,
                )
                copy.start()
                halos[b].append(copy)
    for copy in asks:
        copy.wait_send()

    coef[...] = jnp.zeros_like(coef)
    extra = held_rows.shape[0] - count
    held_rows[count:, :] = jnp.concatenate(
        [start_ref[...], jnp.zeros((extra - RANK, lags), F32)], 0
    ).astype(BF16)
    for p in range(pairs):
        local = lax.rem(rows_ref[1, p], stations)
        relative = lax.div(keys[p], stations)
        low, high = place[0][0], some + stations + place[1][0]
        for j in range(1, stations):
            low = jnp.where(local == j, place[0][j], low)
            high = jnp.where(local == j, some + stations + place[1][j], high)
        at_b = jnp.where(relative == 0, low, jnp.where(relative == 1, some + local, high))
        places[0, p] = some + lax.rem(rows_ref[0, p], stations)
        places[1, p] = jnp.clip(at_b, 0, 2 * stations - 1)
    turn = lax.rem(lax.broadcasted_iota(jnp.int32, (block, cut), 1), 4)
    swap_lanes = lax.rem(turn, 2) == 0
    sign_re = jnp.where((turn == 0) | (turn == 3), 1.0, -1.0)[:1].astype(BF16)
    sign_im = jnp.where(turn >= 2, 1.0, -1.0)[:1].astype(BF16)
    tile = 512
    for b, near in enumerate(nears):
        for copy in halos[b]:
            copy.wait_recv()

        def pair_body(p, carry, b=b, near=near):
            x = near[places[0, p]].astype(F32)
            y = near[places[1, p]].astype(F32)
            re = (x[0] * y[0] + x[1] * y[1]).astype(BF16)
            im = (x[1] * y[0] - x[0] * y[1]).astype(BF16)
            low = pl.ds(pl.multiple_of(p * block, block), block)
            high = pl.ds(pl.multiple_of(count + p * block, block), block)
            reals = slice(2 * b * cut, (2 * b + 1) * cut)
            imags = slice((2 * b + 1) * cut, (2 * b + 2) * cut)
            cross[high, reals] = re
            cross[high, imags] = im
            cross[low, reals] = jnp.where(swap_lanes, im, re) * sign_re
            cross[low, imags] = jnp.where(swap_lanes, re, im) * sign_im
            return carry

        lax.fori_loop(0, pairs, pair_body, 0, unroll=3)
        if b == 0:
            for copy in fills:
                copy.wait()

        def lag_body(n, carry, b=b):
            lanes = pl.ds(pl.multiple_of(n * tile, tile), tile)
            y = jnp.dot(
                cross[:, 2 * b * cut : (2 * b + 2) * cut],
                table[2 * b * cut : (2 * b + 2) * cut, lanes],
                preferred_element_type=F32,
            )
            if b > 0:
                y = y + first_sum[:, lanes]
            if b < CUTS - 1:
                first_sum[:, lanes] = y
                return carry
            y = y.astype(BF16)
            held_rows[:count, lanes] = y[:count]
            held_rows[:count, pl.ds(pl.multiple_of(half + n * tile, tile), tile)] = y[count:]
            return carry

        lax.fori_loop(0, half // tile, lag_body, 0)

    gram = nt(held_rows[: count + 16], held_rows[...])
    lane = lax.broadcasted_iota(jnp.int32, (1, 128), 1)
    group = lax.div(lax.broadcasted_iota(jnp.int32, (1, 256), 1), 8)
    row_batch = lax.div(lax.broadcasted_iota(jnp.int32, (count, 1), 0), 8)
    batch = lax.broadcasted_iota(jnp.int32, (batches, 1), 0)
    mixed = lane >= segments
    near_lanes = lane < segments
    both = lane < segments + RANK
    shift = (128 - (count - 128) + segments) % 128

    def twelve(folded, tail):
        moved = pltpu.roll(tail, shift, 1)
        return jnp.where(near_lanes, folded, jnp.where(both, moved, 0.0))

    square[...] = twelve(fold8(gram[:count], group, row_batch), gram[:count, 128:])
    rows12 = [square[pl.ds(g, batches, stride=segments), :] for g in range(segments)]
    for r in range(RANK):
        line = jnp.broadcast_to(gram[count + r : count + r + 1], (batches, 256))
        rows12.append(twelve(fold8(line, group, batch), line[:, 128:]))

    def product(vectors):
        out = []
        for vector in vectors:
            total = vector[:, 0:1] * rows12[0]
            for j in range(1, segments + RANK):
                total = total + vector[:, j : j + 1] * rows12[j]
            out.append(total)
        return out

    weight = float(lags)
    held = [jnp.where(lane == segments + r, 1.0, 0.0) for r in range(RANK)]
    seen = [rows12[segments + r] for r in range(RANK)]
    for _ in range(TURNS):
        stepped = [weight * held[r] + jnp.where(near_lanes, seen[r], 0.0) for r in range(RANK)]
        image = product(stepped)
        small = [
            [jnp.sum(image[i] * stepped[j], axis=1, keepdims=True) for j in range(i + 1)]
            for i in range(RANK)
        ]
        lower = cholesky(small)
        held = solve(lower, stepped)
        seen = solve(lower, image)
    onto = [jnp.where(near_lanes, seen[r], 0.0) for r in range(RANK)]
    final = [weight * held[r] + onto[r] for r in range(RANK)]
    window = None
    for r in range(RANK):
        term = jnp.sum(onto[r], axis=1, keepdims=True) * held[r]
        window = term if window is None else window + term
    window = window * (1.0 / math.sqrt(segments))

    def spread(x):
        tail = pltpu.roll(jnp.where(mixed, x, 0.0), 128 - shift, 1)
        base = jnp.where(near_lanes, x, 0.0)
        for step in (8, 16, 32, 64):
            base = base + pltpu.roll(base, step, 1)
        left = jnp.where(group[:, :128] == batch, base, 0.0)
        right = jnp.where(group[:, 128:] == batch, base, 0.0) + tail
        return jnp.concatenate([left, right], 1)

    shown = spread(window)
    coef[:batches] = shown
    hours = lax.axis_size("hours")
    units = [spread(x) for x in final] + [shown * (1.0 / math.sqrt(windows * hours))]
    each = pairs // 2
    for r, unit in enumerate(units):
        for side in range(2):
            wide[side] = unit[:, side * 128 : (side + 1) * 128]
            total = wide.at[side][pl.ds(0, pairs, stride=windows), :]
            for w in range(1, windows):
                total = total + wide.at[side][pl.ds(w, pairs, stride=windows), :]
            for c in range(2):
                start = batches + c * slots + r * each
                columns = slice(side * 128, (side + 1) * 128)
                coef[start : start + each, columns] = total[c * each : (c + 1) * each]

    coefs = jnp.concatenate(split(coef[batches:]), 0)
    size = coef.shape[0] - batches
    width = lags // chips
    chunk = across * width
    rows_order = sorted(range(other_side), key=lambda d: -min(d, other_side - d))
    columns_order = sorted(range(across), key=lambda d: -min(d, across - d))
    sends = []
    for i, dx in enumerate(rows_order):
        goal_row = lax.rem(row + dx, other_side)
        columns = pl.ds(pl.multiple_of(goal_row * chunk, chunk), chunk)
        out = jnp.dot(coefs, held_rows[:, columns], preferred_element_type=F32)
        out = out[:size] + out[size:]
        for c in range(2):
            block_rows = out[c * slots : (c + 1) * slots].astype(BF16)
            for y in range(across):
                part[i, c, y] = block_rows[:, y * width : (y + 1) * width]
        for dy in columns_order:
            for flip in range(2):
                if (dx, dy, flip) == (0, 0, 0):
                    continue
                index = places_from.index((dx, dy, flip))
                copy = pltpu.make_async_remote_copy(
                    src_ref=part.at[
                        i, core if flip == 0 else 1 - core, lax.rem(column + dy, across)
                    ],
                    dst_ref=incoming.at[index],
                    send_sem=out_send.at[index], recv_sem=in_recv.at[index],
                    device_id=device((dx, dy, flip)), device_id_type=MESH,
                )
                copy.start()
                sends.append((index, copy))
    coefs = jnp.concatenate(split(coef[:batches]), 0)
    for i in range(other_side):
        columns = slice(i * chunk, (i + 1) * chunk)
        out = jnp.dot(coefs, held_rows[:, columns], preferred_element_type=F32)
        ws_ref[:, columns] = out[:batches] + out[batches:]
    merged = part[other_side - 1, core, column].astype(F32)
    for index, copy in reversed(sends):
        copy.wait_recv()
        merged = merged + incoming[index].astype(F32)
    summed_rows[...] = merged

    swap = pltpu.make_async_remote_copy(
        src_ref=summed_rows, dst_ref=theirs, send_sem=send_sem.at[0], recv_sem=recv_sem.at[0],
        device_id=twin, device_id_type=MESH,
    )
    swap.start()
    vectors = [summed_rows[r * each : (r + 1) * each] for r in range(RANK)]
    order = [(i, j) for i in range(RANK) for j in range(i + 1)]
    line = lax.broadcasted_iota(jnp.int32, (each, 128), 1)
    pair_of = lax.broadcasted_iota(jnp.int32, (each, 128), 0)
    marks = [line == 8 * index + pair_of for index in range(len(order))]
    tile = jnp.zeros((each, 128), F32)
    for mark, (i, j) in zip(marks, order):
        tile = jnp.where(mark, jnp.sum(vectors[i] * vectors[j], axis=1, keepdims=True), tile)
    own_gram[...] = jnp.sum(tile, axis=0, keepdims=True)
    tells = []
    for index, place in enumerate(places_from):
        copy = pltpu.make_async_remote_copy(
            src_ref=own_gram, dst_ref=grams.at[index],
            send_sem=gram_send.at[index], recv_sem=gram_recv.at[index],
            device_id=device(place), device_id_type=MESH,
        )
        copy.start()
        tells.append(copy)
    swap.wait()
    for copy in sum(halos, []):
        copy.wait_send()
    for _, copy in sends:
        copy.wait_send()
    gram_sums = [own_gram[...], None]
    for index in reversed(range(len(tells))):
        tells[index].wait_recv()
        flip = places_from[index][2]
        value = grams[index]
        gram_sums[flip] = value if gram_sums[flip] is None else gram_sums[flip] + value
    own_half = width // 2

    def halved(x):
        return jnp.where(core == 0, x[:, :own_half], x[:, own_half:])

    for flip, source in enumerate((summed_rows, theirs)):
        target = core if flip == 0 else 1 - core
        small = [[None] * RANK for _ in range(RANK)]
        for mark, (i, j) in zip(marks, order):
            small[i][j] = jnp.sum(
                jnp.where(mark, gram_sums[flip], 0.0), axis=1, keepdims=True
            )
        pieces = [halved(source[r * each : (r + 1) * each]) for r in range(RANK)]
        for r, value in enumerate(solve(cholesky(small), pieces)):
            out_ref[target, r * each : (r + 1) * each] = value * math.sqrt(lags)
        out_ref[target, RANK * each :] = halved(source[RANK * each :])
    for copy in tells:
        copy.wait_send()


def finish_kernel(pairs, windows, windows_ref, merged_ref, ws_ref, stack_ref, basis_ref):
    each = pairs // 2
    for p in range(pairs):
        ws_ref[p] = windows_ref[windows * p : windows * (p + 1)]
    rows = merged_ref[...]
    stack_ref[...] = jnp.concatenate(
        [rows[c, RANK * each : (RANK + 1) * each] for c in range(2)], 0
    )
    for p in range(pairs):
        c, q = divmod(p, each)
        for r in range(RANK):
            basis_ref[p, r : r + 1] = rows[c, r * each + q : r * each + q + 1]


def on_device(table, spectra, masks, pair_rows, start_basis):
    stations, windows, segments, _, freq = spectra.shape
    lags = start_basis.shape[1]
    half = lags // 2
    pairs = pair_rows.shape[0]
    block = windows * segments
    count = pairs * block
    batches = pairs * windows
    each = pairs // 2
    slots = 32
    chips = lax.axis_size("hours") // 2
    width = lags // chips
    rows_of_chips = torus_offsets(chips)[1]
    raw = spectra.reshape(stations, block, 2, freq)
    vmem = pl.BlockSpec(memory_space=pltpu.VMEM)
    windows_out, merged = pl.pallas_call(
        functools.partial(station_kernel, stations, segments, windows, pairs, freq, half),
        out_shape=(
            pltpu.VMEM((batches, lags), F32),
            pltpu.VMEM((2, slots, width // 2), F32),
        ),
        in_specs=[
            pl.BlockSpec(memory_space=pltpu.HBM),
        ]
        * 5,
        out_specs=(vmem, vmem),
        scratch_shapes=[
            pltpu.SMEM((2, pairs), jnp.int32),
            pltpu.VMEM((stations, windows, segments), jnp.int32),
            pltpu.VMEM((RANK, lags), F32),
            pltpu.VMEM((stations, block, 2, freq), BF16),
            pltpu.VMEM((CUTS, stations, 2, block, freq // CUTS), BF16),
            pltpu.VMEM((CUTS, 2, stations // 2, 2, block, freq // CUTS), BF16),
            pltpu.SMEM((2, stations // 2), jnp.int32),
            pltpu.SMEM((2, stations // 2), jnp.int32),
            pltpu.SMEM((2, pairs), jnp.int32),
            pltpu.VMEM((2 * stations, 2, block, freq // CUTS), BF16),
            pltpu.VMEM((2 * stations, 2, block, freq // CUTS), BF16),
            pltpu.VMEM((2 * stations, 2, block, freq // CUTS), BF16),
            pltpu.VMEM((2 * stations, 2, block, freq // CUTS), BF16),
            pltpu.VMEM((2 * count, 2 * freq), BF16),
            pltpu.VMEM((2 * count, half), F32),
            pltpu.VMEM((2 * freq, half), BF16),
            pltpu.VMEM((256, lags), BF16),
            pltpu.VMEM((count, 128), F32),
            pltpu.VMEM((2, batches, 128), F32),
            pltpu.VMEM((batches + 2 * slots, 256), F32),
            pltpu.VMEM((rows_of_chips, 2, chips // rows_of_chips, slots, width), BF16),
            pltpu.VMEM((2 * chips - 1, slots, width), BF16),
            pltpu.VMEM((slots, width), F32),
            pltpu.VMEM((slots, width), F32),
            pltpu.VMEM((1, 128), F32),
            pltpu.VMEM((2 * chips - 1, 1, 128), F32),
            pltpu.SemaphoreType.DMA((2,)),
            pltpu.SemaphoreType.DMA((2,)),
            pltpu.SemaphoreType.DMA((CUTS, 2, stations // 2)),
            pltpu.SemaphoreType.DMA((CUTS, 2, stations // 2)),
            pltpu.SemaphoreType.DMA((1,)),
            pltpu.SemaphoreType.DMA((1,)),
            pltpu.SemaphoreType.DMA((5,)),
            pltpu.SemaphoreType.DMA((4,)),
            pltpu.SemaphoreType.DMA((2 * chips - 1,)),
            pltpu.SemaphoreType.DMA((2 * chips - 1,)),
            pltpu.SemaphoreType.DMA((2 * chips - 1,)),
            pltpu.SemaphoreType.DMA((2 * chips - 1,)),
        ],
        compiler_params=pltpu.CompilerParams(
            collective_id=0, has_side_effects=True, vmem_limit_bytes=60 << 20
        ),
        name="station_pairs",
    )(pair_rows.T, masks, raw, table, start_basis)
    return pl.pallas_call(
        functools.partial(finish_kernel, pairs, windows),
        out_shape=(
            jax.ShapeDtypeStruct((pairs, windows, lags), F32),
            jax.ShapeDtypeStruct((pairs, width // 2), F32),
            jax.ShapeDtypeStruct((pairs, RANK, width // 2), F32),
        ),
        in_specs=[vmem, vmem],
        out_specs=(vmem, vmem, vmem),
        compiler_params=pltpu.CompilerParams(vmem_limit_bytes=4 << 20),
        name="outputs",
    )(windows_out, merged)


def solution(mesh):
    in_specs = (
        P("pairs", "hours", None, None, None),
        P("pairs", "hours", None),
        P("pairs", None),
        P(),
    )
    out_specs = (P("pairs", "hours", None), P("pairs", "hours"), P("pairs", None, "hours"))

    def whole(spectra, masks, pair_rows, start_basis):
        table = jnp.asarray(half_table(spectra.shape[4], start_basis.shape[1] // 2))
        return jax.shard_map(
            on_device, mesh=mesh, in_specs=(P(), *in_specs), out_specs=out_specs, check_vma=False
        )(table, spectra, masks, pair_rows, start_basis)

    return whole
```
